32 devices in a mesh: row: 4 (over x, core), col: 8 (over z, y).
Axes of the slice: x: 2, y: 2, z: 4, core: 2. Of those that a mesh axis runs over, the one named last changes fastest.
Arguments:
- design: bfloat16 [18432, 2048], P(('row', 'col')), may hold values from -0.19921875 to 0.19921875
- arc_filter: bfloat16 [2048, 2048], replicated, may hold values from -0.59765625 to 0.59765625
- arc_of_row: int32 [2048], replicated, may hold values from 0 to 255, never falling along the last dimension, each value on 1 to 512 neighbouring positions
- terr_stored: bfloat16 [18432, 128], P(('row', 'col')), may hold values from -3 to 3
- block_order: int32 [144], P('row'), may hold values from 0 to 143, as said below
- directions: float32 [18432, 256], P(('row', 'col')), may hold values from -6 to 6
Outputs:
- normals: float32 [4, 8, 576, 18432], P(None, 'col', None, 'row')
- products: float32 [18432, 256], P(('row', 'col'))
The draws below stay inside these ranges and needn't reach their ends.
Inputs may be any that keep to these rules, and one draw needn't show every extreme that they name: `arc_of_row`: arc numbers never fall along the observations. `block_order`: each aligned group of 36 consecutive entries (the blocks of one block of 4608 unknowns) is a permutation of the positions of that same group.
All inputs are finite; a program needn't handle non-finite values.
Results may differ from the reference program's by a relative error of at most 0.00045.
Values may be sent and summed in bfloat16 or wider, within the bound.
A program may use at most 192 MiB of HBM per device.

```python
import math
import jax
import jax.numpy as jnp
import numpy as np
from jax import lax

M = 18432
BLK = 128
K = 2048
P_SIZE = 256
NQ = 144
QR = 36
N_ROW = 4
N_COL = 8


def draw_block_order(key, part):
    group_keys = jax.random.split(jax.random.fold_in(key, 17), NQ // QR)
    permuted = jax.vmap(lambda single: jax.random.permutation(single, QR))(group_keys)
    offsets = jnp.arange(NQ // QR, dtype=jnp.int32)[:, None] * QR
    return (permuted.astype(jnp.int32) + offsets).reshape(NQ).astype(jnp.int32)


def levels(rng, shape, shards, low, top_value):
    factor_of = 1.0
    for position, parts in shards:
        steps = jax.random.uniform(jax.random.fold_in(jax.random.fold_in(rng, 6), position), (parts,), jnp.float32, low / len(shards), top_value / len(shards))
        factor_of = factor_of * jnp.repeat(jnp.exp(steps), shape[position] // parts).reshape((-1,) + (1,) * (len(shape) - 1 - position))
    return factor_of


def split_up(number_of, total, limit, lean):
    weights = [(1 << 20) // math.isqrt(standing ** lean) + 1 for standing in range(2, number_of + 1)]
    rest, given = total - limit - (number_of - 1), [1] * (number_of - 1)
    while rest > 0:
        free = [i for i in range(number_of - 1) if given[i] < limit]
        mass, remaining = sum([weights[i] for i in free]), rest
        for i in free:
            addition = min(limit - given[i], max(1, remaining * weights[i] // mass), rest)
            given[i] = given[i] + addition
            rest = rest - addition
    return np.array([limit] + given)


def ragged_sizes(stream_key, amount, total, reach, skew):
    if amount == 2:
        one = jax.random.randint(stream_key, (), max(1, total - reach), min(reach, total - 1) + 1)
        return jnp.stack([one, total - one])
    sizes = jnp.asarray(split_up(amount, total, reach, skew), jnp.int32)
    pairs = (amount - 1) // 2
    source_of, sink = sizes[1:1 + 2 * pairs:2], sizes[2:2 + 2 * pairs:2]
    margin = jnp.minimum(source_of - 1, reach - sink)
    moved = jax.random.randint(jax.random.fold_in(stream_key, 1), (pairs,), 0, 1 << 20) % (margin + 1)
    sizes = sizes.at[1:1 + 2 * pairs:2].set(source_of - moved).at[2:2 + 2 * pairs:2].set(sink + moved)
    return sizes[jax.random.permutation(jax.random.fold_in(stream_key, 2), amount)]


def scatter_about(key, extent, scale, reach, shards=(), held_as=jnp.bfloat16):
    drawn = jax.random.normal(key, extent, jnp.float32) * scale
    if len(shards) > 0:
        drawn = levels(key, extent, shards, -0.22, 0.18) * drawn
    return jnp.clip(drawn, min=-reach, max=reach).astype(held_as)


def setup_inputs(seed: int = 0) -> dict:
    keys = jax.random.split(jax.random.key(seed), 7)
    design = scatter_about(keys[0], (M, K), 0.03125, 0.19921875, ((0, 32),))
    arc_filter = scatter_about(keys[1], (K, K), 0.1, 0.59765625)
    arc_of_row = jnp.searchsorted(jnp.cumsum(ragged_sizes(keys[2], K // 8, K, K // 4, 2)), jnp.arange(K), side="right").astype(jnp.int32)
    terr_stored = scatter_about(keys[3], (M, BLK), 0.5, 3.0, ((0, 32),))
    block_order = draw_block_order(jax.random.fold_in(keys[6], 71), 0)
    directions = scatter_about(keys[5], (M, P_SIZE), 1.0, 6.0, ((0, 32),), jnp.float32)
    return {"design": design, "arc_filter": arc_filter, "arc_of_row": arc_of_row, "terr_stored": terr_stored, "block_order": block_order, "directions": directions}


def whiten(design, arc_filter, arc_of_row):
    positions = jnp.arange(arc_filter.shape[0], dtype=jnp.int32)
    keep_mask = (positions[:, None] > positions[None, :]) & (arc_of_row[:, None] == arc_of_row[None, :])
    lower_part = jnp.where(keep_mask, arc_filter, jnp.zeros_like(arc_filter))
    mixed_part = lax.dot_general(design, lower_part, (((1,), (1,)), ((), ())), preferred_element_type=jnp.float32)
    return (design.astype(jnp.float32) + mixed_part).astype(jnp.bfloat16)


def reference(design, arc_filter, arc_of_row, terr_stored, block_order, directions):
    whitened = whiten(design, arc_filter, arc_of_row)
    gram = lax.dot_general(whitened, whitened, (((1,), (1,)), ((), ())), preferred_element_type=jnp.float32)
    stored = terr_stored.astype(jnp.float32).reshape(NQ, BLK, BLK)
    symmetric = jnp.triu(stored) + jnp.swapaxes(jnp.triu(stored, 1), 1, 2)
    ordered = jnp.zeros_like(symmetric).at[block_order].set(symmetric)
    blocked = gram.reshape(NQ, BLK, NQ, BLK)
    diagonal_index = jnp.arange(NQ, dtype=jnp.int32)
    blocked = blocked.at[diagonal_index, :, diagonal_index, :].add(ordered)
    normal_full = blocked.reshape(M, M)
    products = jnp.dot(normal_full, directions, precision=lax.Precision.HIGHEST, preferred_element_type=jnp.float32)
    return normal_full.reshape(N_ROW, N_COL, M // (N_ROW * N_COL), M), products
```

```python
import functools

import jax
import jax.numpy as jnp
import numpy as np
from jax import lax
from jax.experimental import pallas as pl
from jax.experimental.pallas import tpu as pltpu
from jax.sharding import PartitionSpec as P


HIGH = lax.Precision.HIGHEST
NT = (((1,), (1,)), ((), ()))
MESH = pl.DeviceIdType.MESH


def dot_high(a, b):
    return jnp.dot(a, b, precision=HIGH, preferred_element_type=jnp.float32)


def whiten(design, arc_filter, arc_of_row):
    positions = jnp.arange(arc_filter.shape[0], dtype=jnp.int32)
    keep_mask = (positions[:, None] > positions[None, :]) & (
        arc_of_row[:, None] == arc_of_row[None, :]
    )
    lower_part = jnp.where(keep_mask, arc_filter, jnp.zeros_like(arc_filter))
    mixed_part = lax.dot_general(design, lower_part, NT, preferred_element_type=jnp.float32)
    return (design.astype(jnp.float32) + mixed_part).astype(jnp.bfloat16)


def general_body(design, arc_filter, arc_of_row, terr_stored, block_order, directions):
    whitened = whiten(design, arc_filter, arc_of_row)
    own_width = whitened.shape[0]
    rows_block, terr_rows = (
        lax.all_gather(whitened, "col", axis=0, tiled=True),
        lax.all_gather(terr_stored, "col", axis=0, tiled=True),
    )
    cols_block = lax.all_gather(whitened, "row", axis=0, tiled=True)
    normal_tile = lax.dot_general(cols_block, rows_block, NT, preferred_element_type=jnp.float32)
    block_size = terr_rows.shape[1]
    span_rows = terr_rows.shape[0]
    group_count = span_rows // block_size
    row_index = lax.axis_index("row")
    col_index = lax.axis_index("col")
    local_order = block_order - row_index * group_count
    selector = (local_order[None, :] == jnp.arange(group_count, dtype=jnp.int32)[:, None]).astype(
        jnp.float32
    )
    stored = terr_rows.astype(jnp.float32).reshape(group_count, block_size, block_size)
    symmetric = jnp.triu(stored) + jnp.swapaxes(jnp.triu(stored, 1), 1, 2)
    ordered = jnp.einsum("qt,tab->qab", selector, symmetric, precision=HIGH).reshape(
        span_rows, block_size
    )
    own_rows = lax.dynamic_slice_in_dim(ordered, col_index * own_width, own_width, 0)
    positions = col_index * own_width + jnp.arange(own_width, dtype=jnp.int32)
    onehot = (
        (positions // block_size)[:, None] == jnp.arange(group_count, dtype=jnp.int32)[None, :]
    ).astype(jnp.float32)
    terr_added = (onehot[:, :, None] * own_rows[:, None, :]).reshape(own_width, span_rows)
    current = lax.dynamic_slice_in_dim(normal_tile, row_index * own_width, own_width, 0)
    normal_tile = lax.dynamic_update_slice_in_dim(
        normal_tile, current + terr_added, row_index * own_width, 0
    )
    tile_rows = normal_tile.shape[0]
    partial_sum = dot_high(normal_tile, lax.all_gather(directions, "col", axis=0, tiled=True))
    products = lax.psum_scatter(partial_sum, "row", scatter_dimension=0, tiled=True)
    normals = normal_tile.reshape(tile_rows // own_width, 1, own_width, span_rows)
    return (normals, products)


def xor(i, mask):
    return i + mask * (1 - 2 * ((i // mask) % 2))


def split3(x):
    a = x.astype(jnp.bfloat16)
    rest = x - a.astype(jnp.float32)
    b = rest.astype(jnp.bfloat16)
    return a, b, (rest - b.astype(jnp.float32)).astype(jnp.bfloat16)


def wide3(x):
    return jnp.concatenate(split3(x), 1)


def fold3(x):
    n = x.shape[1] // 3
    return x[:, 2 * n :] + x[:, n : 2 * n] + x[:, :n]


def whiten_kernel(d_ref, dp_ref, f_ref, fp_ref, ac_ref, ar_ref, arp_ref, dir_ref, w_ref, v_ref):
    b = pl.program_id(0)
    width = f_ref.shape[0]
    zero = jnp.zeros((width, width), jnp.float32)
    k = lax.broadcasted_iota(jnp.int32, (width, width), 0)
    j = lax.broadcasted_iota(jnp.int32, (width, width), 1)
    keep = (k > j) & (ac_ref[...] == ar_ref[...])
    keep_prev = (ac_ref[...] == arp_ref[...]) & (b > 0)
    here = jnp.where(keep, f_ref[...].astype(jnp.float32), zero).astype(jnp.bfloat16)
    prev = jnp.where(keep_prev, fp_ref[...].astype(jnp.float32), zero).astype(jnp.bfloat16)
    mixed = lax.dot_general(d_ref[...], here, NT, preferred_element_type=jnp.float32)
    mixed += lax.dot_general(dp_ref[...], prev, NT, preferred_element_type=jnp.float32)
    out = (d_ref[...].astype(jnp.float32) + mixed).astype(jnp.bfloat16)
    w_ref[...] = out
    v_ref[...] = fold3(
        lax.dot_general(
            out,
            wide3(dir_ref[...]),
            (((0,), (0,)), ((), ())),
            preferred_element_type=jnp.float32,
        )
    )


def whiten_rows(design, arc_filter, arc_of_row, directions):
    own, total = design.shape
    width = total // 4
    cols = directions.shape[1]
    here = lambda b: (0, b)
    prev = lambda b: (0, jnp.maximum(b - 1, 0))
    row = arc_of_row.reshape(1, total)
    return pl.pallas_call(
        whiten_kernel,
        grid=(total // width,),
        in_specs=[
            pl.BlockSpec((own, width), here),
            pl.BlockSpec((own, width), prev),
            pl.BlockSpec((width, width), lambda b: (b, b)),
            pl.BlockSpec((width, width), lambda b: (b, jnp.maximum(b - 1, 0))),
            pl.BlockSpec((width, 1), lambda b: (b, 0)),
            pl.BlockSpec((1, width), here),
            pl.BlockSpec((1, width), prev),
            pl.BlockSpec((own, cols), lambda b: (0, 0)),
        ],
        out_specs=[
            pl.BlockSpec((own, width), here),
            pl.BlockSpec((width, cols), lambda b: (b, 0)),
        ],
        out_shape=[
            jax.ShapeDtypeStruct((own, total), jnp.bfloat16),
            jax.ShapeDtypeStruct((total, cols), jnp.float32),
        ],
        name="whiten",
        cost_estimate=pl.CostEstimate(
            flops=4 * own * total * width, bytes_accessed=8 * own * total, transcendentals=0
        ),
    )(design, design, arc_filter, arc_filter, arc_of_row.reshape(total, 1), row, row, directions)


def masks_of(n):
    return [1 << i for i in range(n.bit_length() - 1)]


def exchange_kernel(n_row, n_col, parts, w_ref, t_ref, d_ref, v_ref, *refs):
    rows_ref, up1, up2a, up2b, dn1, dn2a, dn2b, terr_ref, edge_ref, vout = refs[:10]
    stage, got, acc, s_loc, s_ring, r_ring, s_row, r_row, s_terr, r_terr, s_v, r_v, s_e, r_e = refs[10:]
    r = lax.axis_index("row")
    c = lax.axis_index("col")
    own = w_ref.shape[0]
    sub = own // parts
    zs = n_col // 2
    z, y = c // 2, c % 2
    place = z + y * (n_col - 1 - 2 * z)

    def col_at(p):
        side = p // zs
        return 2 * (p + side * (n_col - 1 - 2 * p)) + side

    nxt = col_at((place + 1) % n_col)
    prv = col_at((place + n_col - 1) % n_col)
    row_masks, col_masks = masks_of(n_row), masks_of(n_col)
    peers = [(r, nxt), (r, prv)]
    peers += [(xor(r, m), c) for m in row_masks] + [(r, xor(c, m)) for m in col_masks]
    barrier = pltpu.get_barrier_semaphore()
    for peer in peers:
        pl.semaphore_signal(barrier, inc=1, device_id=peer, device_id_type=MESH)
    pl.semaphore_wait(barrier, len(peers))

    def remote(src, dst, ssem, rsem, peer):
        return pltpu.make_async_remote_copy(
            src_ref=src, dst_ref=dst, send_sem=ssem, recv_sem=rsem, device_id=peer,
            device_id_type=MESH,
        )

    def piece(ref, j):
        return ref.at[pl.ds(j * sub, sub)]

    steps = 2 * parts
    half = parts // 2

    def ring(s, way):
        one, two = ((up1, (up2a, up2b)), (dn1, (dn2a, dn2b)))[way]
        j = s % parts
        if s < parts:
            src, dst = piece(w_ref, j), piece(one, j)
        else:
            src, dst = piece(one, j), piece(two[j // half], j % half)
        return remote(src, dst, s_ring.at[way, s], r_ring.at[way, s], (r, (nxt, prv)[way]))

    rings = [[ring(s, way) for way in range(2)] for s in range(steps)]

    sends = []

    def start(copy):
        copy.start()
        sends.append(copy)

    far = n_col // 2

    def terr(k, way):
        src = t_ref if k == 1 else terr_ref.at[(n_col - k + 1) if way == 0 else k - 1]
        at = (n_col - k) if way == 0 else k
        return remote(src, terr_ref.at[at], s_terr.at[way, k - 1], r_terr.at[way, k - 1],
                      (r, (nxt, prv)[way]))

    terrs = {}
    for k in range(1, far + 1):
        terrs[k] = [terr(k, 0)] + ([terr(k, 1)] if k < far else [])

    total = v_ref.shape[0]
    levels = [("row", m) for m in row_masks] + [("col", m) for m in col_masks]
    span = total
    offset = 0
    gives, keeps, backs, spots = [], [], [], []
    base = 0
    for i, (axis, m) in enumerate(levels):
        at = r if axis == "row" else c
        peer = (xor(r, m), c) if axis == "row" else (r, xor(c, m))
        bit = (at // m) % 2
        span //= 2
        give = pl.ds(pl.multiple_of(offset + (1 - bit) * span, span), span)
        offset = offset + bit * span
        keep = pl.ds(pl.multiple_of(offset, span), span)
        src = (v_ref if i == 0 else acc).at[give]
        spot = pl.ds(base, span)
        base += span
        gives.append(remote(src, got.at[spot], s_v.at[i], r_v.at[i], peer))
        n = len(levels)
        backs.append(remote(vout.at[keep], vout.at[keep], s_v.at[n + i], r_v.at[n + i], peer))
        keeps.append(keep)
        spots.append(spot)

    def add(i):
        gives[i].wait()
        held = v_ref if i == 0 else acc
        into = vout if i == len(levels) - 1 else acc
        into[keeps[i]] = held[keeps[i]] + got[spots[i]]

    chain = []
    for i in range(len(levels)):
        chain.append(("give", i))
    for i in reversed(range(len(levels))):
        chain.append(("back", i))

    state = [0]

    def v_next():
        at = state[0]
        if at > len(chain):
            return
        if at > 0:
            kind, i = chain[at - 1]
            if kind == "give":
                add(i)
            else:
                backs[i].wait()
        if at < len(chain):
            kind, i = chain[at]
            (gives if kind == "give" else backs)[i].start()
        state[0] = at + 1

    def row_copy(m, mask, j):
        src = w_ref if m == mask else rows_ref.at[m - mask]
        n = row_index[(m, mask)]
        return remote(piece(src, j), piece(rows_ref.at[m], j), s_row.at[n, j], r_row.at[n, j],
                      (xor(r, mask), c))

    row_index = {}
    order = []
    for mask in reversed(row_masks):
        for m in range(0, n_row, 2 * mask):
            row_index[(m + mask, mask)] = len(row_index)
            order.append((m + mask, mask))

    v_next()
    for copy in terrs[1]:
        start(copy)
    for s in range(2):
        for way in range(2):
            start(rings[s][way])
    mine = pltpu.make_async_copy(w_ref, stage, s_loc.at[0])
    mine.start()
    edge = edge_ref.shape[0]
    edge_at = pl.ds(pl.multiple_of((1 - y) * (own - edge), 8), edge)
    edges = remote(d_ref.at[edge_at], edge_ref, s_e, r_e, (r, xor(c, 1)))
    start(edges)
    v_next()
    copies = {key: [row_copy(*key, j) for j in range(parts)] for key in order}
    first = [key for key in order if key[0] == key[1]]
    later = [key for key in order if key[0] != key[1]]
    for key in first:
        for copy in copies[key]:
            start(copy)
    mine.wait()
    put = pltpu.make_async_copy(stage, rows_ref.at[0], s_loc.at[1])
    put.start()

    hop = 1
    waited = set()
    for s in range(steps):
        for way in range(2):
            rings[s][way].wait_recv()
        if s % 2 == 0 or s > steps - 4:
            v_next()
        if s % 2 == 1 and hop <= far:
            for copy in terrs[hop]:
                copy.wait_recv()
            hop += 1
            if hop <= far:
                for copy in terrs[hop]:
                    start(copy)
        if s + 2 < steps:
            for way in range(2):
                start(rings[s + 2][way])
        j = s - 2
        if 0 <= j < parts:
            for key in later:
                m, mask = key
                up = [k for k in order if k[0] == m - mask][0]
                if (up, j) not in waited:
                    copies[up][j].wait_recv()
                    waited.add((up, j))
                start(copies[key][j])
    while hop <= far:
        for copy in terrs[hop]:
            copy.wait_recv()
        hop += 1
        if hop <= far:
            for copy in terrs[hop]:
                start(copy)
    while state[0] <= len(chain):
        v_next()
    for key in order:
        for j in range(parts):
            if (key, j) not in waited:
                copies[key][j].wait_recv()
    edges.wait_recv()
    put.wait()
    for copy in sends:
        copy.wait_send()


def exchange(n_row, n_col, whitened, terr_stored, directions, partial):
    own, total = whitened.shape
    cols = directions.shape[1]
    block = terr_stored.shape[1]
    parts = 6
    far = n_col // 2
    any_spec = pl.BlockSpec(memory_space=pl.ANY)
    vmem = pl.BlockSpec(memory_space=pltpu.VMEM)
    whole = jax.ShapeDtypeStruct((own, total), jnp.bfloat16)
    part = jax.ShapeDtypeStruct((own // 2, total), jnp.bfloat16)
    levels = n_row.bit_length() + n_col.bit_length() - 2
    moves = n_row - 1
    dma = pltpu.SemaphoreType.DMA
    return pl.pallas_call(
        functools.partial(exchange_kernel, n_row, n_col, parts),
        in_specs=[any_spec, any_spec, any_spec, vmem],
        out_specs=[any_spec] * 9 + [vmem],
        out_shape=[
            jax.ShapeDtypeStruct((n_row, own, total), jnp.bfloat16),
            whole, part, part, whole, part, part,
            jax.ShapeDtypeStruct((n_col, own, block), jnp.bfloat16),
            jax.ShapeDtypeStruct((block // 2, cols), jnp.float32),
            jax.ShapeDtypeStruct((total, cols), jnp.float32),
        ],
        scratch_shapes=[
            pltpu.VMEM((own, total), jnp.bfloat16),
            pltpu.VMEM((total, cols), jnp.float32),
            pltpu.VMEM((total, cols), jnp.float32),
            dma((2,)),
            dma((2, 2 * parts)), dma((2, 2 * parts)),
            dma((moves, parts)), dma((moves, parts)),
            dma((2, far)), dma((2, far)),
            dma((2 * levels,)), dma((2 * levels,)),
            dma(()), dma(()),
        ],
        name="exchange",
        compiler_params=pltpu.CompilerParams(
            collective_id=0, has_side_effects=True, vmem_limit_bytes=56 * 1024 * 1024
        ),
        cost_estimate=pl.CostEstimate(
            flops=1000000, bytes_accessed=40 * own * total, transcendentals=0
        ),
    )(whitened, terr_stored, directions, partial)


def products_kernel(order_ref, spot_ref, s_ref, t0_ref, t_ref, w_ref, v_ref, d_ref, e_ref,
                    p_ref, o_ref, inv_ref):
    own, span = o_ref.shape
    half = e_ref.shape[0]
    block = 2 * half
    per = own // half
    count = order_ref.shape[0]

    @pl.loop(0, count)
    def _(t):
        inv_ref[order_ref[t]] = t

    side = s_ref[1]
    o_ref[...] = jnp.zeros(o_ref.shape, o_ref.dtype)
    p_ref[...] = fold3(
        jnp.dot(w_ref[...], wide3(v_ref[...]), preferred_element_type=jnp.float32)
    )
    k = lax.broadcasted_iota(jnp.int32, (block, block), 0)
    j = lax.broadcasted_iota(jnp.int32, (block, block), 1)

    def stored(g):
        slot, at = spot_ref[g // per], g % per
        there = pl.ds(pl.multiple_of(at * half, half), half)
        return jnp.where(
            slot == 0,
            t0_ref[there, :].astype(jnp.float32),
            t_ref[slot, there, :].astype(jnp.float32),
        )

    edge = e_ref[...]
    for q in range(span // block):
        lo = 2 * q

        @pl.when((lo + 1 >= side * per) & (lo < side * per + per))
        def _(q=q, lo=lo):
            t = inv_ref[s_ref[0] + q]
            s = jnp.concatenate([stored(2 * t), stored(2 * t + 1)], 0)
            sym = jnp.where(k <= j, s, 0.0) + jnp.where(k < j, s, 0.0).T
            for h in range(2):
                i = lo + h - side * per

                @pl.when((i >= 0) & (i < per))
                def _():
                    mine = pl.ds(pl.multiple_of(i * half, half), half)
                    o_ref[mine, q * block : (q + 1) * block] = sym[h * half : (h + 1) * half]
                    other = i + 1 - 2 * h
                    inside = (other >= 0) & (other < per)
                    safe = jnp.minimum(jnp.maximum(other, 0), per - 1)
                    pair = d_ref[pl.ds(pl.multiple_of(safe * half, half), half), :]
                    pair = jnp.where(inside, pair, edge)
                    this = d_ref[mine, :]
                    near = jnp.concatenate([pair, this] if h else [this, pair], 0)
                    rows = sym[h * half : (h + 1) * half].astype(jnp.bfloat16)
                    p_ref[mine, :] += fold3(
                        jnp.dot(rows, wide3(near), preferred_element_type=jnp.float32)
                    )


def products_job(order, spots, scalars, terr_stored, terr_all, whitened, v, directions, edge):
    own = whitened.shape[0]
    cols = directions.shape[1]
    vmem = pl.BlockSpec(memory_space=pltpu.VMEM)
    smem = pl.BlockSpec(memory_space=pltpu.SMEM)
    return pl.pallas_call(
        products_kernel,
        in_specs=[smem] * 3 + [vmem] * 6,
        out_specs=[vmem] * 2,
        out_shape=[
            jax.ShapeDtypeStruct((own, cols), jnp.float32),
            jax.ShapeDtypeStruct((own, 2 * own), jnp.float32),
        ],
        scratch_shapes=[pltpu.SMEM((order.shape[0],), jnp.int32)],
        name="products",
        compiler_params=pltpu.CompilerParams(vmem_limit_bytes=40 * 1024 * 1024),
        cost_estimate=pl.CostEstimate(
            flops=6 * own * whitened.shape[1] * cols, bytes_accessed=10000000, transcendentals=0
        ),
    )(order, spots, scalars, terr_stored, terr_all, whitened, v, directions, edge)


def tile_kernel(wants, sources, width, first, terr, s_ref, *refs):
    n = 1 + max(at for pair in sources.values() for at, _ in pair)
    bufs = refs[:n]
    a_ref = refs[n]
    rest = refs[n + 1 :]
    if terr:
        t_ref, rest = rest[0], rest[1:]
    o_hbm, b_ref, o_ref, sem, o_sem = rest if first else rest[1:]
    i = pl.program_id(0)
    steps = pl.num_programs(0)
    own = a_ref.shape[1]
    half = own // 2
    span = b_ref.shape[0]
    lo = s_ref[4]

    def copy(k, y, h):
        at, row = sources[k][h]
        return pltpu.make_async_copy(
            bufs[at].at[pl.ds(row, half)],
            b_ref.at[pl.ds((2 * y + h) * half, half)],
            sem.at[2 * y + h],
        )

    @pl.when(i == 0)
    def _():
        for y in range(2):
            for h in range(2):
                needed = wants(s_ref, y, h)
                for k in sources:

                    @pl.when((s_ref[1 + y] == k) & needed)
                    def _():
                        copy(k, y, h).start()

        for y in range(2):
            for h in range(2):

                @pl.when(wants(s_ref, y, h))
                def _():
                    copy(next(iter(sources)), y, h).wait()

    slot = i % 2

    def out(i, slot):
        return pltpu.make_async_copy(
            o_ref.at[slot],
            o_hbm.at[
                pl.ds(pl.multiple_of(s_ref[6 + i] * own, own), own),
                pl.ds(pl.multiple_of(s_ref[0] * span + lo, 128), width),
            ],
            o_sem.at[slot],
        )

    @pl.when(i >= 2)
    def _():
        out(i - 2, slot).wait()

    o_ref[slot] = lax.dot_general(
        a_ref[0],
        b_ref[pl.ds(pl.multiple_of(lo, 128), width), :],
        NT,
        preferred_element_type=jnp.float32,
    )
    if terr:

        @pl.when((i == 0) & (s_ref[3] == 1))
        def _():
            o_ref[slot] += t_ref[...]

    out(i, slot).start()

    @pl.when(i == steps - 1)
    def _():
        out(i - 1, 1 - slot).wait()
        out(i, slot).wait()


def tile_job(scalars, wants, cands, bufs, rows, width, terr, out):
    count, own, total = rows.shape
    span = 2 * own
    first = not isinstance(out, jax.Array)
    any_spec = pl.BlockSpec(memory_space=pl.ANY)
    arrays, sources = [], {}
    for k in cands:
        pair = []
        for array, row in bufs[k]:
            at = [i for i, a in enumerate(arrays) if a is array]
            if not at:
                arrays.append(array)
                at = [len(arrays) - 1]
            pair.append((at[0], row))
        sources[k] = pair
    operands = arrays + [rows]
    in_specs = [any_spec] * len(arrays) + [
        pl.BlockSpec((1, own, total), lambda i, s: (i, 0, 0)),
    ]
    if terr is not None:
        operands.append(terr)
        in_specs.append(pl.BlockSpec((own, span), lambda i, s: (0, 0)))
    shape = out
    alias = {}
    if not first:
        alias = {1 + len(operands): 0}
        operands.append(out)
        in_specs.append(any_spec)
        shape = jax.ShapeDtypeStruct(out.shape, out.dtype)
    return pl.pallas_call(
        functools.partial(tile_kernel, wants, sources, width, first, terr is not None),
        grid_spec=pltpu.PrefetchScalarGridSpec(
            num_scalar_prefetch=1,
            grid=(count,),
            in_specs=in_specs,
            out_specs=any_spec,
            scratch_shapes=[
                pltpu.VMEM((span, total), jnp.bfloat16),
                pltpu.VMEM((2, own, width), jnp.float32),
                pltpu.SemaphoreType.DMA((4,)),
                pltpu.SemaphoreType.DMA((2,)),
            ],
        ),
        out_shape=shape,
        input_output_aliases=alias,
        compiler_params=pltpu.CompilerParams(vmem_limit_bytes=48 * 1024 * 1024),
        cost_estimate=pl.CostEstimate(
            flops=2 * count * own * width * total,
            bytes_accessed=2 * count * own * total + 4 * count * own * width,
            transcendentals=0,
        ),
    )(scalars, *operands)


def ring_body(n_row, n_col, design, arc_filter, arc_of_row, terr_stored, block_order, directions):
    own, _ = design.shape
    block = terr_stored.shape[1]
    r = lax.axis_index("row")
    c = lax.axis_index("col")
    zs = n_col // 2
    half = own // 2
    far = n_col // 2

    def hop(a, perm):
        return lax.ppermute(a, "col", perm)

    col_of = [2 * p if p < zs else 2 * (n_col - 1 - p) + 1 for p in range(n_col)]
    pos_of = [0] * n_col
    for p, col in enumerate(col_of):
        pos_of[col] = p
    forward = [(col_of[p], col_of[(p + 1) % n_col]) for p in range(n_col)]
    backward = [(d, s) for s, d in forward]

    whitened, partial = whiten_rows(design, arc_filter, arc_of_row, directions)
    rows, up1, up2a, up2b, dn1, dn2a, dn2b, terr_all, edge, v = exchange(
        n_row, n_col, whitened, terr_stored, directions, partial
    )
    bufs = {
        0: [(whitened, 0), (whitened, half)],
        1: [(dn1, 0), (dn1, half)],
        2: [(dn2a, 0), (dn2b, 0)],
        n_col - 1: [(up1, 0), (up1, half)],
        n_col - 2: [(up2a, 0), (up2b, 0)],
    }
    for k in range(3, far + 1):
        before_up, before_dn = bufs[n_col - k + 1], bufs[k - 1]
        if k < far:
            ua = hop(before_up[0][0], forward)
            db = hop(before_dn[1][0], backward)
            ub = hop(before_up[1][0], forward)
            da = hop(before_dn[0][0], backward)
            bufs[n_col - k] = [(ua, 0), (ub, 0)]
            bufs[k] = [(da, 0), (db, 0)]
        else:
            ua = hop(before_up[0][0], forward)
            db = hop(before_dn[1][0], backward)
            bufs[k] = [(ua, 0), (db, 0)]

    per_pair = 2 * own // block
    count = per_pair * zs
    spots = np.array([[(pos_of[d] - pos_of[s]) % n_col for d in range(n_col)] for s in range(n_col)])
    local_order = block_order - r * count
    products, terr = products_job(
        local_order,
        jnp.asarray(spots, jnp.int32)[c],
        jnp.stack([(c // 2) * per_pair, c % 2]).astype(jnp.int32),
        terr_stored, terr_all, whitened, v, directions, edge,
    )

    wide = own // 128 * 128
    table = np.zeros((zs, n_col, 6), np.int32)
    for col in range(n_col):
        jobs = []
        for zz in range(zs):
            ks = [(pos_of[2 * zz + yy] - pos_of[col]) % n_col for yy in range(2)]
            ready = max(min(k, n_col - k) for k in ks)
            jobs.append((ready, zz, ks))
        for j, (_, zz, ks) in enumerate(sorted(jobs)):
            late = ks.index(far) if far in ks else 0
            table[j, col] = [zz, ks[0], ks[1], int(zz == col // 2), 0, late]
    row_spots = jnp.bitwise_xor(r, jnp.arange(n_row, dtype=jnp.int32))
    out = jax.ShapeDtypeStruct((n_row * own, n_col * own), jnp.float32)

    def job(j, wants, cands, width, terr, out, spot=None):
        use = table[j].copy()
        if spot is not None:
            use[:, 4] = [spot(late) for late in use[:, 5]]
        scalars = jnp.concatenate([jnp.asarray(use)[c], row_spots])
        return tile_job(scalars, wants, cands, bufs, rows, width, terr, out)

    every = lambda s, y, h: s[5] >= 0
    early = lambda s, y, h: s[5] == 1 - y
    tail = lambda s, y, h: (s[5] == y) | (h == 1 - y)
    for j in range(zs - 1):
        cands = tuple(sorted(set(table[j, :, 1:3].ravel().tolist())))
        out = job(j, every, cands, 2 * own, terr, out)
    cands = set(table[zs - 1, :, 1:3].ravel().tolist())
    out = job(zs - 1, early, tuple(sorted(cands - {far})), wide, None, out,
              lambda late: 0 if late == 1 else 2 * own - wide)
    out = job(zs - 1, tail, tuple(sorted(cands)), 2 * own - wide, None, out,
              lambda late: wide if late == 1 else 0)
    return out.reshape(n_row, 1, own, n_col * own), products


def power_of_two(n):
    return n > 1 and n & (n - 1) == 0


def solution(mesh):
    n_row, n_col = mesh.shape["row"], mesh.shape["col"]

    def body(design, arc_filter, arc_of_row, terr_stored, block_order, directions):
        args = (design, arc_filter, arc_of_row, terr_stored, block_order, directions)
        own, block = design.shape[0], terr_stored.shape[1]
        aligned = own % 192 == 0 and own % block == block // 2 and (2 * own) % 128 == 0
        if power_of_two(n_row) and power_of_two(n_col) and n_col > 6 and aligned:
            return ring_body(n_row, n_col, *args)
        return general_body(*args)

    return jax.shard_map(
        body,
        mesh=mesh,
        in_specs=(
            P(("row", "col"), None),
            P(),
            P(),
            P(("row", "col"), None),
            P("row"),
            P(("row", "col"), None),
        ),
        out_specs=(P(None, "col", None, "row"), P(("row", "col"), None)),
        check_vma=False,
    )
```

```python
import functools

import jax
import jax.numpy as jnp
import numpy as np
from jax import lax
from jax.experimental import pallas as pl
from jax.experimental.pallas import tpu as pltpu
from jax.sharding import PartitionSpec as P


HIGH = lax.Precision.HIGHEST
NT = (((1,), (1,)), ((), ()))
MESH = pl.DeviceIdType.MESH


def dot_high(a, b):
    return jnp.dot(a, b, precision=HIGH, preferred_element_type=jnp.float32)


def whiten(design, arc_filter, arc_of_row):
    positions = jnp.arange(arc_filter.shape[0], dtype=jnp.int32)
    keep_mask = (positions[:, None] > positions[None, :]) & (
        arc_of_row[:, None] == arc_of_row[None, :]
    )
    lower_part = jnp.where(keep_mask, arc_filter, jnp.zeros_like(arc_filter))
    mixed_part = lax.dot_general(design, lower_part, NT, preferred_element_type=jnp.float32)
    return (design.astype(jnp.float32) + mixed_part).astype(jnp.bfloat16)


def general_body(design, arc_filter, arc_of_row, terr_stored, block_order, directions):
    whitened = whiten(design, arc_filter, arc_of_row)
    own_width = whitened.shape[0]
    rows_block, terr_rows = (
        lax.all_gather(whitened, "col", axis=0, tiled=True),
        lax.all_gather(terr_stored, "col", axis=0, tiled=True),
    )
    cols_block = lax.all_gather(whitened, "row", axis=0, tiled=True)
    normal_tile = lax.dot_general(cols_block, rows_block, NT, preferred_element_type=jnp.float32)
    block_size = terr_rows.shape[1]
    span_rows = terr_rows.shape[0]
    group_count = span_rows // block_size
    row_index = lax.axis_index("row")
    col_index = lax.axis_index("col")
    local_order = block_order - row_index * group_count
    selector = (local_order[None, :] == jnp.arange(group_count, dtype=jnp.int32)[:, None]).astype(
        jnp.float32
    )
    stored = terr_rows.astype(jnp.float32).reshape(group_count, block_size, block_size)
    symmetric = jnp.triu(stored) + jnp.swapaxes(jnp.triu(stored, 1), 1, 2)
    ordered = jnp.einsum("qt,tab->qab", selector, symmetric, precision=HIGH).reshape(
        span_rows, block_size
    )
    own_rows = lax.dynamic_slice_in_dim(ordered, col_index * own_width, own_width, 0)
    positions = col_index * own_width + jnp.arange(own_width, dtype=jnp.int32)
    onehot = (
        (positions // block_size)[:, None] == jnp.arange(group_count, dtype=jnp.int32)[None, :]
    ).astype(jnp.float32)
    terr_added = (onehot[:, :, None] * own_rows[:, None, :]).reshape(own_width, span_rows)
    current = lax.dynamic_slice_in_dim(normal_tile, row_index * own_width, own_width, 0)
    normal_tile = lax.dynamic_update_slice_in_dim(
        normal_tile, current + terr_added, row_index * own_width, 0
    )
    tile_rows = normal_tile.shape[0]
    partial_sum = dot_high(normal_tile, lax.all_gather(directions, "col", axis=0, tiled=True))
    products = lax.psum_scatter(partial_sum, "row", scatter_dimension=0, tiled=True)
    normals = normal_tile.reshape(tile_rows // own_width, 1, own_width, span_rows)
    return (normals, products)


def xor(i, mask):
    return i + mask * (1 - 2 * ((i // mask) % 2))


def xor_all(i, mask, n):
    for m in masks_of(n):
        if mask & m:
            i = xor(i, m)
    return i


def split3(x):
    a = x.astype(jnp.bfloat16)
    rest = x - a.astype(jnp.float32)
    b = rest.astype(jnp.bfloat16)
    return a, b, (rest - b.astype(jnp.float32)).astype(jnp.bfloat16)


def wide3(x):
    return jnp.concatenate(split3(x), 1)


def fold3(x):
    n = x.shape[1] // 3
    return x[:, 2 * n :] + x[:, n : 2 * n] + x[:, :n]


def whiten_kernel(d_ref, dp_ref, f_ref, fp_ref, ar_ref, arp_ref, w_ref):
    b = pl.program_id(0)
    width = f_ref.shape[0]
    zero = jnp.zeros((width, width), jnp.float32)
    k = lax.broadcasted_iota(jnp.int32, (width, width), 0)
    j = lax.broadcasted_iota(jnp.int32, (width, width), 1)
    column = jnp.broadcast_to(ar_ref[...], (128, width)).T[:, :1]
    keep = (k > j) & (column == ar_ref[...])
    keep_prev = (column == arp_ref[...]) & (b > 0)
    here = jnp.where(keep, f_ref[...].astype(jnp.float32), zero).astype(jnp.bfloat16)
    prev = jnp.where(keep_prev, fp_ref[...].astype(jnp.float32), zero).astype(jnp.bfloat16)
    mixed = lax.dot_general(d_ref[...], here, NT, preferred_element_type=jnp.float32)
    mixed += lax.dot_general(dp_ref[...], prev, NT, preferred_element_type=jnp.float32)
    w_ref[...] = (d_ref[...].astype(jnp.float32) + mixed).astype(jnp.bfloat16)


def whiten_rows(design, arc_filter, arc_of_row):
    own, total = design.shape
    width = total // 4
    here = lambda b: (0, b)
    prev = lambda b: (0, jnp.maximum(b - 1, 0))
    row = arc_of_row.reshape(1, total)
    return pl.pallas_call(
        whiten_kernel,
        grid=(total // width,),
        in_specs=[
            pl.BlockSpec((own, width), here),
            pl.BlockSpec((own, width), prev),
            pl.BlockSpec((width, width), lambda b: (b, b)),
            pl.BlockSpec((width, width), lambda b: (b, jnp.maximum(b - 1, 0))),
            pl.BlockSpec((1, width), here),
            pl.BlockSpec((1, width), prev),
        ],
        out_specs=pl.BlockSpec((own, width), here),
        out_shape=jax.ShapeDtypeStruct((own, total), jnp.bfloat16),
        name="whiten",
        cost_estimate=pl.CostEstimate(
            flops=4 * own * total * width, bytes_accessed=8 * own * total, transcendentals=0
        ),
    )(design, design, arc_filter, arc_filter, row, row)


def masks_of(n):
    return [1 << i for i in range(n.bit_length() - 1)]


def exchange_kernel(n_row, n_col, parts, w_ref, t_ref, d_ref, *refs):
    rows_ref, up1, up2a, up2b, dn1, dn2a, dn2b, terr_ref, edge_ref, side_ref, pre_ref, vout = refs[:12]
    b_ref, a_ref, o_ref, got, acc = refs[12:17]
    s_loc, s_ring, r_ring, s_row, r_row, s_terr, r_terr, s_v, r_v, s_e, r_e = refs[17:]
    r = lax.axis_index("row")
    c = lax.axis_index("col")
    own, width = w_ref.shape
    sub = own // parts
    zs = n_col // 2
    z, y = c // 2, c % 2
    place = z + y * (n_col - 1 - 2 * z)
    by_up = place % zs == 0
    by_down = place % zs == zs - 1
    inner = (place % zs > 0) & (place % zs < zs - 1)

    def col_at(p):
        side = p // zs
        return 2 * (p + side * (n_col - 1 - 2 * p)) + side

    nxt = col_at((place + 1) % n_col)
    prv = col_at((place + n_col - 1) % n_col)
    row_masks = masks_of(n_row)
    peers = [(r, nxt), (r, prv)]
    peers += [(xor(r, m), c) for m in row_masks] + [(r, xor(c, 1))]
    peers += [(r, 2 * xor_all(z, m, zs) + y) for m in range(1, zs)]
    barrier = pltpu.get_barrier_semaphore()
    for peer in peers:
        pl.semaphore_signal(barrier, inc=1, device_id=peer, device_id_type=MESH)
    pl.semaphore_wait(barrier, len(peers))

    def remote(src, dst, ssem, rsem, peer):
        return pltpu.make_async_remote_copy(
            src_ref=src, dst_ref=dst, send_sem=ssem, recv_sem=rsem, device_id=peer,
            device_id_type=MESH,
        )

    def piece(ref, j):
        return ref.at[pl.ds(j * sub, sub)]

    sends = []

    def start(copy):
        copy.start()
        sends.append(copy)

    steps = 2 * parts
    half = parts // 2
    ahead = 4

    def ring(s, way):
        one, two = ((up1, (up2a, up2b)), (dn1, (dn2a, dn2b)))[way]
        j = s % parts
        if s < parts:
            src, dst = piece(w_ref, j), piece(one, j)
        else:
            src, dst = piece(one, j), piece(two[j // half], j % half)
        return remote(src, dst, s_ring.at[way, s], r_ring.at[way, s], (r, (nxt, prv)[way]))

    rings = [[ring(s, way) for way in range(2)] for s in range(steps)]
    for s in range(ahead):
        for way in range(2):
            start(rings[s][way])

    mine = pl.ds(pl.multiple_of(y * own, own), own)
    other = pl.ds(pl.multiple_of((1 - y) * own, own), own)
    load = pltpu.make_async_copy(w_ref, b_ref.at[mine], s_loc.at[0])
    load.start()

    far = n_col // 2

    def terr(k, way):
        src = t_ref if k == 1 else terr_ref.at[(n_col - k + 1) if way == 0 else k - 1]
        at = (n_col - k) if way == 0 else k
        return remote(src, terr_ref.at[at], s_terr.at[way, k - 1], r_terr.at[way, k - 1],
                      (r, (nxt, prv)[way]))

    terrs = {}
    for k in range(1, far + 1):
        terrs[k] = [terr(k, 0)] + ([terr(k, 1)] if k < far else [])
    for copy in terrs[1]:
        start(copy)
    edge = edge_ref.shape[0]
    edge_at = pl.ds(pl.multiple_of((1 - y) * (own - edge), edge), edge)
    edges = remote(d_ref.at[edge_at], edge_ref, s_e.at[0], r_e.at[0], (r, xor(c, 1)))
    start(edges)
    across = remote(w_ref, side_ref, s_e.at[1], r_e.at[1], (r, xor(c, 1)))

    @pl.when(inner)
    def _():
        across.start()

    order = []
    for mask in reversed(row_masks):
        for m in range(0, n_row, 2 * mask):
            order.append((m + mask, mask))

    def row_copy(key, j):
        m, mask = key
        n = order.index(key)
        src = w_ref if m == mask else rows_ref.at[m - mask]
        return remote(piece(src, j), piece(rows_ref.at[m], j), s_row.at[n, j], r_row.at[n, j],
                      (xor(r, mask), c))

    copies = {key: [row_copy(key, j) for j in range(parts)] for key in order}
    filled = {m: (m, mask) for m, mask in order}
    later = [key for key in order if key[0] != key[1]]
    waited = set()

    def row_wait(key, j):
        if (key, j) not in waited:
            copies[key][j].wait_recv()
            waited.add((key, j))

    load.wait()
    put = pltpu.make_async_copy(b_ref.at[mine], rows_ref.at[0], s_loc.at[1])
    put.start()
    dirs = wide3(d_ref[...])
    chunk = width // 8

    @pl.loop(0, 8)
    def _(t):
        span = pl.ds(pl.multiple_of(t * chunk, chunk), chunk)
        acc[span, :] = fold3(
            lax.dot_general(
                b_ref[mine, span], dirs, (((0,), (0,)), ((), ())),
                preferred_element_type=jnp.float32,
            )
        )

    levels = [((xor(r, m), c), (r // m) % 2) for m in row_masks] + [((r, xor(c, 1)), y)]
    n = len(levels)
    span = width
    offset = base = 0
    gives, keeps, spots = [], [], []
    for i, (peer, bit) in enumerate(levels):
        span //= 2
        give = pl.ds(pl.multiple_of(offset + (1 - bit) * span, span), span)
        offset = offset + bit * span
        keep = pl.ds(pl.multiple_of(offset, span), span)
        spot = pl.ds(base, span)
        base += span
        gives.append(remote(acc.at[give], got.at[spot], s_v.at[i], r_v.at[i], peer))
        keeps.append(keep)
        spots.append(spot)
    bit = span // zs
    at_out = pl.ds(pl.multiple_of(y * span + z * bit, bit), bit)
    side_out = pl.ds(pl.multiple_of(y * span, span), span)
    fans, backs = [], []
    for m in range(1, zs):
        zz = xor_all(z, m, zs)
        peer = (r, 2 * zz + y)
        give = pl.ds(pl.multiple_of(offset + zz * bit, bit), bit)
        spot = pl.ds(base + (m - 1) * bit, bit)
        at = n + 2 * m - 2
        fans.append(remote(acc.at[give], got.at[spot], s_v.at[at], r_v.at[at], peer))
        backs.append(
            remote(vout.at[at_out], vout.at[at_out], s_v.at[at + 1], r_v.at[at + 1], peer)
        )
    at = n + 2 * zs - 2
    last = remote(vout.at[side_out], vout.at[side_out], s_v.at[at], r_v.at[at], (r, xor(c, 1)))

    def finish(i):
        gives[i].wait()
        acc[keeps[i]] = acc[keeps[i]] + got[spots[i]]

    def fan_in():
        for copy in fans:
            copy.wait()
        mid = acc[pl.ds(pl.multiple_of(offset + z * bit, bit), bit)]
        for m in range(1, zs):
            mid = mid + got[base + (m - 1) * bit : base + m * bit]
        vout[at_out] = mid

    def each(copies, method):
        for copy in copies:
            getattr(copy, method)()

    todo = [lambda: gives[0].start()]
    for i in range(1, n):
        todo.append(lambda i=i: (finish(i - 1), gives[i].start()))
    todo.append(lambda: (finish(n - 1), each(fans, "start")))
    todo.append(lambda: (fan_in(), each(backs, "start")))
    todo.append(lambda: (each(backs, "wait"), last.start()))
    todo.append(lambda: last.wait())

    def v_next():
        if todo:
            todo.pop(0)()

    v_next()
    v_next()
    for key in order:
        if key[0] == key[1]:
            for copy in copies[key]:
                start(copy)

    def other_load(ref):
        return pltpu.make_async_copy(ref, b_ref.at[other], s_loc.at[2])

    def other_start():
        @pl.when(inner)
        def _():
            across.wait()
            other_load(side_ref).start()

        @pl.when(by_up)
        def _():
            other_load(up1).start()

        @pl.when(by_down)
        def _():
            other_load(dn1).start()

    def a_load(m):
        return pltpu.make_async_copy(rows_ref.at[m], a_ref.at[m % 2], s_loc.at[3 + m % 2])

    def o_store(m):
        return pltpu.make_async_copy(o_ref.at[m % 2], pre_ref.at[m], s_loc.at[5 + m % 2])

    def own_tile(m):
        a_load(m).wait()
        if m == 0:
            other_load(w_ref).wait()
        if m >= 2:
            o_store(m - 2).wait()
        o_ref[m % 2] = lax.dot_general(
            a_ref[m % 2], b_ref[...], NT, preferred_element_type=jnp.float32
        )
        o_store(m).start()

    hop = 1
    lag = parts // 2
    v_at = [ahead + i * (ahead + 1) for i in range(len(todo))]
    for s in range(steps):
        for way in range(2):
            rings[s][way].wait_recv()
        if s in v_at:
            v_next()
        if s % 3 == 2 and hop <= far:
            for copy in terrs[hop]:
                copy.wait_recv()
            hop += 1
            if hop <= far:
                for copy in terrs[hop]:
                    start(copy)
        if s + ahead < steps:
            for way in range(2):
                start(rings[s + ahead][way])
        j = s - lag
        if 0 <= j < parts:
            for key in later:
                row_wait(filled[key[0] - key[1]], j)
                start(copies[key][j])
        if s == parts - 1:
            other_start()
            put.wait()
            a_load(0).start()
        if s == parts + 1:
            for j in range(parts):
                row_wait(filled[1], j)
            a_load(1).start()
            own_tile(0)
        if s == parts + 3:
            own_tile(1)
        if s == parts + lag:
            for m in range(2, n_row):
                for j in range(parts):
                    row_wait(filled[m], j)
            a_load(2).start()
        for m in range(2, n_row):
            if s == parts + lag + m - 1:
                if m + 1 < n_row:
                    a_load(m + 1).start()
                own_tile(m)
    while hop <= far:
        for copy in terrs[hop]:
            copy.wait_recv()
        hop += 1
        if hop <= far:
            for copy in terrs[hop]:
                start(copy)
    while todo:
        v_next()
    edges.wait_recv()
    for m in (n_row - 2, n_row - 1):
        o_store(m).wait()
    for copy in sends:
        copy.wait_send()


def exchange(n_row, n_col, whitened, terr_stored, directions):
    own, total = whitened.shape
    cols = directions.shape[1]
    block = terr_stored.shape[1]
    parts = 12
    far = n_col // 2
    any_spec = pl.BlockSpec(memory_space=pl.ANY)
    vmem = pl.BlockSpec(memory_space=pltpu.VMEM)
    whole = jax.ShapeDtypeStruct((own, total), jnp.bfloat16)
    part = jax.ShapeDtypeStruct((own // 2, total), jnp.bfloat16)
    levels = n_row.bit_length() + n_col
    moves = n_row - 1
    dma = pltpu.SemaphoreType.DMA
    return pl.pallas_call(
        functools.partial(exchange_kernel, n_row, n_col, parts),
        in_specs=[any_spec, any_spec, vmem],
        out_specs=[any_spec] * 11 + [vmem],
        out_shape=[
            jax.ShapeDtypeStruct((n_row, own, total), jnp.bfloat16),
            whole, part, part, whole, part, part,
            jax.ShapeDtypeStruct((n_col, own, block), jnp.bfloat16),
            jax.ShapeDtypeStruct((block // 2, cols), jnp.float32),
            whole,
            jax.ShapeDtypeStruct((n_row, own, 2 * own), jnp.float32),
            jax.ShapeDtypeStruct((total // n_row, cols), jnp.float32),
        ],
        scratch_shapes=[
            pltpu.VMEM((2 * own, total), jnp.bfloat16),
            pltpu.VMEM((2, own, total), jnp.bfloat16),
            pltpu.VMEM((2, own, 2 * own), jnp.float32),
            pltpu.VMEM((total, cols), jnp.float32),
            pltpu.VMEM((total, cols), jnp.float32),
            dma((7,)),
            dma((2, 2 * parts)), dma((2, 2 * parts)),
            dma((moves, parts)), dma((moves, parts)),
            dma((2, far)), dma((2, far)),
            dma((levels,)), dma((levels,)),
            dma((2,)), dma((2,)),
        ],
        name="exchange",
        compiler_params=pltpu.CompilerParams(
            collective_id=0, has_side_effects=True, vmem_limit_bytes=56 * 1024 * 1024
        ),
        cost_estimate=pl.CostEstimate(
            flops=1000000, bytes_accessed=40 * own * total, transcendentals=0
        ),
    )(whitened, terr_stored, directions)


def products_kernel(order_ref, spot_ref, s_ref, t0_ref, t_ref, w_ref, d_ref, e_ref, *refs):
    v_refs = refs[:-3]
    p_ref, o_ref, inv_ref = refs[-3:]
    own, span = o_ref.shape
    half = e_ref.shape[0]
    block = 2 * half
    per = own // half
    count = order_ref.shape[0]

    @pl.loop(0, count)
    def _(t):
        inv_ref[order_ref[t]] = t

    side = s_ref[1]
    o_ref[...] = jnp.zeros(o_ref.shape, o_ref.dtype)
    for m, v_ref in enumerate(v_refs):
        size = v_ref.shape[0]
        part = w_ref[:, pl.ds(pl.multiple_of(s_ref[2 + m], size), size)]
        term = fold3(jnp.dot(part, wide3(v_ref[...]), preferred_element_type=jnp.float32))
        p_ref[...] = p_ref[...] + term if m else term
    k = lax.broadcasted_iota(jnp.int32, (block, block), 0)
    j = lax.broadcasted_iota(jnp.int32, (block, block), 1)

    def stored(g):
        slot, at = spot_ref[g // per], g % per
        there = pl.ds(pl.multiple_of(at * half, half), half)
        return jnp.where(
            slot == 0,
            t0_ref[there, :].astype(jnp.float32),
            t_ref[slot, there, :].astype(jnp.float32),
        )

    edge = e_ref[...]
    for q in range(span // block):
        lo = 2 * q

        @pl.when((lo + 1 >= side * per) & (lo < side * per + per))
        def _(q=q, lo=lo):
            t = inv_ref[s_ref[0] + q]
            s = jnp.concatenate([stored(2 * t), stored(2 * t + 1)], 0)
            sym = jnp.where(k <= j, s, 0.0) + jnp.where(k < j, s, 0.0).T
            for h in range(2):
                i = lo + h - side * per

                @pl.when((i >= 0) & (i < per))
                def _():
                    mine = pl.ds(pl.multiple_of(i * half, half), half)
                    o_ref[mine, q * block : (q + 1) * block] = sym[h * half : (h + 1) * half]
                    other = i + 1 - 2 * h
                    inside = (other >= 0) & (other < per)
                    safe = jnp.minimum(jnp.maximum(other, 0), per - 1)
                    pair = d_ref[pl.ds(pl.multiple_of(safe * half, half), half), :]
                    pair = jnp.where(inside, pair, edge)
                    this = d_ref[mine, :]
                    near = jnp.concatenate([pair, this] if h else [this, pair], 0)
                    rows = sym[h * half : (h + 1) * half].astype(jnp.bfloat16)
                    p_ref[mine, :] += fold3(
                        jnp.dot(rows, wide3(near), preferred_element_type=jnp.float32)
                    )


def products_job(order, spots, scalars, terr_stored, terr_all, whitened, directions, edge, v):
    own = whitened.shape[0]
    cols = directions.shape[1]
    vmem = pl.BlockSpec(memory_space=pltpu.VMEM)
    smem = pl.BlockSpec(memory_space=pltpu.SMEM)
    return pl.pallas_call(
        products_kernel,
        in_specs=[smem] * 3 + [vmem] * (5 + len(v)),
        out_specs=[vmem] * 2,
        out_shape=[
            jax.ShapeDtypeStruct((own, cols), jnp.float32),
            jax.ShapeDtypeStruct((own, 2 * own), jnp.float32),
        ],
        scratch_shapes=[pltpu.SMEM((order.shape[0],), jnp.int32)],
        name="products",
        compiler_params=pltpu.CompilerParams(vmem_limit_bytes=40 * 1024 * 1024),
        cost_estimate=pl.CostEstimate(
            flops=6 * own * whitened.shape[1] * cols, bytes_accessed=10000000, transcendentals=0
        ),
    )(order, spots, scalars, terr_stored, terr_all, whitened, directions, edge, *v)


def tile_kernel(wants, sources, width, first, carry, terr, s_ref, *refs):
    n = 1 + max(at for pair in sources.values() for at, _ in pair)
    bufs = refs[:n]
    a_ref = refs[n]
    rest = refs[n + 1 :]
    if terr:
        t_ref, rest = rest[0], rest[1:]
    if carry:
        pre_ref, rest = rest[0], rest[1:]
    if not first:
        rest = rest[1:]
    o_hbm, b_ref, o_ref, sem, o_sem = rest[:5]
    i = pl.program_id(0)
    steps = pl.num_programs(0)
    own = a_ref.shape[1]
    half = own // 2
    span = b_ref.shape[0]
    lo = s_ref[4]

    def copy(k, y, h):
        at, row = sources[k][h]
        return pltpu.make_async_copy(
            bufs[at].at[pl.ds(row, half)],
            b_ref.at[pl.ds((2 * y + h) * half, half)],
            sem.at[2 * y + h],
        )

    @pl.when(i == 0)
    def _():
        for y in range(2):
            for h in range(2):
                needed = wants(s_ref, y, h)
                for k in sources:

                    @pl.when((s_ref[1 + y] == k) & needed)
                    def _():
                        copy(k, y, h).start()

        for y in range(2):
            for h in range(2):

                @pl.when(wants(s_ref, y, h))
                def _():
                    copy(next(iter(sources)), y, h).wait()

    slot = i % 2

    def out(i, slot):
        return pltpu.make_async_copy(
            o_ref.at[slot],
            o_hbm.at[
                pl.ds(pl.multiple_of(s_ref[6 + i] * own, own), own),
                pl.ds(pl.multiple_of(s_ref[0] * span + lo, 128), width),
            ],
            o_sem.at[slot],
        )

    @pl.when(i >= 2)
    def _():
        out(i - 2, slot).wait()

    if carry:
        q_ref, q_in, q_out = rest[5:]

        def pull(n):
            return pltpu.make_async_copy(pre_ref.at[carry[n]], q_ref.at[n], q_in.at[n])

        def push(n):
            return pltpu.make_async_copy(
                q_ref.at[n],
                o_hbm.at[
                    pl.ds(pl.multiple_of(s_ref[6 + carry[n]] * own, own), own),
                    pl.ds(pl.multiple_of(s_ref[3] * span, span), span),
                ],
                q_out.at[n],
            )

        @pl.when(i == 0)
        def _():
            for n in range(len(carry)):
                pull(n).start()

        for n in range(len(carry)):

            @pl.when(i == 1 + n)
            def _():
                pull(n).wait()
                if terr and carry[n] == 0:
                    q_ref[n] += t_ref[...]
                push(n).start()

    o_ref[slot] = lax.dot_general(
        a_ref[0],
        b_ref[pl.ds(pl.multiple_of(lo, 128), width), :],
        NT,
        preferred_element_type=jnp.float32,
    )
    out(i, slot).start()

    @pl.when(i == steps - 1)
    def _():
        for n in range(len(carry)):
            push(n).wait()
        out(i - 1, 1 - slot).wait()
        out(i, slot).wait()


def tile_job(scalars, wants, cands, bufs, rows, width, carry, pre, terr, out):
    count, own, total = rows.shape
    span = 2 * own
    first = not isinstance(out, jax.Array)
    any_spec = pl.BlockSpec(memory_space=pl.ANY)
    arrays, sources = [], {}
    for k in cands:
        pair = []
        for array, row in bufs[k]:
            at = [i for i, a in enumerate(arrays) if a is array]
            if not at:
                arrays.append(array)
                at = [len(arrays) - 1]
            pair.append((at[0], row))
        sources[k] = pair
    operands = arrays + [rows]
    in_specs = [any_spec] * len(arrays) + [
        pl.BlockSpec((1, own, total), lambda i, s: (i, 0, 0)),
    ]
    scratch = [
        pltpu.VMEM((span, total), jnp.bfloat16),
        pltpu.VMEM((2, own, width), jnp.float32),
        pltpu.SemaphoreType.DMA((4,)),
        pltpu.SemaphoreType.DMA((2,)),
    ]
    if terr is not None:
        operands.append(terr)
        in_specs.append(pl.BlockSpec((own, span), lambda i, s: (0, 0)))
    if carry:
        operands.append(pre)
        in_specs.append(any_spec)
        scratch += [
            pltpu.VMEM((len(carry), own, span), jnp.float32),
            pltpu.SemaphoreType.DMA((len(carry),)),
            pltpu.SemaphoreType.DMA((len(carry),)),
        ]
    shape = out
    alias = {}
    if not first:
        alias = {1 + len(operands): 0}
        operands.append(out)
        in_specs.append(any_spec)
        shape = jax.ShapeDtypeStruct(out.shape, out.dtype)
    return pl.pallas_call(
        functools.partial(tile_kernel, wants, sources, width, first, carry, terr is not None),
        grid_spec=pltpu.PrefetchScalarGridSpec(
            num_scalar_prefetch=1,
            grid=(count,),
            in_specs=in_specs,
            out_specs=any_spec,
            scratch_shapes=scratch,
        ),
        out_shape=shape,
        input_output_aliases=alias,
        compiler_params=pltpu.CompilerParams(vmem_limit_bytes=48 * 1024 * 1024),
        cost_estimate=pl.CostEstimate(
            flops=2 * count * own * width * total,
            bytes_accessed=2 * count * own * total + 4 * count * own * width,
            transcendentals=0,
        ),
    )(scalars, *operands)


def ring_body(n_row, n_col, design, arc_filter, arc_of_row, terr_stored, block_order, directions):
    own, total = design.shape
    block = terr_stored.shape[1]
    r = lax.axis_index("row")
    c = lax.axis_index("col")
    zs = n_col // 2
    half = own // 2
    far = n_col // 2

    def hop(a, perm):
        return lax.ppermute(a, "col", perm)

    col_of = [2 * p if p < zs else 2 * (n_col - 1 - p) + 1 for p in range(n_col)]
    pos_of = [0] * n_col
    for p, col in enumerate(col_of):
        pos_of[col] = p
    forward = [(col_of[p], col_of[(p + 1) % n_col]) for p in range(n_col)]
    backward = [(d, s) for s, d in forward]

    whitened = whiten_rows(design, arc_filter, arc_of_row)
    rows, up1, up2a, up2b, dn1, dn2a, dn2b, terr_all, edge, _, pre, v = exchange(
        n_row, n_col, whitened, terr_stored, directions
    )
    bufs = {
        0: [(whitened, 0), (whitened, half)],
        1: [(dn1, 0), (dn1, half)],
        2: [(dn2a, 0), (dn2b, 0)],
        n_col - 1: [(up1, 0), (up1, half)],
        n_col - 2: [(up2a, 0), (up2b, 0)],
    }
    for k in range(3, far + 1):
        before_up, before_dn = bufs[n_col - k + 1], bufs[k - 1]
        if k < far:
            ua = hop(before_up[0][0], forward)
            db = hop(before_dn[1][0], backward)
            ub = hop(before_up[1][0], forward)
            da = hop(before_dn[0][0], backward)
            bufs[n_col - k] = [(ua, 0), (ub, 0)]
            bufs[k] = [(da, 0), (db, 0)]
        else:
            ua = hop(before_up[0][0], forward)
            db = hop(before_dn[1][0], backward)
            bufs[k] = [(ua, 0), (db, 0)]

    per_pair = 2 * own // block
    count = per_pair * zs
    spots = np.array([[(pos_of[d] - pos_of[s]) % n_col for d in range(n_col)] for s in range(n_col)])
    local_order = block_order - r * count
    pieces = {0: v}
    for mask in reversed(masks_of(n_row)):
        for m in list(pieces):
            pieces[m + mask] = lax.ppermute(pieces[m], "row", [(i, i ^ mask) for i in range(n_row)])
    firsts = np.zeros((n_row, n_row), np.int32)
    for i in range(n_row):
        for m in range(n_row):
            size = total
            for mask in masks_of(n_row):
                size //= 2
                firsts[i, m] += size * (((i ^ m) // mask) % 2)
    products, terr = products_job(
        local_order,
        jnp.asarray(spots, jnp.int32)[c],
        jnp.concatenate([jnp.stack([(c // 2) * per_pair, c % 2]), jnp.asarray(firsts)[r]]),
        terr_stored, terr_all, whitened, directions, edge,
        [pieces[m] for m in range(n_row)],
    )

    wide = own // 128 * 128
    jobs = zs - 1
    table = np.zeros((jobs, n_col, 6), np.int32)
    for col in range(n_col):
        todo = []
        for zz in range(zs):
            ks = [(pos_of[2 * zz + yy] - pos_of[col]) % n_col for yy in range(2)]
            if zz != col // 2:
                todo.append((max(min(k, n_col - k) for k in ks), zz, ks))
        for j, (_, zz, ks) in enumerate(sorted(todo)):
            late = ks.index(far) if far in ks else 0
            table[j, col] = [zz, ks[0], ks[1], col // 2, 0, late]
    row_spots = jnp.bitwise_xor(r, jnp.arange(n_row, dtype=jnp.int32))
    out = jax.ShapeDtypeStruct((n_row * own, n_col * own), jnp.float32)

    def job(j, wants, cands, width, out, spot=None, carry=(), terr=None):
        use = table[j].copy()
        if spot is not None:
            use[:, 4] = [spot(late) for late in use[:, 5]]
        scalars = jnp.concatenate([jnp.asarray(use)[c], row_spots])
        return tile_job(scalars, wants, cands, bufs, rows, width, carry, pre, terr, out)

    every = lambda s, y, h: s[5] >= 0
    early = lambda s, y, h: s[5] == 1 - y
    tail = lambda s, y, h: (s[5] == y) | (h == 1 - y)
    for j in range(jobs - 1):
        cands = tuple(sorted(set(table[j, :, 1:3].ravel().tolist())))
        carry = {0: tuple(range(1, n_row)), 1: (0,)}.get(j, ())
        out = job(j, every, cands, 2 * own, out, None, carry, terr if j == 1 else None)
    cands = set(table[jobs - 1, :, 1:3].ravel().tolist())
    out = job(jobs - 1, early, tuple(sorted(cands - {far})), wide, out,
              lambda late: 0 if late == 1 else 2 * own - wide)
    out = job(jobs - 1, tail, tuple(sorted(cands)), 2 * own - wide, out,
              lambda late: wide if late == 1 else 0)
    return out.reshape(n_row, 1, own, n_col * own), products


def power_of_two(n):
    return n > 1 and n & (n - 1) == 0


def solution(mesh):
    n_row, n_col = mesh.shape["row"], mesh.shape["col"]

    def body(design, arc_filter, arc_of_row, terr_stored, block_order, directions):
        args = (design, arc_filter, arc_of_row, terr_stored, block_order, directions)
        own, block = design.shape[0], terr_stored.shape[1]
        aligned = n_row > 2 and own % 192 == 0 and own % block == block // 2 and (2 * own) % 128 == 0
        if power_of_two(n_row) and power_of_two(n_col) and n_col > 6 and aligned:
            return ring_body(n_row, n_col, *args)
        return general_body(*args)

    return jax.shard_map(
        body,
        mesh=mesh,
        in_specs=(
            P(("row", "col"), None),
            P(),
            P(),
            P(("row", "col"), None),
            P("row"),
            P(("row", "col"), None),
        ),
        out_specs=(P(None, "col", None, "row"), P(("row", "col"), None)),
        check_vma=False,
    )
```

```python
import functools

import jax
import jax.numpy as jnp
from jax import lax
from jax.experimental import pallas as pl
from jax.experimental.pallas import tpu as pltpu
from jax.sharding import PartitionSpec as P


HIGH = lax.Precision.HIGHEST
NT = (((1,), (1,)), ((), ()))
MESH = pl.DeviceIdType.MESH


def dot_high(a, b):
    return jnp.dot(a, b, precision=HIGH, preferred_element_type=jnp.float32)


def whiten(design, arc_filter, arc_of_row):
    positions = jnp.arange(arc_filter.shape[0], dtype=jnp.int32)
    keep_mask = (positions[:, None] > positions[None, :]) & (
        arc_of_row[:, None] == arc_of_row[None, :]
    )
    lower_part = jnp.where(keep_mask, arc_filter, jnp.zeros_like(arc_filter))
    mixed_part = lax.dot_general(design, lower_part, NT, preferred_element_type=jnp.float32)
    return (design.astype(jnp.float32) + mixed_part).astype(jnp.bfloat16)


def general_body(design, arc_filter, arc_of_row, terr_stored, block_order, directions):
    whitened = whiten(design, arc_filter, arc_of_row)
    own_width = whitened.shape[0]
    rows_block, terr_rows = (
        lax.all_gather(whitened, "col", axis=0, tiled=True),
        lax.all_gather(terr_stored, "col", axis=0, tiled=True),
    )
    cols_block = lax.all_gather(whitened, "row", axis=0, tiled=True)
    normal_tile = lax.dot_general(cols_block, rows_block, NT, preferred_element_type=jnp.float32)
    block_size = terr_rows.shape[1]
    span_rows = terr_rows.shape[0]
    group_count = span_rows // block_size
    row_index = lax.axis_index("row")
    col_index = lax.axis_index("col")
    local_order = block_order - row_index * group_count
    selector = (local_order[None, :] == jnp.arange(group_count, dtype=jnp.int32)[:, None]).astype(
        jnp.float32
    )
    stored = terr_rows.astype(jnp.float32).reshape(group_count, block_size, block_size)
    symmetric = jnp.triu(stored) + jnp.swapaxes(jnp.triu(stored, 1), 1, 2)
    ordered = jnp.einsum("qt,tab->qab", selector, symmetric, precision=HIGH).reshape(
        span_rows, block_size
    )
    own_rows = lax.dynamic_slice_in_dim(ordered, col_index * own_width, own_width, 0)
    positions = col_index * own_width + jnp.arange(own_width, dtype=jnp.int32)
    onehot = (
        (positions // block_size)[:, None] == jnp.arange(group_count, dtype=jnp.int32)[None, :]
    ).astype(jnp.float32)
    terr_added = (onehot[:, :, None] * own_rows[:, None, :]).reshape(own_width, span_rows)
    current = lax.dynamic_slice_in_dim(normal_tile, row_index * own_width, own_width, 0)
    normal_tile = lax.dynamic_update_slice_in_dim(
        normal_tile, current + terr_added, row_index * own_width, 0
    )
    tile_rows = normal_tile.shape[0]
    partial_sum = dot_high(normal_tile, lax.all_gather(directions, "col", axis=0, tiled=True))
    products = lax.psum_scatter(partial_sum, "row", scatter_dimension=0, tiled=True)
    normals = normal_tile.reshape(tile_rows // own_width, 1, own_width, span_rows)
    return (normals, products)


def xor(i, mask):
    return i + mask * (1 - 2 * ((i // mask) % 2))


def xor_all(i, mask, n):
    for m in masks_of(n):
        if mask & m:
            i = xor(i, m)
    return i


def split3(x):
    a = x.astype(jnp.bfloat16)
    rest = x - a.astype(jnp.float32)
    b = rest.astype(jnp.bfloat16)
    return a, b, (rest - b.astype(jnp.float32)).astype(jnp.bfloat16)


def wide3(x):
    return jnp.concatenate(split3(x), 1)


def fold3(x):
    n = x.shape[1] // 3
    return x[:, 2 * n :] + x[:, n : 2 * n] + x[:, :n]


def whiten_kernel(d_ref, dp_ref, f_ref, fp_ref, ar_ref, arp_ref, w_ref):
    b = pl.program_id(0)
    width = f_ref.shape[0]
    zero = jnp.zeros((width, width), jnp.float32)
    k = lax.broadcasted_iota(jnp.int32, (width, width), 0)
    j = lax.broadcasted_iota(jnp.int32, (width, width), 1)
    column = jnp.broadcast_to(ar_ref[...], (128, width)).T[:, :1]
    keep = (k > j) & (column == ar_ref[...])
    keep_prev = (column == arp_ref[...]) & (b > 0)
    here = jnp.where(keep, f_ref[...].astype(jnp.float32), zero).astype(jnp.bfloat16)
    prev = jnp.where(keep_prev, fp_ref[...].astype(jnp.float32), zero).astype(jnp.bfloat16)
    mixed = lax.dot_general(d_ref[...], here, NT, preferred_element_type=jnp.float32)
    mixed += lax.dot_general(dp_ref[...], prev, NT, preferred_element_type=jnp.float32)
    w_ref[...] = (d_ref[...].astype(jnp.float32) + mixed).astype(jnp.bfloat16)


def whiten_rows(design, arc_filter, arc_of_row):
    own, total = design.shape
    width = total // 4
    here = lambda b: (0, b)
    prev = lambda b: (0, jnp.maximum(b - 1, 0))
    row = arc_of_row.reshape(1, total)
    return pl.pallas_call(
        whiten_kernel,
        grid=(total // width,),
        in_specs=[
            pl.BlockSpec((own, width), here),
            pl.BlockSpec((own, width), prev),
            pl.BlockSpec((width, width), lambda b: (b, b)),
            pl.BlockSpec((width, width), lambda b: (b, jnp.maximum(b - 1, 0))),
            pl.BlockSpec((1, width), here),
            pl.BlockSpec((1, width), prev),
        ],
        out_specs=pl.BlockSpec((own, width), here),
        out_shape=jax.ShapeDtypeStruct((own, total), jnp.bfloat16),
        name="whiten",
        cost_estimate=pl.CostEstimate(
            flops=4 * own * total * width, bytes_accessed=8 * own * total, transcendentals=0
        ),
    )(design, design, arc_filter, arc_filter, row, row)


def masks_of(n):
    return [1 << i for i in range(n.bit_length() - 1)]


def exchange_kernel(n_row, n_col, parts, w_ref, t_ref, d_ref, *refs):
    rows_ref, up1, up2a, up2b, up3a, dn1, dn2a, dn2b, dn3b = refs[:9]
    terr_ref, edge_ref, side_ref, pre_ref, pre0_ref, pre1_ref, vout = refs[9:16]
    b_ref, b0_ref, b1_ref, a_ref, o_ref, got, acc = refs[16:23]
    s_loc, s_a, s_o, s_ring, r_ring, s_row, r_row, s_terr, r_terr, s_v, r_v, s_e, r_e = refs[23:]
    r = lax.axis_index("row")
    c = lax.axis_index("col")
    own, width = w_ref.shape
    sub = own // parts
    zs = n_col // 2
    z, y = c // 2, c % 2
    place = z + y * (n_col - 1 - 2 * z)
    by_up = place % zs == 0
    by_down = place % zs == zs - 1
    inner = (place % zs > 0) & (place % zs < zs - 1)

    def col_at(p):
        side = p // zs
        return 2 * (p + side * (n_col - 1 - 2 * p)) + side

    nxt = col_at((place + 1) % n_col)
    prv = col_at((place + n_col - 1) % n_col)
    row_masks = masks_of(n_row)
    peers = [(r, nxt), (r, prv)]
    peers += [(xor(r, m), c) for m in row_masks] + [(r, xor(c, 1))]
    peers += [(r, 2 * xor_all(z, m, zs) + y) for m in range(1, zs)]
    barrier = pltpu.get_barrier_semaphore()
    for peer in peers:
        pl.semaphore_signal(barrier, inc=1, device_id=peer, device_id_type=MESH)
    pl.semaphore_wait(barrier, len(peers))

    def remote(src, dst, ssem, rsem, peer):
        return pltpu.make_async_remote_copy(
            src_ref=src, dst_ref=dst, send_sem=ssem, recv_sem=rsem, device_id=peer,
            device_id_type=MESH,
        )

    def piece(ref, j):
        return ref.at[pl.ds(j * sub, sub)]

    sends = []

    def start(copy):
        copy.start()
        sends.append(copy)

    half = parts // 2
    steps = 2 * parts + half
    ahead = 4

    def ring(s, way):
        one, two, three = ((up1, (up2a, up2b), up3a), (dn1, (dn2a, dn2b), dn3b))[way]
        j = s % parts
        if s < parts:
            src, dst = piece(w_ref, j), piece(one, j)
        elif s < 2 * parts:
            src, dst = piece(one, j), piece(two[j // half], j % half)
        else:
            src, dst = piece(two[way], j), piece(three, j)
        return remote(src, dst, s_ring.at[way, s], r_ring.at[way, s], (r, (nxt, prv)[way]))

    rings = [[ring(s, way) for way in range(2)] for s in range(steps)]
    for s in range(ahead):
        for way in range(2):
            start(rings[s][way])

    mine = pl.ds(pl.multiple_of(y * own, own), own)
    other = pl.ds(pl.multiple_of((1 - y) * own, own), own)
    load = pltpu.make_async_copy(w_ref, b_ref.at[mine], s_loc.at[0])
    load.start()

    far = n_col // 2

    def terr(k, way):
        src = t_ref if k == 1 else terr_ref.at[(n_col - k + 1) if way == 0 else k - 1]
        at = (n_col - k) if way == 0 else k
        return remote(src, terr_ref.at[at], s_terr.at[way, k - 1], r_terr.at[way, k - 1],
                      (r, (nxt, prv)[way]))

    terrs = {}
    for k in range(1, far + 1):
        terrs[k] = [terr(k, 0)] + ([terr(k, 1)] if k < far else [])
    for copy in terrs[1]:
        start(copy)
    edge = edge_ref.shape[0]
    edge_at = pl.ds(pl.multiple_of((1 - y) * (own - edge), edge), edge)
    edges = remote(d_ref.at[edge_at], edge_ref, s_e.at[0], r_e.at[0], (r, xor(c, 1)))
    start(edges)
    across = remote(w_ref, side_ref, s_e.at[1], r_e.at[1], (r, xor(c, 1)))

    @pl.when(inner)
    def _():
        across.start()

    order = []
    for mask in reversed(row_masks):
        for m in range(0, n_row, 2 * mask):
            order.append((m + mask, mask))

    def row_copy(key, j):
        m, mask = key
        n = order.index(key)
        src = w_ref if m == mask else rows_ref.at[m - mask]
        return remote(piece(src, j), piece(rows_ref.at[m], j), s_row.at[n, j], r_row.at[n, j],
                      (xor(r, mask), c))

    copies = {key: [row_copy(key, j) for j in range(parts)] for key in order}
    filled = {m: (m, mask) for m, mask in order}
    later = [key for key in order if key[0] != key[1]]
    waited = set()

    def row_wait(key, j):
        if (key, j) not in waited:
            copies[key][j].wait_recv()
            waited.add((key, j))

    load.wait()
    put = pltpu.make_async_copy(b_ref.at[mine], rows_ref.at[0], s_loc.at[1])
    put.start()
    dirs = wide3(d_ref[...])
    chunk = width // 8

    @pl.loop(0, 8)
    def _(t):
        span = pl.ds(pl.multiple_of(t * chunk, chunk), chunk)
        acc[span, :] = fold3(
            lax.dot_general(
                b_ref[mine, span], dirs, (((0,), (0,)), ((), ())),
                preferred_element_type=jnp.float32,
            )
        )

    levels = [((xor(r, m), c), (r // m) % 2) for m in row_masks] + [((r, xor(c, 1)), y)]
    n = len(levels)
    span = width
    offset = base = 0
    gives, keeps, spots = [], [], []
    for i, (peer, bit) in enumerate(levels):
        span //= 2
        give = pl.ds(pl.multiple_of(offset + (1 - bit) * span, span), span)
        offset = offset + bit * span
        keep = pl.ds(pl.multiple_of(offset, span), span)
        spot = pl.ds(base, span)
        base += span
        gives.append(remote(acc.at[give], got.at[spot], s_v.at[i], r_v.at[i], peer))
        keeps.append(keep)
        spots.append(spot)
    bit = span // zs
    at_out = pl.ds(pl.multiple_of(offset + z * bit, bit), bit)
    fans, backs = [], []
    for m in range(1, zs):
        zz = xor_all(z, m, zs)
        peer = (r, 2 * zz + y)
        give = pl.ds(pl.multiple_of(offset + zz * bit, bit), bit)
        spot = pl.ds(base + (m - 1) * bit, bit)
        at = n + 2 * m - 2
        fans.append(remote(acc.at[give], got.at[spot], s_v.at[at], r_v.at[at], peer))
        backs.append(
            remote(vout.at[at_out], vout.at[at_out], s_v.at[at + 1], r_v.at[at + 1], peer)
        )
    at = n + 2 * zs - 2
    wider = [
        remote(vout.at[keeps[i]], vout.at[keeps[i]], s_v.at[at + i], r_v.at[at + i], levels[i][0])
        for i in range(n)
    ]

    def finish(i):
        gives[i].wait()
        acc[keeps[i]] = acc[keeps[i]] + got[spots[i]]

    def fan_in():
        for copy in fans:
            copy.wait()
        mid = acc[pl.ds(pl.multiple_of(offset + z * bit, bit), bit)]
        for m in range(1, zs):
            mid = mid + got[base + (m - 1) * bit : base + m * bit]
        vout[at_out] = mid

    def each(copies, method):
        for copy in copies:
            getattr(copy, method)()

    todo = [lambda: gives[0].start()]
    for i in range(1, n):
        todo.append(lambda i=i: (finish(i - 1), gives[i].start()))
    todo.append(lambda: (finish(n - 1), each(fans, "start")))
    todo.append(lambda: (fan_in(), each(backs, "start")))
    todo.append(lambda: (each(backs, "wait"), wider[n - 1].start()))
    for i in range(n - 1, 0, -1):
        todo.append(lambda i=i: (wider[i].wait(), wider[i - 1].start()))
    todo.append(lambda: wider[0].wait())

    def v_next():
        if todo:
            todo.pop(0)()

    v_next()
    v_next()
    for key in order:
        if key[0] == key[1]:
            for copy in copies[key]:
                start(copy)

    wide = own // 128 * 128
    rest = 2 * own - wide
    near_at = pl.multiple_of(y * (2 * own - wide), 128)
    rest_at = pl.multiple_of((1 - y) * wide, 128)
    up_first = place % zs < zs // 2

    def fill(refs, b, at, n):
        size = own // len(refs)
        return [
            pltpu.make_async_copy(ref, b.at[pl.ds(at + i * size, size)], s_loc.at[n + i])
            for i, ref in enumerate(refs)
        ]

    def other_start():
        start_at = (1 - y) * own

        @pl.when(inner)
        def _():
            across.wait()
            each(fill([side_ref], b_ref, start_at, 2), "start")

        @pl.when(by_up)
        def _():
            each(fill([up1], b_ref, start_at, 2), "start")

        @pl.when(by_down)
        def _():
            each(fill([dn1], b_ref, start_at, 2), "start")

        @pl.when(place % 2 == 0)
        def _():
            each(fill([dn1], b0_ref, y * own, 3), "start")

        @pl.when(place % 2 == 1)
        def _():
            each(fill([up1], b0_ref, y * own, 3), "start")

    def second_start():
        @pl.when(up_first)
        def _():
            each(fill([up2a, up2b], b0_ref, (1 - y) * own, 4), "start")
            each(fill([dn2a, dn2b], b1_ref, 0, 6), "start")

        @pl.when(place % zs >= zs // 2)
        def _():
            each(fill([dn2a, dn2b], b0_ref, (1 - y) * own, 4), "start")
            each(fill([up2a, up2b], b1_ref, 0, 6), "start")

    def a_load(m):
        return pltpu.make_async_copy(rows_ref.at[m], a_ref.at[m], s_a.at[m])

    stores = []

    def dots(m, rows, width, into):
        n = len(stores)
        for store in stores[-2:]:
            store.wait()

        def store(t):
            return pltpu.make_async_copy(
                o_ref.at[t, :, pl.ds(0, width)], into(m + t), s_o.at[n + t]
            )

        @pl.loop(0, 2)
        def _(t):
            o_ref[t, :, :width] = lax.dot_general(
                a_ref[m + t], rows(), NT, preferred_element_type=jnp.float32
            )
            store(t).start()

        stores.extend([store(0), store(1)])

    def own_tile(m):
        for i in range(2):
            a_load(m + i).wait()
        if m == 0:
            each(fill([side_ref], b_ref, 0, 2), "wait")
        dots(m, lambda: b_ref[...], 2 * own, lambda m: pre_ref.at[m])

    def near_tile(m):
        if m == 0:
            each(fill([up1], b0_ref, 0, 3), "wait")
        span = pl.ds(near_at, wide)
        dots(m, lambda: b0_ref[span, :], wide, lambda m: pre0_ref.at[m, :, span])

    def rest_tile(m):
        if m == 0:
            each(fill([up2a, up2b], b0_ref, 0, 4), "wait")
        span = pl.ds(rest_at, rest)
        dots(m, lambda: b0_ref[span, :], rest, lambda m: pre0_ref.at[m, :, span])

    def side_tile(m):
        if m == 0:
            each(fill([up2a, up2b], b1_ref, 0, 6), "wait")
        at = pl.multiple_of(y * (own - wide), own - wide)
        dots(m, lambda: b1_ref[pl.ds(at, wide), :], wide, lambda m: pre1_ref.at[m])

    hop = 1
    lag = parts // 2
    v_at = [ahead + i * (ahead + 1) for i in range(5)] + [steps - 3, steps - 1]
    work = {}
    for m in range(0, n_row, 2):
        work.setdefault(parts + 1 + (lag + 1) * (m // 2), []).append((own_tile, m))
        work.setdefault(2 * parts - 3 + m // 2, []).append((near_tile, m))
        work.setdefault(2 * parts + m // 2, []).append((rest_tile, m))
        work.setdefault(2 * parts + 3 + m // 2, []).append((side_tile, m))
    for s in range(steps):
        for way in range(2):
            rings[s][way].wait_recv()
        if s in v_at:
            v_next()
        if s % 3 == 2 and hop <= far:
            for copy in terrs[hop]:
                copy.wait_recv()
            hop += 1
            if hop <= far:
                for copy in terrs[hop]:
                    start(copy)
        if s + ahead < steps:
            for way in range(2):
                start(rings[s + ahead][way])
        j = s - lag
        if 0 <= j < parts:
            for key in later:
                row_wait(filled[key[0] - key[1]], j)
                start(copies[key][j])
        if s == parts - 1:
            other_start()
            put.wait()
            a_load(0).start()
            for j in range(parts):
                row_wait(filled[1], j)
            a_load(1).start()
        if s == parts + lag - 1:
            for m in range(2, n_row):
                for j in range(parts):
                    row_wait(filled[m], j)
                a_load(m).start()
        if s == 2 * parts - 1:
            second_start()
        for do, m in work.get(s, []):
            do(m)
    while hop <= far:
        for copy in terrs[hop]:
            copy.wait_recv()
        hop += 1
        if hop <= far:
            for copy in terrs[hop]:
                start(copy)
    while todo:
        v_next()
    edges.wait_recv()
    for store in stores[-2:]:
        store.wait()
    for copy in sends:
        copy.wait_send()


def exchange(n_row, n_col, whitened, terr_stored, directions):
    own, total = whitened.shape
    cols = directions.shape[1]
    block = terr_stored.shape[1]
    parts = 12
    far = n_col // 2
    any_spec = pl.BlockSpec(memory_space=pl.ANY)
    vmem = pl.BlockSpec(memory_space=pltpu.VMEM)
    whole = jax.ShapeDtypeStruct((own, total), jnp.bfloat16)
    part = jax.ShapeDtypeStruct((own // 2, total), jnp.bfloat16)
    levels = 2 * n_row.bit_length() + n_col
    moves = n_row - 1
    dma = pltpu.SemaphoreType.DMA
    return pl.pallas_call(
        functools.partial(exchange_kernel, n_row, n_col, parts),
        in_specs=[any_spec, any_spec, vmem],
        out_specs=[any_spec] * 15 + [vmem],
        out_shape=[
            jax.ShapeDtypeStruct((n_row, own, total), jnp.bfloat16),
            whole, part, part, part, whole, part, part, part,
            jax.ShapeDtypeStruct((n_col, own, block), jnp.bfloat16),
            jax.ShapeDtypeStruct((block // 2, cols), jnp.float32),
            whole,
            jax.ShapeDtypeStruct((n_row, own, 2 * own), jnp.float32),
            jax.ShapeDtypeStruct((n_row, own, 2 * own), jnp.float32),
            jax.ShapeDtypeStruct((n_row, own, own // 128 * 128), jnp.float32),
            jax.ShapeDtypeStruct((total, cols), jnp.float32),
        ],
        scratch_shapes=[
            pltpu.VMEM((2 * own, total), jnp.bfloat16),
            pltpu.VMEM((2 * own, total), jnp.bfloat16),
            pltpu.VMEM((own, total), jnp.bfloat16),
            pltpu.VMEM((n_row, own, total), jnp.bfloat16),
            pltpu.VMEM((2, own, 2 * own), jnp.float32),
            pltpu.VMEM((total, cols), jnp.float32),
            pltpu.VMEM((total, cols), jnp.float32),
            dma((8,)),
            dma((n_row,)),
            dma((4 * n_row,)),
            dma((2, 3 * parts)), dma((2, 3 * parts)),
            dma((moves, parts)), dma((moves, parts)),
            dma((2, far)), dma((2, far)),
            dma((levels,)), dma((levels,)),
            dma((2,)), dma((2,)),
        ],
        name="exchange",
        compiler_params=pltpu.CompilerParams(
            collective_id=0, has_side_effects=True, vmem_limit_bytes=60 * 1024 * 1024
        ),
        cost_estimate=pl.CostEstimate(
            flops=1000000, bytes_accessed=40 * own * total, transcendentals=0
        ),
    )(whitened, terr_stored, directions)


def carry_kernel(at, n_row, s_ref, order_ref, t0_ref, t_ref, w_ref, d_ref, e_ref, v_ref, *refs):
    pre_ref, pre0_ref, pre1_ref, p_ref, out_ref, inv_ref, q_ref, q1_ref, pull_sem, push_sem = refs
    own, span = q_ref.shape[1:]
    wide = q1_ref.shape[2]
    half = e_ref.shape[0]
    block = 2 * half
    per = own // half
    count = order_ref.shape[0]
    side = s_ref[at["side"]]
    pair = s_ref[at["pair"]]

    def pull(n):
        src = (pre_ref, pre0_ref, pre1_ref)[n // n_row].at[n % n_row]
        dst = q_ref.at[n] if n < 2 * n_row else q1_ref.at[n - 2 * n_row]
        return pltpu.make_async_copy(src, dst, pull_sem.at[n])

    def push(n):
        kind, m = n // n_row, n % n_row
        zz = s_ref[at["own"] + kind]
        column = zz * span if kind < 2 else zz * span + side * (span - wide)
        src = q_ref.at[n] if kind < 2 else q1_ref.at[m]
        return pltpu.make_async_copy(
            src,
            out_ref.at[
                pl.ds(pl.multiple_of(s_ref[at["rows"] + m] * own, own), own),
                pl.ds(pl.multiple_of(column, 128), span if kind < 2 else wide),
            ],
            push_sem.at[n],
        )

    total = 3 * n_row
    for n in range(total):
        pull(n).start()

    @pl.loop(0, count)
    def _(t):
        inv_ref[order_ref[t] - s_ref[at["first"]]] = t

    def pass_on(lo, hi):
        for n in range(lo, hi):
            pull(n).wait()
            push(n).start()

    size = v_ref.shape[0] // n_row
    for m in range(n_row):
        part = slice(m * size, (m + 1) * size)
        term = fold3(
            jnp.dot(w_ref[:, part], wide3(v_ref[part, :]), preferred_element_type=jnp.float32)
        )
        p_ref[...] = p_ref[...] + term if m else term
        pass_on(1 + 2 * m, 3 + 2 * m)
    pull(0).wait()
    k = lax.broadcasted_iota(jnp.int32, (block, block), 0)
    j = lax.broadcasted_iota(jnp.int32, (block, block), 1)

    def stored(g):
        slot, spot = s_ref[at["spots"] + g // per], g % per
        there = pl.ds(pl.multiple_of(spot * half, half), half)
        return jnp.where(
            slot == 0,
            t0_ref[there, :].astype(jnp.float32),
            t_ref[slot, there, :].astype(jnp.float32),
        )

    edge = e_ref[...]
    for q in range(span // block):
        lo = 2 * q

        @pl.when((lo + 1 >= side * per) & (lo < side * per + per))
        def _(q=q, lo=lo):
            t = inv_ref[pair + q]
            s = jnp.concatenate([stored(2 * t), stored(2 * t + 1)], 0)
            sym = jnp.where(k <= j, s, 0.0) + jnp.where(k < j, s, 0.0).T
            for h in range(2):
                i = lo + h - side * per

                @pl.when((i >= 0) & (i < per))
                def _():
                    mine = pl.ds(pl.multiple_of(i * half, half), half)
                    rows = sym[h * half : (h + 1) * half]
                    q_ref[0, mine, q * block : (q + 1) * block] += rows
                    other = i + 1 - 2 * h
                    inside = (other >= 0) & (other < per)
                    safe = jnp.minimum(jnp.maximum(other, 0), per - 1)
                    beside = d_ref[pl.ds(pl.multiple_of(safe * half, half), half), :]
                    beside = jnp.where(inside, beside, edge)
                    this = d_ref[mine, :]
                    near = jnp.concatenate([beside, this] if h else [this, beside], 0)
                    p_ref[mine, :] += fold3(
                        jnp.dot(
                            rows.astype(jnp.bfloat16), wide3(near),
                            preferred_element_type=jnp.float32,
                        )
                    )

    push(0).start()
    pass_on(1 + 2 * n_row, total)
    for n in range(total):
        push(n).wait()


def carry_job(at, scalars, order, terr_stored, terr_all, whitened, directions, edge, v, pres, out):
    own = whitened.shape[0]
    cols = directions.shape[1]
    n_row = pres[0].shape[0]
    vmem = pl.BlockSpec(memory_space=pltpu.VMEM)
    smem = pl.BlockSpec(memory_space=pltpu.SMEM)
    any_spec = pl.BlockSpec(memory_space=pl.ANY)
    return pl.pallas_call(
        functools.partial(carry_kernel, at, n_row),
        in_specs=[smem] * 2 + [vmem] * 6 + [any_spec] * 3,
        out_specs=[vmem, any_spec],
        out_shape=[jax.ShapeDtypeStruct((own, cols), jnp.float32), out],
        scratch_shapes=[
            pltpu.SMEM((order.shape[0],), jnp.int32),
            pltpu.VMEM((2 * n_row, own, 2 * own), jnp.float32),
            pltpu.VMEM((n_row, own, pres[2].shape[2]), jnp.float32),
            pltpu.SemaphoreType.DMA((3 * n_row,)),
            pltpu.SemaphoreType.DMA((3 * n_row,)),
        ],
        name="carry",
        compiler_params=pltpu.CompilerParams(vmem_limit_bytes=60 * 1024 * 1024),
        cost_estimate=pl.CostEstimate(
            flops=6 * own * whitened.shape[1] * cols, bytes_accessed=60000000, transcendentals=0
        ),
    )(scalars, order, terr_stored, terr_all, whitened, directions, edge, v, *pres)


def tile_kernel(parts, rows_at, s_ref, *refs):
    n = 1 + max(i for _, _, sources, _ in parts for pair in sources.values() for i, _ in pair)
    bufs = refs[:n]
    a_ref, _, o_hbm, b_ref, o_ref, sem, o_sem = refs[n:]
    i = pl.program_id(0)
    steps = pl.num_programs(0)
    own = a_ref.shape[1]
    half = own // 2
    span = b_ref.shape[1]

    def copy(p, k, y, h):
        spot, row = parts[p][2][k][h]
        return pltpu.make_async_copy(
            bufs[spot].at[pl.ds(row, half)],
            b_ref.at[p, pl.ds((2 * y + h) * half, half)],
            sem.at[p, 2 * y + h],
        )

    @pl.when(i == 0)
    def _():
        for p, (at, wants, sources, _) in enumerate(parts):
            for y in range(2):
                for h in range(2):
                    needed = wants(s_ref[at + 4], y, h)
                    for k in sources:

                        @pl.when((s_ref[at + 1 + y] == k) & needed)
                        def _():
                            copy(p, k, y, h).start()

    slot = i % 2

    def outs(i, slot):
        copies = []
        first = 0
        for p, (at, _, _, width) in enumerate(parts):
            copies.append(
                pltpu.make_async_copy(
                    o_ref.at[slot, :, pl.ds(first, width)],
                    o_hbm.at[
                        pl.ds(pl.multiple_of(s_ref[rows_at + i] * own, own), own),
                        pl.ds(pl.multiple_of(s_ref[at] * span + s_ref[at + 3], 128), width),
                    ],
                    o_sem.at[p, slot],
                )
            )
            first += width
        return copies

    @pl.when(i >= 2)
    def _():
        for out in outs(i - 2, slot):
            out.wait()

    first = 0
    for p, (at, wants, sources, width) in enumerate(parts):

        @pl.when(i == 0)
        def _():
            for y in range(2):
                for h in range(2):

                    @pl.when(wants(s_ref[at + 4], y, h))
                    def _():
                        copy(p, next(iter(sources)), y, h).wait()

        o_ref[slot, :, first : first + width] = lax.dot_general(
            a_ref[0],
            b_ref[p, pl.ds(pl.multiple_of(s_ref[at + 3], 128), width), :],
            NT,
            preferred_element_type=jnp.float32,
        )
        outs(i, slot)[p].start()
        first += width

    @pl.when(i == steps - 1)
    def _():
        for out in outs(i - 1, 1 - slot) + outs(i, slot):
            out.wait()


def tile_job(scalars, rows_at, parts, bufs, rows, out):
    count, own, total = rows.shape
    span = 2 * own
    any_spec = pl.BlockSpec(memory_space=pl.ANY)
    arrays, made = [], []
    for at, wants, cands, width in parts:
        sources = {}
        for k in cands:
            pair = []
            for array, row in bufs[k]:
                spot = [i for i, a in enumerate(arrays) if a is array]
                if not spot:
                    arrays.append(array)
                    spot = [len(arrays) - 1]
                pair.append((spot[0], row))
            sources[k] = pair
        made.append((at, wants, sources, width))
    columns = sum(width for *_, width in parts)
    return pl.pallas_call(
        functools.partial(tile_kernel, made, rows_at),
        grid_spec=pltpu.PrefetchScalarGridSpec(
            num_scalar_prefetch=1,
            grid=(count,),
            in_specs=[any_spec] * len(arrays)
            + [pl.BlockSpec((1, own, total), lambda i, s: (i, 0, 0)), any_spec],
            out_specs=any_spec,
            scratch_shapes=[
                pltpu.VMEM((len(parts), span, total), jnp.bfloat16),
                pltpu.VMEM((2, own, columns), jnp.float32),
                pltpu.SemaphoreType.DMA((len(parts), 4)),
                pltpu.SemaphoreType.DMA((len(parts), 2)),
            ],
        ),
        out_shape=jax.ShapeDtypeStruct(out.shape, out.dtype),
        input_output_aliases={2 + len(arrays): 0},
        compiler_params=pltpu.CompilerParams(vmem_limit_bytes=60 * 1024 * 1024),
        cost_estimate=pl.CostEstimate(
            flops=2 * count * own * columns * total,
            bytes_accessed=2 * count * own * total + 4 * count * own * columns,
            transcendentals=0,
        ),
    )(scalars, *arrays, rows, out)


def ring_body(n_row, n_col, design, arc_filter, arc_of_row, terr_stored, block_order, directions):
    own, _ = design.shape
    block = terr_stored.shape[1]
    r = lax.axis_index("row")
    c = lax.axis_index("col")
    zs = n_col // 2
    half = own // 2
    far = n_col // 2

    def hop(a, perm):
        return lax.ppermute(a, "col", perm)

    col_of = [2 * p if p < zs else 2 * (n_col - 1 - p) + 1 for p in range(n_col)]
    pos_of = [0] * n_col
    for p, col in enumerate(col_of):
        pos_of[col] = p
    forward = [(col_of[p], col_of[(p + 1) % n_col]) for p in range(n_col)]
    backward = [(d, s) for s, d in forward]

    whitened = whiten_rows(design, arc_filter, arc_of_row)
    rows, up1, up2a, up2b, up3a, dn1, dn2a, dn2b, dn3b, terr_all, edge, _, *pres, v = exchange(
        n_row, n_col, whitened, terr_stored, directions
    )
    last = far - 1
    bufs = {
        2: [(dn2a, 0), (dn2b, 0)],
        n_col - 2: [(up2a, 0), (up2b, 0)],
        1: [(dn1, 0), (dn1, half)],
        n_col - 1: [(up1, 0), (up1, half)],
    }
    upper = hop(up2b, forward)
    lower = hop(dn2a, backward)
    bufs[n_col - last] = [(up3a, 0), (upper, 0)]
    bufs[last] = [(lower, 0), (dn3b, 0)]
    bufs[far] = [(hop(up3a, forward), 0), (hop(dn3b, backward), 0)]

    per_pair = 2 * own // block

    wide = own // 128 * 128
    names = ["tile1b", "tile2a", "tile2b"]
    by_col, by_row, ks_of = [], [], {name: [set(), set()] for name in names}
    for col in range(n_col):
        z, y = col // 2, col % 2
        line = []
        for name in names:
            zz = z ^ 2 if name == "tile1b" else z ^ 3
            ks = [(pos_of[2 * zz + yy] - pos_of[col]) % n_col for yy in range(2)]
            near = [min(k, n_col - k) for k in ks]
            late = int(near[1] > near[0])
            soon = name[-1] == "a"
            lo = (2 * own - wide) * (1 - late) if soon else wide * late
            line += [zz, ks[0], ks[1], lo, late]
            ks_of[name][0].add(ks[1 - late])
            ks_of[name][1].add(ks[late])
        line += [(pos_of[s] - pos_of[col]) % n_col for s in range(n_col)]
        by_col.append(line + [y, z * per_pair, z, z ^ 1, z ^ 2])
    for row in range(n_row):
        by_row.append([row ^ m for m in range(n_row)] + [row * per_pair * zs])
    scalars = jnp.concatenate(
        [jnp.asarray(by_col, jnp.int32)[c], jnp.asarray(by_row, jnp.int32)[r]]
    )
    at = {"spots": 5 * len(names)}
    at["side"] = at["spots"] + n_col
    at["pair"] = at["side"] + 1
    at["own"] = at["side"] + 2
    at["rows"] = at["side"] + 5
    at["first"] = at["rows"] + n_row

    out = jax.ShapeDtypeStruct((n_row * own, n_col * own), jnp.float32)
    products, out = carry_job(
        at, scalars, block_order, terr_stored, terr_all, whitened, directions, edge,
        v, pres, out,
    )
    early = lambda late, y, h: late == 1 - y
    tail = lambda late, y, h: (late == y) | (h == 1 - y)
    parts = []
    for j, name in enumerate(names):
        soon, late = ks_of[name]
        if name[-1] == "a":
            parts.append((5 * j, early, sorted(soon), wide))
        else:
            parts.append((5 * j, tail, sorted(soon | late), 2 * own - wide))
    for some in (parts[:2], parts[2:]):
        out = tile_job(scalars, at["rows"], some, bufs, rows, out)
    return out.reshape(n_row, 1, own, n_col * own), products


def power_of_two(n):
    return n > 1 and n & (n - 1) == 0


def solution(mesh):
    n_row, n_col = mesh.shape["row"], mesh.shape["col"]

    def body(design, arc_filter, arc_of_row, terr_stored, block_order, directions):
        args = (design, arc_filter, arc_of_row, terr_stored, block_order, directions)
        own, block = design.shape[0], terr_stored.shape[1]
        aligned = n_row > 2 and own % 192 == 0 and own % block == block // 2 and (2 * own) % 128 == 0
        if power_of_two(n_row) and n_col == 8 and aligned:
            return ring_body(n_row, n_col, *args)
        return general_body(*args)

    return jax.shard_map(
        body,
        mesh=mesh,
        in_specs=(
            P(("row", "col"), None),
            P(),
            P(),
            P(("row", "col"), None),
            P("row"),
            P(("row", "col"), None),
        ),
        out_specs=(P(None, "col", None, "row"), P(("row", "col"), None)),
        check_vma=False,
    )
```

```python
import functools

import jax
import jax.numpy as jnp
from jax import lax
from jax.experimental import pallas as pl
from jax.experimental.pallas import tpu as pltpu
from jax.sharding import PartitionSpec as P


HIGH = lax.Precision.HIGHEST
NT = (((1,), (1,)), ((), ()))
MESH = pl.DeviceIdType.MESH


def dot_high(a, b):
    return jnp.dot(a, b, precision=HIGH, preferred_element_type=jnp.float32)


def whiten(design, arc_filter, arc_of_row):
    positions = jnp.arange(arc_filter.shape[0], dtype=jnp.int32)
    keep_mask = (positions[:, None] > positions[None, :]) & (
        arc_of_row[:, None] == arc_of_row[None, :]
    )
    lower_part = jnp.where(keep_mask, arc_filter, jnp.zeros_like(arc_filter))
    mixed_part = lax.dot_general(design, lower_part, NT, preferred_element_type=jnp.float32)
    return (design.astype(jnp.float32) + mixed_part).astype(jnp.bfloat16)


def general_body(design, arc_filter, arc_of_row, terr_stored, block_order, directions):
    whitened = whiten(design, arc_filter, arc_of_row)
    own_width = whitened.shape[0]
    rows_block, terr_rows = (
        lax.all_gather(whitened, "col", axis=0, tiled=True),
        lax.all_gather(terr_stored, "col", axis=0, tiled=True),
    )
    cols_block = lax.all_gather(whitened, "row", axis=0, tiled=True)
    normal_tile = lax.dot_general(cols_block, rows_block, NT, preferred_element_type=jnp.float32)
    block_size = terr_rows.shape[1]
    span_rows = terr_rows.shape[0]
    group_count = span_rows // block_size
    row_index = lax.axis_index("row")
    col_index = lax.axis_index("col")
    local_order = block_order - row_index * group_count
    selector = (local_order[None, :] == jnp.arange(group_count, dtype=jnp.int32)[:, None]).astype(
        jnp.float32
    )
    stored = terr_rows.astype(jnp.float32).reshape(group_count, block_size, block_size)
    symmetric = jnp.triu(stored) + jnp.swapaxes(jnp.triu(stored, 1), 1, 2)
    ordered = jnp.einsum("qt,tab->qab", selector, symmetric, precision=HIGH).reshape(
        span_rows, block_size
    )
    own_rows = lax.dynamic_slice_in_dim(ordered, col_index * own_width, own_width, 0)
    positions = col_index * own_width + jnp.arange(own_width, dtype=jnp.int32)
    onehot = (
        (positions // block_size)[:, None] == jnp.arange(group_count, dtype=jnp.int32)[None, :]
    ).astype(jnp.float32)
    terr_added = (onehot[:, :, None] * own_rows[:, None, :]).reshape(own_width, span_rows)
    current = lax.dynamic_slice_in_dim(normal_tile, row_index * own_width, own_width, 0)
    normal_tile = lax.dynamic_update_slice_in_dim(
        normal_tile, current + terr_added, row_index * own_width, 0
    )
    tile_rows = normal_tile.shape[0]
    partial_sum = dot_high(normal_tile, lax.all_gather(directions, "col", axis=0, tiled=True))
    products = lax.psum_scatter(partial_sum, "row", scatter_dimension=0, tiled=True)
    normals = normal_tile.reshape(tile_rows // own_width, 1, own_width, span_rows)
    return (normals, products)


def xor(i, mask):
    return i + mask * (1 - 2 * ((i // mask) % 2))


def xor_all(i, mask, n):
    for m in masks_of(n):
        if mask & m:
            i = xor(i, m)
    return i


def split3(x):
    a = x.astype(jnp.bfloat16)
    rest = x - a.astype(jnp.float32)
    b = rest.astype(jnp.bfloat16)
    return a, b, (rest - b.astype(jnp.float32)).astype(jnp.bfloat16)


def wide3(x):
    return jnp.concatenate(split3(x), 1)


def fold3(x):
    n = x.shape[1] // 3
    return x[:, 2 * n :] + x[:, n : 2 * n] + x[:, :n]


def whiten_kernel(d_ref, dp_ref, f_ref, fp_ref, ar_ref, arp_ref, w_ref):
    b = pl.program_id(0)
    width = f_ref.shape[0]
    zero = jnp.zeros((width, width), jnp.float32)
    k = lax.broadcasted_iota(jnp.int32, (width, width), 0)
    j = lax.broadcasted_iota(jnp.int32, (width, width), 1)
    column = jnp.broadcast_to(ar_ref[...], (128, width)).T[:, :1]
    keep = (k > j) & (column == ar_ref[...])
    keep_prev = (column == arp_ref[...]) & (b > 0)
    here = jnp.where(keep, f_ref[...].astype(jnp.float32), zero).astype(jnp.bfloat16)
    prev = jnp.where(keep_prev, fp_ref[...].astype(jnp.float32), zero).astype(jnp.bfloat16)
    mixed = lax.dot_general(d_ref[...], here, NT, preferred_element_type=jnp.float32)
    mixed += lax.dot_general(dp_ref[...], prev, NT, preferred_element_type=jnp.float32)
    w_ref[...] = (d_ref[...].astype(jnp.float32) + mixed).astype(jnp.bfloat16)


def whiten_rows(design, arc_filter, arc_of_row):
    own, total = design.shape
    width = total // 4
    here = lambda b: (0, b)
    prev = lambda b: (0, jnp.maximum(b - 1, 0))
    row = arc_of_row.reshape(1, total)
    return pl.pallas_call(
        whiten_kernel,
        grid=(total // width,),
        in_specs=[
            pl.BlockSpec((own, width), here),
            pl.BlockSpec((own, width), prev),
            pl.BlockSpec((width, width), lambda b: (b, b)),
            pl.BlockSpec((width, width), lambda b: (b, jnp.maximum(b - 1, 0))),
            pl.BlockSpec((1, width), here),
            pl.BlockSpec((1, width), prev),
        ],
        out_specs=pl.BlockSpec((own, width), here),
        out_shape=jax.ShapeDtypeStruct((own, total), jnp.bfloat16),
        name="whiten",
        cost_estimate=pl.CostEstimate(
            flops=4 * own * total * width, bytes_accessed=8 * own * total, transcendentals=0
        ),
    )(design, design, arc_filter, arc_filter, row, row)


def masks_of(n):
    return [1 << i for i in range(n.bit_length() - 1)]


def exchange_kernel(n_row, n_col, parts, w_ref, t_ref, d_ref, *refs):
    rows_ref, up1, up2a, up2b, up3a, dn1, dn2a, dn2b, dn3b = refs[:9]
    terr_ref, edge_ref, side_ref, pre_ref, pre0_ref, pre1_ref, vout = refs[9:16]
    b_ref, b0_ref, b1_ref, a_ref, o_ref, got, acc, pack = refs[16:24]
    s_loc, s_a, s_o, s_ring, r_ring, s_row, r_row, s_terr, r_terr, s_v, r_v, s_e, r_e = refs[24:]
    r = lax.axis_index("row")
    c = lax.axis_index("col")
    own, width = w_ref.shape
    sub = own // parts
    zs = n_col // 2
    z, y = c // 2, c % 2
    place = z + y * (n_col - 1 - 2 * z)
    by_up = place % zs == 0
    by_down = place % zs == zs - 1
    inner = (place % zs > 0) & (place % zs < zs - 1)

    def col_at(p):
        side = p // zs
        return 2 * (p + side * (n_col - 1 - 2 * p)) + side

    nxt = col_at((place + 1) % n_col)
    prv = col_at((place + n_col - 1) % n_col)
    row_masks = masks_of(n_row)
    peers = [(r, nxt), (r, prv)]
    peers += [(xor(r, m), c) for m in row_masks] + [(r, xor(c, 1))]
    peers += [(r, 2 * xor_all(z, m, zs) + y) for m in range(1, zs)]
    barrier = pltpu.get_barrier_semaphore()
    for peer in peers:
        pl.semaphore_signal(barrier, inc=1, device_id=peer, device_id_type=MESH)
    pl.semaphore_wait(barrier, len(peers))

    def remote(src, dst, ssem, rsem, peer):
        return pltpu.make_async_remote_copy(
            src_ref=src, dst_ref=dst, send_sem=ssem, recv_sem=rsem, device_id=peer,
            device_id_type=MESH,
        )

    def piece(ref, j):
        return ref.at[pl.ds(j * sub, sub)]

    sends = []

    def start(copy):
        copy.start()
        sends.append(copy)

    half = parts // 2
    steps = 2 * parts + half
    ahead = 4

    def ring(s, way):
        one, two, three = ((up1, (up2a, up2b), up3a), (dn1, (dn2a, dn2b), dn3b))[way]
        j = s % parts
        if s < parts:
            src, dst = piece(w_ref, j), piece(one, j)
        elif s < 2 * parts:
            src, dst = piece(one, j), piece(two[j // half], j % half)
        else:
            src, dst = piece(two[way], j), piece(three, j)
        return remote(src, dst, s_ring.at[way, s], r_ring.at[way, s], (r, (nxt, prv)[way]))

    rings = [[ring(s, way) for way in range(2)] for s in range(steps)]
    for s in range(ahead):
        for way in range(2):
            start(rings[s][way])

    mine = pl.ds(pl.multiple_of(y * own, own), own)
    other = pl.ds(pl.multiple_of((1 - y) * own, own), own)
    load = pltpu.make_async_copy(w_ref, b_ref.at[mine], s_loc.at[0])
    load.start()

    far = n_col // 2
    h = t_ref.shape[1] // 2
    pairs = own // h // 2
    k = lax.broadcasted_iota(jnp.int32, (h, 2 * h), 0)
    lane = lax.broadcasted_iota(jnp.int32, (h, 2 * h), 1)
    line = lax.broadcasted_iota(jnp.int32, (16, 2 * h), 0)
    diagonals = jnp.zeros((16, 2 * h), jnp.float32)

    def stored(i):
        return t_ref[pl.ds(pl.multiple_of(i * h, h), h), :].astype(jnp.float32)

    for p in range(pairs):
        top, low = stored(2 * p + y), stored(2 * p + 1 + y)
        turned = pltpu.roll(jnp.concatenate([top, low], 0).T[h:], h, 1)
        pack[p * h : (p + 1) * h] = jnp.where(k <= lane, top, turned).astype(pack.dtype)
        row = jnp.sum(jnp.where(lane == k + h, low, 0.0), axis=0, keepdims=True)
        diagonals = jnp.where(line == p, row, diagonals)
    pack[pairs * h : (pairs + 1) * h] = stored(2 * pairs * (1 - y)).astype(pack.dtype)
    pack[(pairs + 1) * h :] = diagonals.astype(pack.dtype)
    keep_pack = pltpu.make_async_copy(pack, terr_ref.at[0], s_loc.at[8])
    keep_pack.start()

    def terr(k, way):
        src = pack if k == 1 else terr_ref.at[(n_col - k + 1) if way == 0 else k - 1]
        at = (n_col - k) if way == 0 else k
        return remote(src, terr_ref.at[at], s_terr.at[way, k - 1], r_terr.at[way, k - 1],
                      (r, (nxt, prv)[way]))

    terrs = {}
    for k in range(1, far + 1):
        terrs[k] = [terr(k, 0)] + ([terr(k, 1)] if k < far else [])
    for copy in terrs[1]:
        start(copy)
    edge = edge_ref.shape[0]
    edge_at = pl.ds(pl.multiple_of((1 - y) * (own - edge), edge), edge)
    edges = remote(d_ref.at[edge_at], edge_ref, s_e.at[0], r_e.at[0], (r, xor(c, 1)))
    start(edges)
    across = remote(w_ref, side_ref, s_e.at[1], r_e.at[1], (r, xor(c, 1)))

    @pl.when(inner)
    def _():
        across.start()

    order = []
    for mask in reversed(row_masks):
        for m in range(0, n_row, 2 * mask):
            order.append((m + mask, mask))

    def row_copy(key, j):
        m, mask = key
        n = order.index(key)
        src = w_ref if m == mask else rows_ref.at[m - mask]
        return remote(piece(src, j), piece(rows_ref.at[m], j), s_row.at[n, j], r_row.at[n, j],
                      (xor(r, mask), c))

    copies = {key: [row_copy(key, j) for j in range(parts)] for key in order}
    filled = {m: (m, mask) for m, mask in order}
    later = [key for key in order if key[0] != key[1]]
    waited = set()

    def row_wait(key, j):
        if (key, j) not in waited:
            copies[key][j].wait_recv()
            waited.add((key, j))

    load.wait()
    put = pltpu.make_async_copy(b_ref.at[mine], rows_ref.at[0], s_loc.at[1])
    put.start()
    dirs = wide3(d_ref[...])
    chunk = width // 8

    @pl.loop(0, 8)
    def _(t):
        span = pl.ds(pl.multiple_of(t * chunk, chunk), chunk)
        acc[span, :] = fold3(
            lax.dot_general(
                b_ref[mine, span], dirs, (((0,), (0,)), ((), ())),
                preferred_element_type=jnp.float32,
            )
        )

    levels = [((xor(r, m), c), (r // m) % 2) for m in row_masks] + [((r, xor(c, 1)), y)]
    n = len(levels)
    span = width
    offset = base = 0
    gives, keeps, spots = [], [], []
    for i, (peer, bit) in enumerate(levels):
        span //= 2
        give = pl.ds(pl.multiple_of(offset + (1 - bit) * span, span), span)
        offset = offset + bit * span
        keep = pl.ds(pl.multiple_of(offset, span), span)
        spot = pl.ds(base, span)
        base += span
        gives.append(remote(acc.at[give], got.at[spot], s_v.at[i], r_v.at[i], peer))
        keeps.append(keep)
        spots.append(spot)
    bit = span // zs
    at_out = pl.ds(pl.multiple_of(offset + z * bit, bit), bit)
    fans, backs = [], []
    for m in range(1, zs):
        zz = xor_all(z, m, zs)
        peer = (r, 2 * zz + y)
        give = pl.ds(pl.multiple_of(offset + zz * bit, bit), bit)
        spot = pl.ds(base + (m - 1) * bit, bit)
        at = n + 2 * m - 2
        fans.append(remote(acc.at[give], got.at[spot], s_v.at[at], r_v.at[at], peer))
        backs.append(
            remote(vout.at[at_out], vout.at[at_out], s_v.at[at + 1], r_v.at[at + 1], peer)
        )
    at = n + 2 * zs - 2
    wider = [
        remote(vout.at[keeps[i]], vout.at[keeps[i]], s_v.at[at + i], r_v.at[at + i], levels[i][0])
        for i in range(n)
    ]

    def finish(i):
        gives[i].wait()
        acc[keeps[i]] = acc[keeps[i]] + got[spots[i]]

    def fan_in():
        for copy in fans:
            copy.wait()
        mid = acc[pl.ds(pl.multiple_of(offset + z * bit, bit), bit)]
        for m in range(1, zs):
            mid = mid + got[base + (m - 1) * bit : base + m * bit]
        vout[at_out] = mid

    def each(copies, method):
        for copy in copies:
            getattr(copy, method)()

    todo = [lambda: gives[0].start()]
    for i in range(1, n):
        todo.append(lambda i=i: (finish(i - 1), gives[i].start()))
    todo.append(lambda: (finish(n - 1), each(fans, "start")))
    todo.append(lambda: (fan_in(), each(backs, "start")))
    todo.append(lambda: (each(backs, "wait"), wider[n - 1].start()))
    for i in range(n - 1, 0, -1):
        todo.append(lambda i=i: (wider[i].wait(), wider[i - 1].start()))
    todo.append(lambda: wider[0].wait())

    def v_next():
        if todo:
            todo.pop(0)()

    v_next()
    v_next()
    for key in order:
        if key[0] == key[1]:
            for copy in copies[key]:
                start(copy)

    wide = own // 128 * 128
    rest = 2 * own - wide
    near_at = pl.multiple_of(y * (2 * own - wide), 128)
    rest_at = pl.multiple_of((1 - y) * wide, 128)
    up_first = place % zs < zs // 2

    def fill(refs, b, at, n):
        size = own // len(refs)
        return [
            pltpu.make_async_copy(ref, b.at[pl.ds(at + i * size, size)], s_loc.at[n + i])
            for i, ref in enumerate(refs)
        ]

    def other_start():
        start_at = (1 - y) * own

        @pl.when(inner)
        def _():
            across.wait()
            each(fill([side_ref], b_ref, start_at, 2), "start")

        @pl.when(by_up)
        def _():
            each(fill([up1], b_ref, start_at, 2), "start")

        @pl.when(by_down)
        def _():
            each(fill([dn1], b_ref, start_at, 2), "start")

        @pl.when(place % 2 == 0)
        def _():
            each(fill([dn1], b0_ref, y * own, 3), "start")

        @pl.when(place % 2 == 1)
        def _():
            each(fill([up1], b0_ref, y * own, 3), "start")

    def second_start():
        @pl.when(up_first)
        def _():
            each(fill([up2a, up2b], b0_ref, (1 - y) * own, 4), "start")
            each(fill([dn2a, dn2b], b1_ref, 0, 6), "start")

        @pl.when(place % zs >= zs // 2)
        def _():
            each(fill([dn2a, dn2b], b0_ref, (1 - y) * own, 4), "start")
            each(fill([up2a, up2b], b1_ref, 0, 6), "start")

    def a_load(m):
        return pltpu.make_async_copy(rows_ref.at[m], a_ref.at[m], s_a.at[m])

    stores = []

    def dots(m, rows, width, into):
        n = len(stores)
        for store in stores[-2:]:
            store.wait()

        def store(t):
            return pltpu.make_async_copy(
                o_ref.at[t, :, pl.ds(0, width)], into(m + t), s_o.at[n + t]
            )

        @pl.loop(0, 2)
        def _(t):
            o_ref[t, :, :width] = lax.dot_general(
                a_ref[m + t], rows(), NT, preferred_element_type=jnp.float32
            )
            store(t).start()

        stores.extend([store(0), store(1)])

    def own_tile(m):
        for i in range(2):
            a_load(m + i).wait()
        if m == 0:
            each(fill([side_ref], b_ref, 0, 2), "wait")
        dots(m, lambda: b_ref[...], 2 * own, lambda m: pre_ref.at[m])

    def near_tile(m):
        if m == 0:
            each(fill([up1], b0_ref, 0, 3), "wait")
        span = pl.ds(near_at, wide)
        dots(m, lambda: b0_ref[span, :], wide, lambda m: pre0_ref.at[m, :, span])

    def rest_tile(m):
        if m == 0:
            each(fill([up2a, up2b], b0_ref, 0, 4), "wait")
        span = pl.ds(rest_at, rest)
        dots(m, lambda: b0_ref[span, :], rest, lambda m: pre0_ref.at[m, :, span])

    def side_tile(m):
        if m == 0:
            each(fill([up2a, up2b], b1_ref, 0, 6), "wait")
        at = pl.multiple_of(y * (own - wide), own - wide)
        dots(m, lambda: b1_ref[pl.ds(at, wide), :], wide, lambda m: pre1_ref.at[m])

    hop = 1
    lag = parts // 2
    v_at = [ahead + i * (ahead + 1) for i in range(5)] + [steps - 3, steps - 1]
    work = {}
    for m in range(0, n_row, 2):
        work.setdefault(parts + 1 + (lag + 1) * (m // 2), []).append((own_tile, m))
        work.setdefault(2 * parts - 3 + m // 2, []).append((near_tile, m))
        work.setdefault(2 * parts + m // 2, []).append((rest_tile, m))
        work.setdefault(2 * parts + 3 + m // 2, []).append((side_tile, m))
    for s in range(steps):
        for way in range(2):
            rings[s][way].wait_recv()
        if s in v_at:
            v_next()
        if s % 3 == 2 and hop <= far:
            for copy in terrs[hop]:
                copy.wait_recv()
            hop += 1
            if hop <= far:
                for copy in terrs[hop]:
                    start(copy)
        if s + ahead < steps:
            for way in range(2):
                start(rings[s + ahead][way])
        j = s - lag
        if 0 <= j < parts:
            for key in later:
                row_wait(filled[key[0] - key[1]], j)
                start(copies[key][j])
        if s == parts - 1:
            other_start()
            put.wait()
            a_load(0).start()
            for j in range(parts):
                row_wait(filled[1], j)
            a_load(1).start()
        if s == parts + lag - 1:
            for m in range(2, n_row):
                for j in range(parts):
                    row_wait(filled[m], j)
                a_load(m).start()
        if s == 2 * parts - 1:
            second_start()
        for do, m in work.get(s, []):
            do(m)
    while hop <= far:
        for copy in terrs[hop]:
            copy.wait_recv()
        hop += 1
        if hop <= far:
            for copy in terrs[hop]:
                start(copy)
    while todo:
        v_next()
    edges.wait_recv()
    keep_pack.wait()
    for store in stores[-2:]:
        store.wait()
    for copy in sends:
        copy.wait_send()


def exchange(n_row, n_col, whitened, terr_stored, directions):
    own, total = whitened.shape
    cols = directions.shape[1]
    block = terr_stored.shape[1]
    packed = ((2 * own // block // 2 + 1) * block // 2 + 16, block)
    parts = 12
    far = n_col // 2
    any_spec = pl.BlockSpec(memory_space=pl.ANY)
    vmem = pl.BlockSpec(memory_space=pltpu.VMEM)
    whole = jax.ShapeDtypeStruct((own, total), jnp.bfloat16)
    part = jax.ShapeDtypeStruct((own // 2, total), jnp.bfloat16)
    levels = 2 * n_row.bit_length() + n_col
    moves = n_row - 1
    dma = pltpu.SemaphoreType.DMA
    return pl.pallas_call(
        functools.partial(exchange_kernel, n_row, n_col, parts),
        in_specs=[any_spec, vmem, vmem],
        out_specs=[any_spec] * 15 + [vmem],
        out_shape=[
            jax.ShapeDtypeStruct((n_row, own, total), jnp.bfloat16),
            whole, part, part, part, whole, part, part, part,
            jax.ShapeDtypeStruct((n_col,) + packed, jnp.bfloat16),
            jax.ShapeDtypeStruct((block // 2, cols), jnp.float32),
            whole,
            jax.ShapeDtypeStruct((n_row, own, 2 * own), jnp.float32),
            jax.ShapeDtypeStruct((n_row, own, 2 * own), jnp.float32),
            jax.ShapeDtypeStruct((n_row, own, own // 128 * 128), jnp.float32),
            jax.ShapeDtypeStruct((total, cols), jnp.float32),
        ],
        scratch_shapes=[
            pltpu.VMEM((2 * own, total), jnp.bfloat16),
            pltpu.VMEM((2 * own, total), jnp.bfloat16),
            pltpu.VMEM((own, total), jnp.bfloat16),
            pltpu.VMEM((n_row, own, total), jnp.bfloat16),
            pltpu.VMEM((2, own, 2 * own), jnp.float32),
            pltpu.VMEM((total, cols), jnp.float32),
            pltpu.VMEM((total, cols), jnp.float32),
            pltpu.VMEM(packed, jnp.bfloat16),
            dma((9,)),
            dma((n_row,)),
            dma((4 * n_row,)),
            dma((2, 3 * parts)), dma((2, 3 * parts)),
            dma((moves, parts)), dma((moves, parts)),
            dma((2, far)), dma((2, far)),
            dma((levels,)), dma((levels,)),
            dma((2,)), dma((2,)),
        ],
        name="exchange",
        compiler_params=pltpu.CompilerParams(
            collective_id=0, has_side_effects=True, vmem_limit_bytes=60 * 1024 * 1024
        ),
        cost_estimate=pl.CostEstimate(
            flops=1000000, bytes_accessed=40 * own * total, transcendentals=0
        ),
    )(whitened, terr_stored, directions)


def carry_kernel(at, n_row, s_ref, order_ref, t_ref, w_ref, d_ref, e_ref, v_ref, *refs):
    pre_ref, pre0_ref, pre1_ref, p_ref, out_ref, inv_ref, q_ref, q1_ref, pull_sem, push_sem = refs
    own, span = q_ref.shape[1:]
    wide = q1_ref.shape[2]
    half = e_ref.shape[0]
    block = 2 * half
    per = own // half
    count = order_ref.shape[0]
    side = s_ref[at["side"]]
    pair = s_ref[at["pair"]]

    def pull(n):
        src = (pre_ref, pre0_ref, pre1_ref)[n // n_row].at[n % n_row]
        dst = q_ref.at[n] if n < 2 * n_row else q1_ref.at[n - 2 * n_row]
        return pltpu.make_async_copy(src, dst, pull_sem.at[n])

    def push(n):
        kind, m = n // n_row, n % n_row
        zz = s_ref[at["own"] + kind]
        column = zz * span if kind < 2 else zz * span + side * (span - wide)
        src = q_ref.at[n] if kind < 2 else q1_ref.at[m]
        return pltpu.make_async_copy(
            src,
            out_ref.at[
                pl.ds(pl.multiple_of(s_ref[at["rows"] + m] * own, own), own),
                pl.ds(pl.multiple_of(column, 128), span if kind < 2 else wide),
            ],
            push_sem.at[n],
        )

    total = 3 * n_row
    for n in range(total):
        pull(n).start()

    @pl.loop(0, count)
    def _(t):
        inv_ref[order_ref[t] - s_ref[at["first"]]] = t

    def pass_on(lo, hi):
        for n in range(lo, hi):
            pull(n).wait()
            push(n).start()

    size = v_ref.shape[0] // n_row
    for m in range(n_row):
        part = slice(m * size, (m + 1) * size)
        term = fold3(
            jnp.dot(w_ref[:, part], wide3(v_ref[part, :]), preferred_element_type=jnp.float32)
        )
        p_ref[...] = p_ref[...] + term if m else term
        pass_on(1 + 2 * m, 3 + 2 * m)
    pull(0).wait()
    k = lax.broadcasted_iota(jnp.int32, (block, block), 0)
    j = lax.broadcasted_iota(jnp.int32, (block, block), 1)

    pairs = per // 2
    zero = jnp.zeros((half, block), jnp.float32)
    upper = lax.broadcasted_iota(jnp.int32, (half, block), 0)
    lane = lax.broadcasted_iota(jnp.int32, (half, block), 1)
    line = lax.broadcasted_iota(jnp.int32, (16, block), 0)

    def symmetric(t):
        one, two = 2 * t // per, (2 * t + 1) // per
        p = 2 * t % per // 2
        slot = s_ref[at["spots"] + one]
        split = one != two

        def read(slot, first, n):
            return t_ref[slot, pl.ds(first, n), :].astype(jnp.float32)

        top = read(slot, pl.multiple_of(p * half, half), half)
        low = read(s_ref[at["spots"] + two], pairs * half, half)
        row = jnp.sum(
            jnp.where(line == p, read(slot, (pairs + 1) * half, 16), 0.0), axis=0, keepdims=True
        )
        turned = jnp.where((upper > lane) & (lane < half), top, 0.0)
        turned = jnp.where(split, zero, pltpu.roll(turned, half, 1))
        s = jnp.concatenate([top, jnp.where(split, low, zero)], 0)
        strict = jnp.where(k < j, s, 0.0) + jnp.concatenate([zero, turned], 0)
        diagonal = jnp.where(split | (k < half), s, row)
        return strict + strict.T + jnp.where(k == j, diagonal, 0.0)

    edge = e_ref[...]
    for q in range(span // block):
        lo = 2 * q

        @pl.when((lo + 1 >= side * per) & (lo < side * per + per))
        def _(q=q, lo=lo):
            sym = symmetric(inv_ref[pair + q])
            for h in range(2):
                i = lo + h - side * per

                @pl.when((i >= 0) & (i < per))
                def _():
                    mine = pl.ds(pl.multiple_of(i * half, half), half)
                    rows = sym[h * half : (h + 1) * half]
                    q_ref[0, mine, q * block : (q + 1) * block] += rows
                    other = i + 1 - 2 * h
                    inside = (other >= 0) & (other < per)
                    safe = jnp.minimum(jnp.maximum(other, 0), per - 1)
                    beside = d_ref[pl.ds(pl.multiple_of(safe * half, half), half), :]
                    beside = jnp.where(inside, beside, edge)
                    this = d_ref[mine, :]
                    near = jnp.concatenate([beside, this] if h else [this, beside], 0)
                    p_ref[mine, :] += fold3(
                        jnp.dot(
                            rows.astype(jnp.bfloat16), wide3(near),
                            preferred_element_type=jnp.float32,
                        )
                    )

    push(0).start()
    pass_on(1 + 2 * n_row, total)
    for n in range(total):
        push(n).wait()


def carry_job(at, scalars, order, terr_all, whitened, directions, edge, v, pres, out):
    own = whitened.shape[0]
    cols = directions.shape[1]
    n_row = pres[0].shape[0]
    vmem = pl.BlockSpec(memory_space=pltpu.VMEM)
    smem = pl.BlockSpec(memory_space=pltpu.SMEM)
    any_spec = pl.BlockSpec(memory_space=pl.ANY)
    return pl.pallas_call(
        functools.partial(carry_kernel, at, n_row),
        in_specs=[smem] * 2 + [vmem] * 5 + [any_spec] * 3,
        out_specs=[vmem, any_spec],
        out_shape=[jax.ShapeDtypeStruct((own, cols), jnp.float32), out],
        scratch_shapes=[
            pltpu.SMEM((order.shape[0],), jnp.int32),
            pltpu.VMEM((2 * n_row, own, 2 * own), jnp.float32),
            pltpu.VMEM((n_row, own, pres[2].shape[2]), jnp.float32),
            pltpu.SemaphoreType.DMA((3 * n_row,)),
            pltpu.SemaphoreType.DMA((3 * n_row,)),
        ],
        name="carry",
        compiler_params=pltpu.CompilerParams(vmem_limit_bytes=60 * 1024 * 1024),
        cost_estimate=pl.CostEstimate(
            flops=6 * own * whitened.shape[1] * cols, bytes_accessed=60000000, transcendentals=0
        ),
    )(scalars, order, terr_all, whitened, directions, edge, v, *pres)


def tile_kernel(parts, rows_at, s_ref, *refs):
    n = 1 + max(i for _, _, sources, _ in parts for pair in sources.values() for i, _ in pair)
    bufs = refs[:n]
    a_ref, _, o_hbm, b_ref, o_ref, sem, o_sem = refs[n:]
    i = pl.program_id(0)
    steps = pl.num_programs(0)
    own = a_ref.shape[1]
    half = own // 2
    span = b_ref.shape[1]

    def copy(p, k, y, h):
        spot, row = parts[p][2][k][h]
        return pltpu.make_async_copy(
            bufs[spot].at[pl.ds(row, half)],
            b_ref.at[p, pl.ds((2 * y + h) * half, half)],
            sem.at[p, 2 * y + h],
        )

    @pl.when(i == 0)
    def _():
        for p, (at, wants, sources, _) in enumerate(parts):
            for y in range(2):
                for h in range(2):
                    needed = wants(s_ref[at + 4], y, h)
                    for k in sources:

                        @pl.when((s_ref[at + 1 + y] == k) & needed)
                        def _():
                            copy(p, k, y, h).start()

    slot = i % 2

    def outs(i, slot):
        copies = []
        first = 0
        for p, (at, _, _, width) in enumerate(parts):
            copies.append(
                pltpu.make_async_copy(
                    o_ref.at[slot, :, pl.ds(first, width)],
                    o_hbm.at[
                        pl.ds(pl.multiple_of(s_ref[rows_at + i] * own, own), own),
                        pl.ds(pl.multiple_of(s_ref[at] * span + s_ref[at + 3], 128), width),
                    ],
                    o_sem.at[p, slot],
                )
            )
            first += width
        return copies

    @pl.when(i >= 2)
    def _():
        for out in outs(i - 2, slot):
            out.wait()

    first = 0
    for p, (at, wants, sources, width) in enumerate(parts):

        @pl.when(i == 0)
        def _():
            for y in range(2):
                for h in range(2):

                    @pl.when(wants(s_ref[at + 4], y, h))
                    def _():
                        copy(p, next(iter(sources)), y, h).wait()

        o_ref[slot, :, first : first + width] = lax.dot_general(
            a_ref[0],
            b_ref[p, pl.ds(pl.multiple_of(s_ref[at + 3], 128), width), :],
            NT,
            preferred_element_type=jnp.float32,
        )
        outs(i, slot)[p].start()
        first += width

    @pl.when(i == steps - 1)
    def _():
        for out in outs(i - 1, 1 - slot) + outs(i, slot):
            out.wait()


def tile_job(scalars, rows_at, parts, bufs, rows, out):
    count, own, total = rows.shape
    span = 2 * own
    any_spec = pl.BlockSpec(memory_space=pl.ANY)
    arrays, made = [], []
    for at, wants, cands, width in parts:
        sources = {}
        for k in cands:
            pair = []
            for array, row in bufs[k]:
                spot = [i for i, a in enumerate(arrays) if a is array]
                if not spot:
                    arrays.append(array)
                    spot = [len(arrays) - 1]
                pair.append((spot[0], row))
            sources[k] = pair
        made.append((at, wants, sources, width))
    columns = sum(width for *_, width in parts)
    return pl.pallas_call(
        functools.partial(tile_kernel, made, rows_at),
        grid_spec=pltpu.PrefetchScalarGridSpec(
            num_scalar_prefetch=1,
            grid=(count,),
            in_specs=[any_spec] * len(arrays)
            + [pl.BlockSpec((1, own, total), lambda i, s: (i, 0, 0)), any_spec],
            out_specs=any_spec,
            scratch_shapes=[
                pltpu.VMEM((len(parts), span, total), jnp.bfloat16),
                pltpu.VMEM((2, own, columns), jnp.float32),
                pltpu.SemaphoreType.DMA((len(parts), 4)),
                pltpu.SemaphoreType.DMA((len(parts), 2)),
            ],
        ),
        out_shape=jax.ShapeDtypeStruct(out.shape, out.dtype),
        input_output_aliases={2 + len(arrays): 0},
        compiler_params=pltpu.CompilerParams(vmem_limit_bytes=60 * 1024 * 1024),
        cost_estimate=pl.CostEstimate(
            flops=2 * count * own * columns * total,
            bytes_accessed=2 * count * own * total + 4 * count * own * columns,
            transcendentals=0,
        ),
    )(scalars, *arrays, rows, out)


def ring_body(n_row, n_col, design, arc_filter, arc_of_row, terr_stored, block_order, directions):
    own, _ = design.shape
    block = terr_stored.shape[1]
    r = lax.axis_index("row")
    c = lax.axis_index("col")
    zs = n_col // 2
    half = own // 2
    far = n_col // 2

    def hop(a, perm):
        return lax.ppermute(a, "col", perm)

    col_of = [2 * p if p < zs else 2 * (n_col - 1 - p) + 1 for p in range(n_col)]
    pos_of = [0] * n_col
    for p, col in enumerate(col_of):
        pos_of[col] = p
    forward = [(col_of[p], col_of[(p + 1) % n_col]) for p in range(n_col)]
    backward = [(d, s) for s, d in forward]

    whitened = whiten_rows(design, arc_filter, arc_of_row)
    rows, up1, up2a, up2b, up3a, dn1, dn2a, dn2b, dn3b, terr_all, edge, _, *pres, v = exchange(
        n_row, n_col, whitened, terr_stored, directions
    )
    last = far - 1
    bufs = {
        2: [(dn2a, 0), (dn2b, 0)],
        n_col - 2: [(up2a, 0), (up2b, 0)],
        1: [(dn1, 0), (dn1, half)],
        n_col - 1: [(up1, 0), (up1, half)],
    }
    upper = hop(up2b, forward)
    lower = hop(dn2a, backward)
    bufs[n_col - last] = [(up3a, 0), (upper, 0)]
    bufs[last] = [(lower, 0), (dn3b, 0)]
    bufs[far] = [(hop(up3a, forward), 0), (hop(dn3b, backward), 0)]

    per_pair = 2 * own // block

    wide = own // 128 * 128
    names = ["tile1b", "tile2a", "tile2b"]
    by_col, by_row, ks_of = [], [], {name: [set(), set()] for name in names}
    for col in range(n_col):
        z, y = col // 2, col % 2
        line = []
        for name in names:
            zz = z ^ 2 if name == "tile1b" else z ^ 3
            ks = [(pos_of[2 * zz + yy] - pos_of[col]) % n_col for yy in range(2)]
            near = [min(k, n_col - k) for k in ks]
            late = int(near[1] > near[0])
            soon = name[-1] == "a"
            lo = (2 * own - wide) * (1 - late) if soon else wide * late
            line += [zz, ks[0], ks[1], lo, late]
            ks_of[name][0].add(ks[1 - late])
            ks_of[name][1].add(ks[late])
        line += [(pos_of[s] - pos_of[col]) % n_col for s in range(n_col)]
        by_col.append(line + [y, z * per_pair, z, z ^ 1, z ^ 2])
    for row in range(n_row):
        by_row.append([row ^ m for m in range(n_row)] + [row * per_pair * zs])
    scalars = jnp.concatenate(
        [jnp.asarray(by_col, jnp.int32)[c], jnp.asarray(by_row, jnp.int32)[r]]
    )
    at = {"spots": 5 * len(names)}
    at["side"] = at["spots"] + n_col
    at["pair"] = at["side"] + 1
    at["own"] = at["side"] + 2
    at["rows"] = at["side"] + 5
    at["first"] = at["rows"] + n_row

    out = jax.ShapeDtypeStruct((n_row * own, n_col * own), jnp.float32)
    products, out = carry_job(
        at, scalars, block_order, terr_all, whitened, directions, edge,
        v, pres, out,
    )
    early = lambda late, y, h: late == 1 - y
    tail = lambda late, y, h: (late == y) | (h == 1 - y)
    parts = []
    for j, name in enumerate(names):
        soon, late = ks_of[name]
        if name[-1] == "a":
            parts.append((5 * j, early, sorted(soon), wide))
        else:
            parts.append((5 * j, tail, sorted(soon | late), 2 * own - wide))
    for some in (parts[:2], parts[2:]):
        out = tile_job(scalars, at["rows"], some, bufs, rows, out)
    return out.reshape(n_row, 1, own, n_col * own), products


def power_of_two(n):
    return n > 1 and n & (n - 1) == 0


def solution(mesh):
    n_row, n_col = mesh.shape["row"], mesh.shape["col"]

    def body(design, arc_filter, arc_of_row, terr_stored, block_order, directions):
        args = (design, arc_filter, arc_of_row, terr_stored, block_order, directions)
        own, block = design.shape[0], terr_stored.shape[1]
        aligned = n_row > 2 and own % 192 == 0 and own % block == block // 2 and (2 * own) % 128 == 0
        if power_of_two(n_row) and n_col == 8 and aligned:
            return ring_body(n_row, n_col, *args)
        return general_body(*args)

    return jax.shard_map(
        body,
        mesh=mesh,
        in_specs=(
            P(("row", "col"), None),
            P(),
            P(),
            P(("row", "col"), None),
            P("row"),
            P(("row", "col"), None),
        ),
        out_specs=(P(None, "col", None, "row"), P(("row", "col"), None)),
        check_vma=False,
    )
```

```python
import functools

import jax
import jax.numpy as jnp
from jax import lax
from jax.experimental import pallas as pl
from jax.experimental.pallas import tpu as pltpu
from jax.sharding import PartitionSpec as P


HIGH = lax.Precision.HIGHEST
NT = (((1,), (1,)), ((), ()))
MESH = pl.DeviceIdType.MESH
VMEM_BYTES = 67043328


def dot_high(a, b):
    return jnp.dot(a, b, precision=HIGH, preferred_element_type=jnp.float32)


def whiten(design, arc_filter, arc_of_row):
    positions = jnp.arange(arc_filter.shape[0], dtype=jnp.int32)
    keep_mask = (positions[:, None] > positions[None, :]) & (
        arc_of_row[:, None] == arc_of_row[None, :]
    )
    lower_part = jnp.where(keep_mask, arc_filter, jnp.zeros_like(arc_filter))
    mixed_part = lax.dot_general(design, lower_part, NT, preferred_element_type=jnp.float32)
    return (design.astype(jnp.float32) + mixed_part).astype(jnp.bfloat16)


def general_body(design, arc_filter, arc_of_row, terr_stored, block_order, directions):
    whitened = whiten(design, arc_filter, arc_of_row)
    own_width = whitened.shape[0]
    rows_block, terr_rows = (
        lax.all_gather(whitened, "col", axis=0, tiled=True),
        lax.all_gather(terr_stored, "col", axis=0, tiled=True),
    )
    cols_block = lax.all_gather(whitened, "row", axis=0, tiled=True)
    normal_tile = lax.dot_general(cols_block, rows_block, NT, preferred_element_type=jnp.float32)
    block_size = terr_rows.shape[1]
    span_rows = terr_rows.shape[0]
    group_count = span_rows // block_size
    row_index = lax.axis_index("row")
    col_index = lax.axis_index("col")
    local_order = block_order - row_index * group_count
    selector = (local_order[None, :] == jnp.arange(group_count, dtype=jnp.int32)[:, None]).astype(
        jnp.float32
    )
    stored = terr_rows.astype(jnp.float32).reshape(group_count, block_size, block_size)
    symmetric = jnp.triu(stored) + jnp.swapaxes(jnp.triu(stored, 1), 1, 2)
    ordered = jnp.einsum("qt,tab->qab", selector, symmetric, precision=HIGH).reshape(
        span_rows, block_size
    )
    own_rows = lax.dynamic_slice_in_dim(ordered, col_index * own_width, own_width, 0)
    positions = col_index * own_width + jnp.arange(own_width, dtype=jnp.int32)
    onehot = (
        (positions // block_size)[:, None] == jnp.arange(group_count, dtype=jnp.int32)[None, :]
    ).astype(jnp.float32)
    terr_added = (onehot[:, :, None] * own_rows[:, None, :]).reshape(own_width, span_rows)
    current = lax.dynamic_slice_in_dim(normal_tile, row_index * own_width, own_width, 0)
    normal_tile = lax.dynamic_update_slice_in_dim(
        normal_tile, current + terr_added, row_index * own_width, 0
    )
    tile_rows = normal_tile.shape[0]
    partial_sum = dot_high(normal_tile, lax.all_gather(directions, "col", axis=0, tiled=True))
    products = lax.psum_scatter(partial_sum, "row", scatter_dimension=0, tiled=True)
    normals = normal_tile.reshape(tile_rows // own_width, 1, own_width, span_rows)
    return (normals, products)


def xor(i, mask):
    return i + mask * (1 - 2 * ((i // mask) % 2))


def xor_all(i, mask, n):
    for m in masks_of(n):
        if mask & m:
            i = xor(i, m)
    return i


def split3(x):
    a = x.astype(jnp.bfloat16)
    rest = x - a.astype(jnp.float32)
    b = rest.astype(jnp.bfloat16)
    return a, b, (rest - b.astype(jnp.float32)).astype(jnp.bfloat16)


def wide3(x):
    return jnp.concatenate(split3(x), 1)


def fold3(x):
    n = x.shape[1] // 3
    return x[:, 2 * n :] + x[:, n : 2 * n] + x[:, :n]


def whiten_kernel(d_ref, dp_ref, f_ref, fp_ref, ar_ref, arp_ref, w_ref):
    b = pl.program_id(0)
    width = f_ref.shape[0]
    zero = jnp.zeros((width, width), jnp.float32)
    k = lax.broadcasted_iota(jnp.int32, (width, width), 0)
    j = lax.broadcasted_iota(jnp.int32, (width, width), 1)
    column = jnp.broadcast_to(ar_ref[...], (128, width)).T[:, :1]
    keep = (k > j) & (column == ar_ref[...])
    keep_prev = (column == arp_ref[...]) & (b > 0)
    here = jnp.where(keep, f_ref[...].astype(jnp.float32), zero).astype(jnp.bfloat16)
    prev = jnp.where(keep_prev, fp_ref[...].astype(jnp.float32), zero).astype(jnp.bfloat16)
    mixed = lax.dot_general(d_ref[...], here, NT, preferred_element_type=jnp.float32)
    mixed += lax.dot_general(dp_ref[...], prev, NT, preferred_element_type=jnp.float32)
    w_ref[...] = (d_ref[...].astype(jnp.float32) + mixed).astype(jnp.bfloat16)


def whiten_rows(design, arc_filter, arc_of_row):
    own, total = design.shape
    width = total // 4
    here = lambda b: (0, b)
    prev = lambda b: (0, jnp.maximum(b - 1, 0))
    row = arc_of_row.reshape(1, total)
    return pl.pallas_call(
        whiten_kernel,
        grid=(total // width,),
        in_specs=[
            pl.BlockSpec((own, width), here),
            pl.BlockSpec((own, width), prev),
            pl.BlockSpec((width, width), lambda b: (b, b)),
            pl.BlockSpec((width, width), lambda b: (b, jnp.maximum(b - 1, 0))),
            pl.BlockSpec((1, width), here),
            pl.BlockSpec((1, width), prev),
        ],
        out_specs=pl.BlockSpec((own, width), here),
        out_shape=jax.ShapeDtypeStruct((own, total), jnp.bfloat16),
        name="whiten",
        cost_estimate=pl.CostEstimate(
            flops=4 * own * total * width, bytes_accessed=8 * own * total, transcendentals=0
        ),
    )(design, design, arc_filter, arc_filter, row, row)


def masks_of(n):
    return [1 << i for i in range(n.bit_length() - 1)]


def exchange_kernel(n_row, n_col, parts, w_ref, t_ref, d_ref, *refs):
    rows_ref, up1, up2a, up2b, up3a, dn1, dn2a, dn2b, dn3b = refs[:9]
    terr_ref, edge_ref, side_ref, pre_ref, pre0_ref, pre1_ref, vout = refs[9:16]
    b_ref, b0_ref, b1_ref, a_ref, o_ref, got, acc, pack = refs[16:24]
    s_loc, s_a, s_o, s_ring, r_ring, s_row, r_row, s_terr, r_terr, s_v, r_v, s_e, r_e = refs[24:]
    r = lax.axis_index("row")
    c = lax.axis_index("col")
    own, width = w_ref.shape
    sub = own // parts
    zs = n_col // 2
    z, y = c // 2, c % 2
    place = z + y * (n_col - 1 - 2 * z)
    by_up = place % zs == 0
    by_down = place % zs == zs - 1
    inner = (place % zs > 0) & (place % zs < zs - 1)

    def col_at(p):
        side = p // zs
        return 2 * (p + side * (n_col - 1 - 2 * p)) + side

    nxt = col_at((place + 1) % n_col)
    prv = col_at((place + n_col - 1) % n_col)
    row_masks = masks_of(n_row)
    peers = [(r, nxt), (r, prv)]
    peers += [(xor(r, m), c) for m in row_masks] + [(r, xor(c, 1))]
    peers += [(r, 2 * xor_all(z, m, zs) + y) for m in range(1, zs)]
    barrier = pltpu.get_barrier_semaphore()
    for peer in peers:
        pl.semaphore_signal(barrier, inc=1, device_id=peer, device_id_type=MESH)
    pl.semaphore_wait(barrier, len(peers))

    def remote(src, dst, ssem, rsem, peer):
        return pltpu.make_async_remote_copy(
            src_ref=src, dst_ref=dst, send_sem=ssem, recv_sem=rsem, device_id=peer,
            device_id_type=MESH,
        )

    def piece(ref, j):
        return ref.at[pl.ds(j * sub, sub)]

    sends = []

    def start(copy):
        copy.start()
        sends.append(copy)

    half = parts // 2
    steps = 2 * parts + half
    ahead = 4

    def ring(s, way):
        one, two, three = ((up1, (up2a, up2b), up3a), (dn1, (dn2a, dn2b), dn3b))[way]
        j = s % parts
        if s < parts:
            src, dst = piece(w_ref, j), piece(one, j)
        elif s < 2 * parts:
            src, dst = piece(one, j), piece(two[j // half], j % half)
        else:
            src, dst = piece(two[way], j), piece(three, j)
        return remote(src, dst, s_ring.at[way, s], r_ring.at[way, s], (r, (nxt, prv)[way]))

    rings = [[ring(s, way) for way in range(2)] for s in range(steps)]
    for s in range(ahead):
        for way in range(2):
            start(rings[s][way])

    mine = pl.ds(pl.multiple_of(y * own, own), own)
    other = pl.ds(pl.multiple_of((1 - y) * own, own), own)
    load = pltpu.make_async_copy(w_ref, b_ref.at[mine], s_loc.at[0])
    load.start()

    far = n_col // 2
    h = t_ref.shape[1] // 2
    pairs = own // h // 2
    k = lax.broadcasted_iota(jnp.int32, (h, 2 * h), 0)
    lane = lax.broadcasted_iota(jnp.int32, (h, 2 * h), 1)
    line = lax.broadcasted_iota(jnp.int32, (16, 2 * h), 0)
    diagonals = jnp.zeros((16, 2 * h), jnp.float32)

    def stored(i):
        return t_ref[pl.ds(pl.multiple_of(i * h, h), h), :].astype(jnp.float32)

    for p in range(pairs):
        top, low = stored(2 * p + y), stored(2 * p + 1 + y)
        turned = pltpu.roll(jnp.concatenate([top, low], 0).T[h:], h, 1)
        pack[p * h : (p + 1) * h] = jnp.where(k <= lane, top, turned).astype(pack.dtype)
        row = jnp.sum(jnp.where(lane == k + h, low, 0.0), axis=0, keepdims=True)
        diagonals = jnp.where(line == p, row, diagonals)
    pack[pairs * h : (pairs + 1) * h] = stored(2 * pairs * (1 - y)).astype(pack.dtype)
    pack[(pairs + 1) * h :] = diagonals.astype(pack.dtype)
    keep_pack = pltpu.make_async_copy(pack, terr_ref.at[0], s_loc.at[8])
    keep_pack.start()

    def terr(k, way):
        src = pack if k == 1 else terr_ref.at[(n_col - k + 1) if way == 0 else k - 1]
        at = (n_col - k) if way == 0 else k
        return remote(src, terr_ref.at[at], s_terr.at[way, k - 1], r_terr.at[way, k - 1],
                      (r, (nxt, prv)[way]))

    terrs = {}
    for k in range(1, far + 1):
        terrs[k] = [terr(k, 0)] + ([terr(k, 1)] if k < far else [])
    for copy in terrs[1]:
        start(copy)
    edge = edge_ref.shape[0]
    edge_at = pl.ds(pl.multiple_of((1 - y) * (own - edge), edge), edge)
    edges = remote(d_ref.at[edge_at], edge_ref, s_e.at[0], r_e.at[0], (r, xor(c, 1)))
    start(edges)
    across = remote(w_ref, side_ref, s_e.at[1], r_e.at[1], (r, xor(c, 1)))

    @pl.when(inner)
    def _():
        across.start()

    order = []
    for mask in reversed(row_masks):
        for m in range(0, n_row, 2 * mask):
            order.append((m + mask, mask))

    def row_copy(key, j):
        m, mask = key
        n = order.index(key)
        src = w_ref if m == mask else rows_ref.at[m - mask]
        return remote(piece(src, j), piece(rows_ref.at[m], j), s_row.at[n, j], r_row.at[n, j],
                      (xor(r, mask), c))

    copies = {key: [row_copy(key, j) for j in range(parts)] for key in order}
    filled = {m: (m, mask) for m, mask in order}
    later = [key for key in order if key[0] != key[1]]
    waited = set()

    def row_wait(key, j):
        if (key, j) not in waited:
            copies[key][j].wait_recv()
            waited.add((key, j))

    load.wait()
    put = pltpu.make_async_copy(b_ref.at[mine], rows_ref.at[0], s_loc.at[1])
    put.start()
    dirs = wide3(d_ref[...])
    chunk = width // 8

    @pl.loop(0, 8)
    def _(t):
        span = pl.ds(pl.multiple_of(t * chunk, chunk), chunk)
        acc[span, :] = fold3(
            lax.dot_general(
                b_ref[mine, span], dirs, (((0,), (0,)), ((), ())),
                preferred_element_type=jnp.float32,
            )
        )

    levels = [((xor(r, m), c), (r // m) % 2) for m in row_masks] + [((r, xor(c, 1)), y)]
    n = len(levels)
    span = width
    offset = base = 0
    gives, keeps, spots = [], [], []
    for i, (peer, bit) in enumerate(levels):
        span //= 2
        give = pl.ds(pl.multiple_of(offset + (1 - bit) * span, span), span)
        offset = offset + bit * span
        keep = pl.ds(pl.multiple_of(offset, span), span)
        spot = pl.ds(base, span)
        base += span
        gives.append(remote(acc.at[give], got.at[spot], s_v.at[i], r_v.at[i], peer))
        keeps.append(keep)
        spots.append(spot)
    bit = span // zs
    at_out = pl.ds(pl.multiple_of(offset + z * bit, bit), bit)
    fans, backs = [], []
    for m in range(1, zs):
        zz = xor_all(z, m, zs)
        peer = (r, 2 * zz + y)
        give = pl.ds(pl.multiple_of(offset + zz * bit, bit), bit)
        spot = pl.ds(base + (m - 1) * bit, bit)
        at = n + 2 * m - 2
        fans.append(remote(acc.at[give], got.at[spot], s_v.at[at], r_v.at[at], peer))
        backs.append(
            remote(vout.at[at_out], vout.at[at_out], s_v.at[at + 1], r_v.at[at + 1], peer)
        )
    at = n + 2 * zs - 2
    wider = [
        remote(vout.at[keeps[i]], vout.at[keeps[i]], s_v.at[at + i], r_v.at[at + i], levels[i][0])
        for i in range(n)
    ]

    def finish(i):
        gives[i].wait()
        acc[keeps[i]] = acc[keeps[i]] + got[spots[i]]

    def fan_in():
        for copy in fans:
            copy.wait()
        mid = acc[pl.ds(pl.multiple_of(offset + z * bit, bit), bit)]
        for m in range(1, zs):
            mid = mid + got[base + (m - 1) * bit : base + m * bit]
        vout[at_out] = mid

    def each(copies, method):
        for copy in copies:
            getattr(copy, method)()

    todo = [lambda: gives[0].start()]
    for i in range(1, n):
        todo.append(lambda i=i: (finish(i - 1), gives[i].start()))
    todo.append(lambda: (finish(n - 1), each(fans, "start")))
    todo.append(lambda: (fan_in(), each(backs, "start")))
    todo.append(lambda: (each(backs, "wait"), wider[n - 1].start()))
    for i in range(n - 1, 0, -1):
        todo.append(lambda i=i: (wider[i].wait(), wider[i - 1].start()))
    todo.append(lambda: wider[0].wait())

    def v_next():
        if todo:
            todo.pop(0)()

    v_next()
    v_next()
    for key in order:
        if key[0] == key[1]:
            for copy in copies[key]:
                start(copy)

    wide = own // 128 * 128
    rest = 2 * own - wide
    near_at = pl.multiple_of(y * (2 * own - wide), 128)
    rest_at = pl.multiple_of((1 - y) * wide, 128)
    up_first = place % zs < zs // 2

    def fill(refs, b, at, n):
        size = own // len(refs)
        return [
            pltpu.make_async_copy(ref, b.at[pl.ds(at + i * size, size)], s_loc.at[n + i])
            for i, ref in enumerate(refs)
        ]

    def other_start():
        start_at = (1 - y) * own

        @pl.when(inner)
        def _():
            across.wait()
            each(fill([side_ref], b_ref, start_at, 2), "start")

        @pl.when(by_up)
        def _():
            each(fill([up1], b_ref, start_at, 2), "start")

        @pl.when(by_down)
        def _():
            each(fill([dn1], b_ref, start_at, 2), "start")

        @pl.when(place % 2 == 0)
        def _():
            each(fill([dn1], b0_ref, y * own, 3), "start")

        @pl.when(place % 2 == 1)
        def _():
            each(fill([up1], b0_ref, y * own, 3), "start")

    def second_start():
        @pl.when(up_first)
        def _():
            each(fill([up2a, up2b], b0_ref, (1 - y) * own, 4), "start")
            each(fill([dn2a, dn2b], b1_ref, 0, 6), "start")

        @pl.when(place % zs >= zs // 2)
        def _():
            each(fill([dn2a, dn2b], b0_ref, (1 - y) * own, 4), "start")
            each(fill([up2a, up2b], b1_ref, 0, 6), "start")

    def a_load(m):
        return pltpu.make_async_copy(rows_ref.at[m], a_ref.at[m], s_a.at[m])

    stores = []

    def dots(m, rows, width, into):
        n = len(stores)
        for store in stores[-2:]:
            store.wait()

        def store(t):
            return pltpu.make_async_copy(
                o_ref.at[t, :, pl.ds(0, width)], into(m + t), s_o.at[n + t]
            )

        @pl.loop(0, 2)
        def _(t):
            o_ref[t, :, :width] = lax.dot_general(
                a_ref[m + t], rows(), NT, preferred_element_type=jnp.float32
            )
            store(t).start()

        stores.extend([store(0), store(1)])

    def own_tile(m):
        for i in range(2):
            a_load(m + i).wait()
        if m == 0:
            each(fill([side_ref], b_ref, 0, 2), "wait")
        dots(m, lambda: b_ref[...], 2 * own, lambda m: pre_ref.at[m])

    def near_tile(m):
        if m == 0:
            each(fill([up1], b0_ref, 0, 3), "wait")
        span = pl.ds(near_at, wide)
        dots(m, lambda: b0_ref[span, :], wide, lambda m: pre0_ref.at[m, :, span])

    def rest_tile(m):
        if m == 0:
            each(fill([up2a, up2b], b0_ref, 0, 4), "wait")
        span = pl.ds(rest_at, rest)
        dots(m, lambda: b0_ref[span, :], rest, lambda m: pre0_ref.at[m, :, span])

    def side_tile(m):
        if m == 0:
            each(fill([up2a, up2b], b1_ref, 0, 6), "wait")
        at = pl.multiple_of(y * (own - wide), own - wide)
        dots(m, lambda: b1_ref[pl.ds(at, wide), :], wide, lambda m: pre1_ref.at[m])

    hop = 1
    lag = parts // 2
    v_at = [ahead + i * (ahead + 1) for i in range(5)] + [steps - 3, steps - 1]
    work = {}
    for m in range(0, n_row, 2):
        work.setdefault(parts + 1 + (lag + 1) * (m // 2), []).append((own_tile, m))
        work.setdefault(2 * parts - 3 + m // 2, []).append((near_tile, m))
        work.setdefault(2 * parts + m // 2, []).append((rest_tile, m))
        work.setdefault(2 * parts + 3 + m // 2, []).append((side_tile, m))
    for s in range(steps):
        for way in range(2):
            rings[s][way].wait_recv()
        if s in v_at:
            v_next()
        if s % 3 == 2 and hop <= far:
            for copy in terrs[hop]:
                copy.wait_recv()
            hop += 1
            if hop <= far:
                for copy in terrs[hop]:
                    start(copy)
        if s + ahead < steps:
            for way in range(2):
                start(rings[s + ahead][way])
        j = s - lag
        if 0 <= j < parts:
            for key in later:
                row_wait(filled[key[0] - key[1]], j)
                start(copies[key][j])
        if s == parts - 1:
            other_start()
            put.wait()
            a_load(0).start()
            for j in range(parts):
                row_wait(filled[1], j)
            a_load(1).start()
        if s == parts + lag - 1:
            for m in range(2, n_row):
                for j in range(parts):
                    row_wait(filled[m], j)
                a_load(m).start()
        if s == 2 * parts - 1:
            second_start()
        for do, m in work.get(s, []):
            do(m)
    while hop <= far:
        for copy in terrs[hop]:
            copy.wait_recv()
        hop += 1
        if hop <= far:
            for copy in terrs[hop]:
                start(copy)
    while todo:
        v_next()
    edges.wait_recv()
    keep_pack.wait()
    for store in stores[-2:]:
        store.wait()
    for copy in sends:
        copy.wait_send()


def exchange(n_row, n_col, whitened, terr_stored, directions):
    own, total = whitened.shape
    cols = directions.shape[1]
    block = terr_stored.shape[1]
    packed = ((2 * own // block // 2 + 1) * block // 2 + 16, block)
    parts = 12
    far = n_col // 2
    any_spec = pl.BlockSpec(memory_space=pl.ANY)
    vmem = pl.BlockSpec(memory_space=pltpu.VMEM)
    whole = jax.ShapeDtypeStruct((own, total), jnp.bfloat16)
    part = jax.ShapeDtypeStruct((own // 2, total), jnp.bfloat16)
    levels = 2 * n_row.bit_length() + n_col
    moves = n_row - 1
    dma = pltpu.SemaphoreType.DMA
    return pl.pallas_call(
        functools.partial(exchange_kernel, n_row, n_col, parts),
        in_specs=[any_spec, vmem, vmem],
        out_specs=[any_spec] * 15 + [vmem],
        out_shape=[
            jax.ShapeDtypeStruct((n_row, own, total), jnp.bfloat16),
            whole, part, part, part, whole, part, part, part,
            jax.ShapeDtypeStruct((n_col,) + packed, jnp.bfloat16),
            jax.ShapeDtypeStruct((block // 2, cols), jnp.float32),
            whole,
            jax.ShapeDtypeStruct((n_row, own, 2 * own), jnp.float32),
            jax.ShapeDtypeStruct((n_row, own, 2 * own), jnp.float32),
            jax.ShapeDtypeStruct((n_row, own, own // 128 * 128), jnp.float32),
            jax.ShapeDtypeStruct((total, cols), jnp.float32),
        ],
        scratch_shapes=[
            pltpu.VMEM((2 * own, total), jnp.bfloat16),
            pltpu.VMEM((2 * own, total), jnp.bfloat16),
            pltpu.VMEM((own, total), jnp.bfloat16),
            pltpu.VMEM((n_row, own, total), jnp.bfloat16),
            pltpu.VMEM((2, own, 2 * own), jnp.float32),
            pltpu.VMEM((total, cols), jnp.float32),
            pltpu.VMEM((total, cols), jnp.float32),
            pltpu.VMEM(packed, jnp.bfloat16),
            dma((9,)),
            dma((n_row,)),
            dma((4 * n_row,)),
            dma((2, 3 * parts)), dma((2, 3 * parts)),
            dma((moves, parts)), dma((moves, parts)),
            dma((2, far)), dma((2, far)),
            dma((levels,)), dma((levels,)),
            dma((2,)), dma((2,)),
        ],
        name="exchange",
        compiler_params=pltpu.CompilerParams(
            collective_id=0, has_side_effects=True, vmem_limit_bytes=VMEM_BYTES
        ),
        cost_estimate=pl.CostEstimate(
            flops=1000000, bytes_accessed=40 * own * total, transcendentals=0
        ),
    )(whitened, terr_stored, directions)


def carry_kernel(at, n_row, s_ref, order_ref, t_ref, w_ref, d_ref, e_ref, v_ref, *refs):
    pre_ref, pre0_ref, pre1_ref, p_ref, out_ref, inv_ref, q_ref, q1_ref, pull_sem, push_sem = refs
    own, span = q_ref.shape[1:]
    wide = q1_ref.shape[2]
    half = e_ref.shape[0]
    block = 2 * half
    per = own // half
    count = order_ref.shape[0]
    side = s_ref[at["side"]]
    pair = s_ref[at["pair"]]

    def pull(n):
        src = (pre_ref, pre0_ref, pre1_ref)[n // n_row].at[n % n_row]
        dst = q_ref.at[n] if n < 2 * n_row else q1_ref.at[n - 2 * n_row]
        return pltpu.make_async_copy(src, dst, pull_sem.at[n])

    def push(n):
        kind, m = n // n_row, n % n_row
        zz = s_ref[at["own"] + kind]
        column = zz * span if kind < 2 else zz * span + side * (span - wide)
        src = q_ref.at[n] if kind < 2 else q1_ref.at[m]
        return pltpu.make_async_copy(
            src,
            out_ref.at[
                pl.ds(pl.multiple_of(s_ref[at["rows"] + m] * own, own), own),
                pl.ds(pl.multiple_of(column, 128), span if kind < 2 else wide),
            ],
            push_sem.at[n],
        )

    total = 3 * n_row
    for n in range(total):
        pull(n).start()

    @pl.loop(0, count)
    def _(t):
        inv_ref[order_ref[t] - s_ref[at["first"]]] = t

    def pass_on(lo, hi):
        for n in range(lo, hi):
            pull(n).wait()
            push(n).start()

    size = v_ref.shape[0] // n_row
    for m in range(n_row):
        part = slice(m * size, (m + 1) * size)
        term = fold3(
            jnp.dot(w_ref[:, part], wide3(v_ref[part, :]), preferred_element_type=jnp.float32)
        )
        p_ref[...] = p_ref[...] + term if m else term
        pass_on(1 + 2 * m, 3 + 2 * m)
    pull(0).wait()
    k = lax.broadcasted_iota(jnp.int32, (block, block), 0)
    j = lax.broadcasted_iota(jnp.int32, (block, block), 1)

    pairs = per // 2
    zero = jnp.zeros((half, block), jnp.float32)
    upper = lax.broadcasted_iota(jnp.int32, (half, block), 0)
    lane = lax.broadcasted_iota(jnp.int32, (half, block), 1)
    line = lax.broadcasted_iota(jnp.int32, (16, block), 0)

    def symmetric(t):
        one, two = 2 * t // per, (2 * t + 1) // per
        p = 2 * t % per // 2
        slot = s_ref[at["spots"] + one]
        split = one != two

        def read(slot, first, n):
            return t_ref[slot, pl.ds(first, n), :].astype(jnp.float32)

        top = read(slot, pl.multiple_of(p * half, half), half)
        low = read(s_ref[at["spots"] + two], pairs * half, half)
        row = jnp.sum(
            jnp.where(line == p, read(slot, (pairs + 1) * half, 16), 0.0), axis=0, keepdims=True
        )
        turned = jnp.where((upper > lane) & (lane < half), top, 0.0)
        turned = jnp.where(split, zero, pltpu.roll(turned, half, 1))
        s = jnp.concatenate([top, jnp.where(split, low, zero)], 0)
        strict = jnp.where(k < j, s, 0.0) + jnp.concatenate([zero, turned], 0)
        diagonal = jnp.where(split | (k < half), s, row)
        return strict + strict.T + jnp.where(k == j, diagonal, 0.0)

    edge = e_ref[...]
    for q in range(span // block):
        lo = 2 * q

        @pl.when((lo + 1 >= side * per) & (lo < side * per + per))
        def _(q=q, lo=lo):
            sym = symmetric(inv_ref[pair + q])
            for h in range(2):
                i = lo + h - side * per

                @pl.when((i >= 0) & (i < per))
                def _():
                    mine = pl.ds(pl.multiple_of(i * half, half), half)
                    rows = sym[h * half : (h + 1) * half]
                    q_ref[0, mine, q * block : (q + 1) * block] += rows
                    other = i + 1 - 2 * h
                    inside = (other >= 0) & (other < per)
                    safe = jnp.minimum(jnp.maximum(other, 0), per - 1)
                    beside = d_ref[pl.ds(pl.multiple_of(safe * half, half), half), :]
                    beside = jnp.where(inside, beside, edge)
                    this = d_ref[mine, :]
                    near = jnp.concatenate([beside, this] if h else [this, beside], 0)
                    p_ref[mine, :] += fold3(
                        jnp.dot(
                            rows.astype(jnp.bfloat16), wide3(near),
                            preferred_element_type=jnp.float32,
                        )
                    )

    push(0).start()
    pass_on(1 + 2 * n_row, total)
    for n in range(total):
        push(n).wait()


def carry_job(at, scalars, order, terr_all, whitened, directions, edge, v, pres, out):
    own = whitened.shape[0]
    cols = directions.shape[1]
    n_row = pres[0].shape[0]
    vmem = pl.BlockSpec(memory_space=pltpu.VMEM)
    smem = pl.BlockSpec(memory_space=pltpu.SMEM)
    any_spec = pl.BlockSpec(memory_space=pl.ANY)
    return pl.pallas_call(
        functools.partial(carry_kernel, at, n_row),
        in_specs=[smem] * 2 + [vmem] * 5 + [any_spec] * 3,
        out_specs=[vmem, any_spec],
        out_shape=[jax.ShapeDtypeStruct((own, cols), jnp.float32), out],
        scratch_shapes=[
            pltpu.SMEM((order.shape[0],), jnp.int32),
            pltpu.VMEM((2 * n_row, own, 2 * own), jnp.float32),
            pltpu.VMEM((n_row, own, pres[2].shape[2]), jnp.float32),
            pltpu.SemaphoreType.DMA((3 * n_row,)),
            pltpu.SemaphoreType.DMA((3 * n_row,)),
        ],
        name="carry",
        compiler_params=pltpu.CompilerParams(vmem_limit_bytes=VMEM_BYTES),
        cost_estimate=pl.CostEstimate(
            flops=6 * own * whitened.shape[1] * cols, bytes_accessed=60000000, transcendentals=0
        ),
    )(scalars, order, terr_all, whitened, directions, edge, v, *pres)


def tile_kernel(parts, rows_at, s_ref, *refs):
    n = 1 + max(i for _, _, sources, _ in parts for pair in sources.values() for i, _ in pair)
    bufs = refs[:n]
    a_ref, _, o_hbm, b_ref, o_ref, sem, o_sem = refs[n:]
    i = pl.program_id(0)
    steps = pl.num_programs(0)
    own = a_ref.shape[1]
    half = own // 2
    span = b_ref.shape[1]

    def copy(p, k, y, h):
        spot, row = parts[p][2][k][h]
        return pltpu.make_async_copy(
            bufs[spot].at[pl.ds(row, half)],
            b_ref.at[p, pl.ds((2 * y + h) * half, half)],
            sem.at[p, 2 * y + h],
        )

    @pl.when(i == 0)
    def _():
        for p, (at, wants, sources, _) in enumerate(parts):
            for y in range(2):
                for h in range(2):
                    needed = wants(s_ref[at + 4], y, h)
                    for k in sources:

                        @pl.when((s_ref[at + 1 + y] == k) & needed)
                        def _():
                            copy(p, k, y, h).start()

    slot = i % 2

    def outs(i, slot):
        copies = []
        first = 0
        for p, (at, _, _, width) in enumerate(parts):
            copies.append(
                pltpu.make_async_copy(
                    o_ref.at[slot, :, pl.ds(first, width)],
                    o_hbm.at[
                        pl.ds(pl.multiple_of(s_ref[rows_at + i] * own, own), own),
                        pl.ds(pl.multiple_of(s_ref[at] * span + s_ref[at + 3], 128), width),
                    ],
                    o_sem.at[p, slot],
                )
            )
            first += width
        return copies

    @pl.when(i >= 2)
    def _():
        for out in outs(i - 2, slot):
            out.wait()

    first = 0
    for p, (at, wants, sources, width) in enumerate(parts):

        @pl.when(i == 0)
        def _():
            for y in range(2):
                for h in range(2):

                    @pl.when(wants(s_ref[at + 4], y, h))
                    def _():
                        copy(p, next(iter(sources)), y, h).wait()

        o_ref[slot, :, first : first + width] = lax.dot_general(
            a_ref[0],
            b_ref[p, pl.ds(pl.multiple_of(s_ref[at + 3], 128), width), :],
            NT,
            preferred_element_type=jnp.float32,
        )
        outs(i, slot)[p].start()
        first += width

    @pl.when(i == steps - 1)
    def _():
        for out in outs(i - 1, 1 - slot) + outs(i, slot):
            out.wait()


def tile_job(scalars, rows_at, parts, bufs, rows, out):
    count, own, total = rows.shape
    span = 2 * own
    any_spec = pl.BlockSpec(memory_space=pl.ANY)
    arrays, made = [], []
    for at, wants, cands, width in parts:
        sources = {}
        for k in cands:
            pair = []
            for array, row in bufs[k]:
                spot = [i for i, a in enumerate(arrays) if a is array]
                if not spot:
                    arrays.append(array)
                    spot = [len(arrays) - 1]
                pair.append((spot[0], row))
            sources[k] = pair
        made.append((at, wants, sources, width))
    columns = sum(width for *_, width in parts)
    return pl.pallas_call(
        functools.partial(tile_kernel, made, rows_at),
        grid_spec=pltpu.PrefetchScalarGridSpec(
            num_scalar_prefetch=1,
            grid=(count,),
            in_specs=[any_spec] * len(arrays)
            + [pl.BlockSpec((1, own, total), lambda i, s: (i, 0, 0)), any_spec],
            out_specs=any_spec,
            scratch_shapes=[
                pltpu.VMEM((len(parts), span, total), jnp.bfloat16),
                pltpu.VMEM((2, own, columns), jnp.float32),
                pltpu.SemaphoreType.DMA((len(parts), 4)),
                pltpu.SemaphoreType.DMA((len(parts), 2)),
            ],
        ),
        out_shape=jax.ShapeDtypeStruct(out.shape, out.dtype),
        input_output_aliases={2 + len(arrays): 0},
        compiler_params=pltpu.CompilerParams(vmem_limit_bytes=VMEM_BYTES),
        cost_estimate=pl.CostEstimate(
            flops=2 * count * own * columns * total,
            bytes_accessed=2 * count * own * total + 4 * count * own * columns,
            transcendentals=0,
        ),
    )(scalars, *arrays, rows, out)


def ring_body(n_row, n_col, design, arc_filter, arc_of_row, terr_stored, block_order, directions):
    own, _ = design.shape
    block = terr_stored.shape[1]
    r = lax.axis_index("row")
    c = lax.axis_index("col")
    zs = n_col // 2
    half = own // 2
    far = n_col // 2

    def hop(a, perm):
        return lax.ppermute(a, "col", perm)

    col_of = [2 * p if p < zs else 2 * (n_col - 1 - p) + 1 for p in range(n_col)]
    pos_of = [0] * n_col
    for p, col in enumerate(col_of):
        pos_of[col] = p
    forward = [(col_of[p], col_of[(p + 1) % n_col]) for p in range(n_col)]
    backward = [(d, s) for s, d in forward]

    whitened = whiten_rows(design, arc_filter, arc_of_row)
    rows, up1, up2a, up2b, up3a, dn1, dn2a, dn2b, dn3b, terr_all, edge, _, *pres, v = exchange(
        n_row, n_col, whitened, terr_stored, directions
    )
    last = far - 1
    bufs = {
        2: [(dn2a, 0), (dn2b, 0)],
        n_col - 2: [(up2a, 0), (up2b, 0)],
        1: [(dn1, 0), (dn1, half)],
        n_col - 1: [(up1, 0), (up1, half)],
    }
    upper = hop(up2b, forward)
    lower = hop(dn2a, backward)
    bufs[n_col - last] = [(up3a, 0), (upper, 0)]
    bufs[last] = [(lower, 0), (dn3b, 0)]
    bufs[far] = [(hop(up3a, forward), 0), (hop(dn3b, backward), 0)]

    per_pair = 2 * own // block

    wide = own // 128 * 128
    names = ["tile1b", "tile2a", "tile2b"]
    by_col, by_row, ks_of = [], [], {name: [set(), set()] for name in names}
    for col in range(n_col):
        z, y = col // 2, col % 2
        line = []
        for name in names:
            zz = z ^ 2 if name == "tile1b" else z ^ 3
            ks = [(pos_of[2 * zz + yy] - pos_of[col]) % n_col for yy in range(2)]
            near = [min(k, n_col - k) for k in ks]
            late = int(near[1] > near[0])
            soon = name[-1] == "a"
            lo = (2 * own - wide) * (1 - late) if soon else wide * late
            line += [zz, ks[0], ks[1], lo, late]
            ks_of[name][0].add(ks[1 - late])
            ks_of[name][1].add(ks[late])
        line += [(pos_of[s] - pos_of[col]) % n_col for s in range(n_col)]
        by_col.append(line + [y, z * per_pair, z, z ^ 1, z ^ 2])
    for row in range(n_row):
        by_row.append([row ^ m for m in range(n_row)] + [row * per_pair * zs])
    scalars = jnp.concatenate(
        [jnp.asarray(by_col, jnp.int32)[c], jnp.asarray(by_row, jnp.int32)[r]]
    )
    at = {"spots": 5 * len(names)}
    at["side"] = at["spots"] + n_col
    at["pair"] = at["side"] + 1
    at["own"] = at["side"] + 2
    at["rows"] = at["side"] + 5
    at["first"] = at["rows"] + n_row

    out = jax.ShapeDtypeStruct((n_row * own, n_col * own), jnp.float32)
    products, out = carry_job(
        at, scalars, block_order, terr_all, whitened, directions, edge,
        v, pres, out,
    )
    early = lambda late, y, h: late == 1 - y
    tail = lambda late, y, h: (late == y) | (h == 1 - y)
    parts = []
    for j, name in enumerate(names):
        soon, late = ks_of[name]
        if name[-1] == "a":
            parts.append((5 * j, early, sorted(soon), wide))
        else:
            parts.append((5 * j, tail, sorted(soon | late), 2 * own - wide))
    for some in (parts[:2], parts[2:]):
        out = tile_job(scalars, at["rows"], some, bufs, rows, out)
    return out.reshape(n_row, 1, own, n_col * own), products


def power_of_two(n):
    return n > 1 and n & (n - 1) == 0


def solution(mesh):
    n_row, n_col = mesh.shape["row"], mesh.shape["col"]

    def body(design, arc_filter, arc_of_row, terr_stored, block_order, directions):
        args = (design, arc_filter, arc_of_row, terr_stored, block_order, directions)
        own, block = design.shape[0], terr_stored.shape[1]
        aligned = n_row > 2 and own % 192 == 0 and own % block == block // 2 and (2 * own) % 128 == 0
        if power_of_two(n_row) and n_col == 8 and aligned:
            return ring_body(n_row, n_col, *args)
        return general_body(*args)

    return jax.shard_map(
        body,
        mesh=mesh,
        in_specs=(
            P(("row", "col"), None),
            P(),
            P(),
            P(("row", "col"), None),
            P("row"),
            P(("row", "col"), None),
        ),
        out_specs=(P(None, "col", None, "row"), P(("row", "col"), None)),
        check_vma=False,
    )
```

```python
import functools

import jax
import jax.numpy as jnp
from jax import lax
from jax.experimental import pallas as pl
from jax.experimental.pallas import tpu as pltpu
from jax.sharding import PartitionSpec as P


HIGH = lax.Precision.HIGHEST
NT = (((1,), (1,)), ((), ()))
MESH = pl.DeviceIdType.MESH
VMEM_BYTES = 67043328


def dot_high(a, b):
    return jnp.dot(a, b, precision=HIGH, preferred_element_type=jnp.float32)


def whiten(design, arc_filter, arc_of_row):
    positions = jnp.arange(arc_filter.shape[0], dtype=jnp.int32)
    keep_mask = (positions[:, None] > positions[None, :]) & (
        arc_of_row[:, None] == arc_of_row[None, :]
    )
    lower_part = jnp.where(keep_mask, arc_filter, jnp.zeros_like(arc_filter))
    mixed_part = lax.dot_general(design, lower_part, NT, preferred_element_type=jnp.float32)
    return (design.astype(jnp.float32) + mixed_part).astype(jnp.bfloat16)


def general_body(design, arc_filter, arc_of_row, terr_stored, block_order, directions):
    whitened = whiten(design, arc_filter, arc_of_row)
    own_width = whitened.shape[0]
    rows_block, terr_rows = (
        lax.all_gather(whitened, "col", axis=0, tiled=True),
        lax.all_gather(terr_stored, "col", axis=0, tiled=True),
    )
    cols_block = lax.all_gather(whitened, "row", axis=0, tiled=True)
    normal_tile = lax.dot_general(cols_block, rows_block, NT, preferred_element_type=jnp.float32)
    block_size = terr_rows.shape[1]
    span_rows = terr_rows.shape[0]
    group_count = span_rows // block_size
    row_index = lax.axis_index("row")
    col_index = lax.axis_index("col")
    local_order = block_order - row_index * group_count
    selector = (local_order[None, :] == jnp.arange(group_count, dtype=jnp.int32)[:, None]).astype(
        jnp.float32
    )
    stored = terr_rows.astype(jnp.float32).reshape(group_count, block_size, block_size)
    symmetric = jnp.triu(stored) + jnp.swapaxes(jnp.triu(stored, 1), 1, 2)
    ordered = jnp.einsum("qt,tab->qab", selector, symmetric, precision=HIGH).reshape(
        span_rows, block_size
    )
    own_rows = lax.dynamic_slice_in_dim(ordered, col_index * own_width, own_width, 0)
    positions = col_index * own_width + jnp.arange(own_width, dtype=jnp.int32)
    onehot = (
        (positions // block_size)[:, None] == jnp.arange(group_count, dtype=jnp.int32)[None, :]
    ).astype(jnp.float32)
    terr_added = (onehot[:, :, None] * own_rows[:, None, :]).reshape(own_width, span_rows)
    current = lax.dynamic_slice_in_dim(normal_tile, row_index * own_width, own_width, 0)
    normal_tile = lax.dynamic_update_slice_in_dim(
        normal_tile, current + terr_added, row_index * own_width, 0
    )
    tile_rows = normal_tile.shape[0]
    partial_sum = dot_high(normal_tile, lax.all_gather(directions, "col", axis=0, tiled=True))
    products = lax.psum_scatter(partial_sum, "row", scatter_dimension=0, tiled=True)
    normals = normal_tile.reshape(tile_rows // own_width, 1, own_width, span_rows)
    return (normals, products)


def xor(i, mask):
    return i + mask * (1 - 2 * ((i // mask) % 2))


def xor_all(i, mask, n):
    for m in masks_of(n):
        if mask & m:
            i = xor(i, m)
    return i


def split3(x):
    a = x.astype(jnp.bfloat16)
    rest = x - a.astype(jnp.float32)
    b = rest.astype(jnp.bfloat16)
    return a, b, (rest - b.astype(jnp.float32)).astype(jnp.bfloat16)


def wide3(x):
    return jnp.concatenate(split3(x), 1)


def fold3(x):
    n = x.shape[1] // 3
    return x[:, 2 * n :] + x[:, n : 2 * n] + x[:, :n]


def whiten_kernel(d_ref, f_ref, fp_ref, ar_ref, arp_ref, w_ref):
    b = pl.program_id(0)
    width = f_ref.shape[0]
    own = d_ref[:, pl.ds(pl.multiple_of(b * width, width), width)]
    before = d_ref[:, pl.ds(pl.multiple_of(jnp.maximum(b - 1, 0) * width, width), width)]
    zero = jnp.zeros((width, width), jnp.float32)
    k = lax.broadcasted_iota(jnp.int32, (width, width), 0)
    j = lax.broadcasted_iota(jnp.int32, (width, width), 1)
    column = jnp.broadcast_to(ar_ref[...], (128, width)).T[:, :1]
    keep = (k > j) & (column == ar_ref[...])
    keep_prev = (column == arp_ref[...]) & (b > 0)
    here = jnp.where(keep, f_ref[...].astype(jnp.float32), zero).astype(jnp.bfloat16)
    prev = jnp.where(keep_prev, fp_ref[...].astype(jnp.float32), zero).astype(jnp.bfloat16)
    mixed = lax.dot_general(own, here, NT, preferred_element_type=jnp.float32)
    mixed += lax.dot_general(before, prev, NT, preferred_element_type=jnp.float32)
    w_ref[...] = (own.astype(jnp.float32) + mixed).astype(jnp.bfloat16)


def whiten_rows(design, arc_filter, arc_of_row):
    own, total = design.shape
    width = total // 4
    here = lambda b: (0, b)
    prev = lambda b: (0, jnp.maximum(b - 1, 0))
    row = arc_of_row.reshape(1, total)
    return pl.pallas_call(
        whiten_kernel,
        grid=(total // width,),
        in_specs=[
            pl.BlockSpec((own, total), lambda b: (0, 0)),
            pl.BlockSpec((width, width), lambda b: (b, b)),
            pl.BlockSpec((width, width), lambda b: (b, jnp.maximum(b - 1, 0))),
            pl.BlockSpec((1, width), here),
            pl.BlockSpec((1, width), prev),
        ],
        out_specs=pl.BlockSpec((own, width), here),
        out_shape=jax.ShapeDtypeStruct((own, total), jnp.bfloat16),
        name="whiten",
        cost_estimate=pl.CostEstimate(
            flops=4 * own * total * width, bytes_accessed=8 * own * total, transcendentals=0
        ),
    )(design, arc_filter, arc_filter, row, row)


def masks_of(n):
    return [1 << i for i in range(n.bit_length() - 1)]


def exchange_kernel(n_row, n_col, parts, w_ref, t_ref, d_ref, *refs):
    rows_ref, up1, up2a, up2b, up3a, dn1, dn2a, dn2b, dn3b = refs[:9]
    terr_ref, edge_ref, side_ref, pre_ref, pre0_ref, pre1_ref, vout = refs[9:16]
    b_ref, b0_ref, b1_ref, a_ref, o_ref, got, acc, pack = refs[16:24]
    s_loc, s_a, s_o, s_ring, r_ring, s_row, r_row, s_terr, r_terr, s_v, r_v, s_e, r_e = refs[24:]
    r = lax.axis_index("row")
    c = lax.axis_index("col")
    own, width = w_ref.shape
    sub = own // parts
    zs = n_col // 2
    z, y = c // 2, c % 2
    place = z + y * (n_col - 1 - 2 * z)
    by_up = place % zs == 0
    by_down = place % zs == zs - 1
    inner = (place % zs > 0) & (place % zs < zs - 1)

    def col_at(p):
        side = p // zs
        return 2 * (p + side * (n_col - 1 - 2 * p)) + side

    nxt = col_at((place + 1) % n_col)
    prv = col_at((place + n_col - 1) % n_col)
    row_masks = masks_of(n_row)
    peers = [(r, nxt), (r, prv)]
    peers += [(xor(r, m), c) for m in row_masks] + [(r, xor(c, 1))]
    peers += [(r, 2 * xor_all(z, m, zs) + y) for m in range(1, zs)]
    barrier = pltpu.get_barrier_semaphore()
    for peer in peers:
        pl.semaphore_signal(barrier, inc=1, device_id=peer, device_id_type=MESH)
    pl.semaphore_wait(barrier, len(peers))

    def remote(src, dst, ssem, rsem, peer):
        return pltpu.make_async_remote_copy(
            src_ref=src, dst_ref=dst, send_sem=ssem, recv_sem=rsem, device_id=peer,
            device_id_type=MESH,
        )

    def piece(ref, j):
        return ref.at[pl.ds(j * sub, sub)]

    sends = []

    def start(copy):
        copy.start()
        sends.append(copy)

    half = parts // 2
    steps = 2 * parts + half
    ahead = 4

    def ring(s, way):
        one, two, three = ((up1, (up2a, up2b), up3a), (dn1, (dn2a, dn2b), dn3b))[way]
        j = s % parts
        if s < parts:
            src, dst = piece(w_ref, j), piece(one, j)
        elif s < 2 * parts:
            src, dst = piece(one, j), piece(two[j // half], j % half)
        else:
            src, dst = piece(two[way], j), piece(three, j)
        return remote(src, dst, s_ring.at[way, s], r_ring.at[way, s], (r, (nxt, prv)[way]))

    rings = [[ring(s, way) for way in range(2)] for s in range(steps)]
    for s in range(ahead):
        for way in range(2):
            start(rings[s][way])

    mine = pl.ds(pl.multiple_of(y * own, own), own)
    other = pl.ds(pl.multiple_of((1 - y) * own, own), own)
    load = pltpu.make_async_copy(w_ref, b_ref.at[mine], s_loc.at[0])
    load.start()

    far = n_col // 2
    h = t_ref.shape[1] // 2
    pairs = own // h // 2
    k = lax.broadcasted_iota(jnp.int32, (h, 2 * h), 0)
    lane = lax.broadcasted_iota(jnp.int32, (h, 2 * h), 1)
    line = lax.broadcasted_iota(jnp.int32, (16, 2 * h), 0)
    diagonals = jnp.zeros((16, 2 * h), jnp.float32)

    def stored(i):
        return t_ref[pl.ds(pl.multiple_of(i * h, h), h), :].astype(jnp.float32)

    for p in range(pairs):
        top, low = stored(2 * p + y), stored(2 * p + 1 + y)
        turned = pltpu.roll(jnp.concatenate([top, low], 0).T[h:], h, 1)
        pack[p * h : (p + 1) * h] = jnp.where(k <= lane, top, turned).astype(pack.dtype)
        row = jnp.sum(jnp.where(lane == k + h, low, 0.0), axis=0, keepdims=True)
        diagonals = jnp.where(line == p, row, diagonals)
    pack[pairs * h : (pairs + 1) * h] = stored(2 * pairs * (1 - y)).astype(pack.dtype)
    pack[(pairs + 1) * h :] = diagonals.astype(pack.dtype)
    keep_pack = pltpu.make_async_copy(pack, terr_ref.at[0], s_loc.at[8])
    keep_pack.start()

    def terr(k, way):
        src = pack if k == 1 else terr_ref.at[(n_col - k + 1) if way == 0 else k - 1]
        at = (n_col - k) if way == 0 else k
        return remote(src, terr_ref.at[at], s_terr.at[way, k - 1], r_terr.at[way, k - 1],
                      (r, (nxt, prv)[way]))

    terrs = {}
    for k in range(1, far + 1):
        terrs[k] = [terr(k, 0)] + ([terr(k, 1)] if k < far else [])
    for copy in terrs[1]:
        start(copy)
    edge = edge_ref.shape[0]
    edge_at = pl.ds(pl.multiple_of((1 - y) * (own - edge), edge), edge)
    edges = remote(d_ref.at[edge_at], edge_ref, s_e.at[0], r_e.at[0], (r, xor(c, 1)))
    start(edges)
    across = remote(w_ref, side_ref, s_e.at[1], r_e.at[1], (r, xor(c, 1)))

    @pl.when(inner)
    def _():
        across.start()

    order = []
    for mask in reversed(row_masks):
        for m in range(0, n_row, 2 * mask):
            order.append((m + mask, mask))

    def row_copy(key, j):
        m, mask = key
        n = order.index(key)
        src = w_ref if m == mask else rows_ref.at[m - mask]
        return remote(piece(src, j), piece(rows_ref.at[m], j), s_row.at[n, j], r_row.at[n, j],
                      (xor(r, mask), c))

    copies = {key: [row_copy(key, j) for j in range(parts)] for key in order}
    filled = {m: (m, mask) for m, mask in order}
    later = [key for key in order if key[0] != key[1]]
    waited = set()

    def row_wait(key, j):
        if (key, j) not in waited:
            copies[key][j].wait_recv()
            waited.add((key, j))

    load.wait()
    put = pltpu.make_async_copy(b_ref.at[mine], rows_ref.at[0], s_loc.at[1])
    put.start()
    dirs = wide3(d_ref[...])
    chunk = width // 8

    @pl.loop(0, 8)
    def _(t):
        span = pl.ds(pl.multiple_of(t * chunk, chunk), chunk)
        acc[span, :] = fold3(
            lax.dot_general(
                b_ref[mine, span], dirs, (((0,), (0,)), ((), ())),
                preferred_element_type=jnp.float32,
            )
        )

    levels = [((xor(r, m), c), (r // m) % 2) for m in row_masks] + [((r, xor(c, 1)), y)]
    n = len(levels)
    span = width
    offset = base = 0
    gives, keeps, spots = [], [], []
    for i, (peer, bit) in enumerate(levels):
        span //= 2
        give = pl.ds(pl.multiple_of(offset + (1 - bit) * span, span), span)
        offset = offset + bit * span
        keep = pl.ds(pl.multiple_of(offset, span), span)
        spot = pl.ds(base, span)
        base += span
        gives.append(remote(acc.at[give], got.at[spot], s_v.at[i], r_v.at[i], peer))
        keeps.append(keep)
        spots.append(spot)
    bit = span // zs
    at_out = pl.ds(pl.multiple_of(offset + z * bit, bit), bit)
    fans, backs = [], []
    for m in range(1, zs):
        zz = xor_all(z, m, zs)
        peer = (r, 2 * zz + y)
        give = pl.ds(pl.multiple_of(offset + zz * bit, bit), bit)
        spot = pl.ds(base + (m - 1) * bit, bit)
        at = n + 2 * m - 2
        fans.append(remote(acc.at[give], got.at[spot], s_v.at[at], r_v.at[at], peer))
        backs.append(
            remote(vout.at[at_out], vout.at[at_out], s_v.at[at + 1], r_v.at[at + 1], peer)
        )
    at = n + 2 * zs - 2
    wider = [
        remote(vout.at[keeps[i]], vout.at[keeps[i]], s_v.at[at + i], r_v.at[at + i], levels[i][0])
        for i in range(n)
    ]

    def finish(i):
        gives[i].wait()
        acc[keeps[i]] = acc[keeps[i]] + got[spots[i]]

    def fan_in():
        for copy in fans:
            copy.wait()
        mid = acc[pl.ds(pl.multiple_of(offset + z * bit, bit), bit)]
        for m in range(1, zs):
            mid = mid + got[base + (m - 1) * bit : base + m * bit]
        vout[at_out] = mid

    def each(copies, method):
        for copy in copies:
            getattr(copy, method)()

    todo = [lambda: gives[0].start()]
    for i in range(1, n):
        todo.append(lambda i=i: (finish(i - 1), gives[i].start()))
    todo.append(lambda: (finish(n - 1), each(fans, "start")))
    todo.append(lambda: (fan_in(), each(backs, "start")))
    todo.append(lambda: (each(backs, "wait"), wider[n - 1].start()))
    for i in range(n - 1, 0, -1):
        todo.append(lambda i=i: (wider[i].wait(), wider[i - 1].start()))
    todo.append(lambda: wider[0].wait())

    def v_next():
        if todo:
            todo.pop(0)()

    v_next()
    v_next()
    for key in order:
        if key[0] == key[1]:
            for copy in copies[key]:
                start(copy)

    wide = own // 128 * 128
    rest = 2 * own - wide
    near_at = pl.multiple_of(y * (2 * own - wide), 128)
    rest_at = pl.multiple_of((1 - y) * wide, 128)
    up_first = place % zs < zs // 2

    def fill(refs, b, at, n):
        size = own // len(refs)
        return [
            pltpu.make_async_copy(ref, b.at[pl.ds(at + i * size, size)], s_loc.at[n + i])
            for i, ref in enumerate(refs)
        ]

    def other_start():
        start_at = (1 - y) * own

        @pl.when(inner)
        def _():
            across.wait()
            each(fill([side_ref], b_ref, start_at, 2), "start")

        @pl.when(by_up)
        def _():
            each(fill([up1], b_ref, start_at, 2), "start")

        @pl.when(by_down)
        def _():
            each(fill([dn1], b_ref, start_at, 2), "start")

        @pl.when(place % 2 == 0)
        def _():
            each(fill([dn1], b0_ref, y * own, 3), "start")

        @pl.when(place % 2 == 1)
        def _():
            each(fill([up1], b0_ref, y * own, 3), "start")

    def second_start():
        @pl.when(up_first)
        def _():
            each(fill([up2a, up2b], b0_ref, (1 - y) * own, 4), "start")
            each(fill([dn2a, dn2b], b1_ref, 0, 6), "start")

        @pl.when(place % zs >= zs // 2)
        def _():
            each(fill([dn2a, dn2b], b0_ref, (1 - y) * own, 4), "start")
            each(fill([up2a, up2b], b1_ref, 0, 6), "start")

    def a_load(m):
        return pltpu.make_async_copy(rows_ref.at[m], a_ref.at[m], s_a.at[m])

    stores = []

    def dots(m, rows, width, into):
        n = len(stores)
        for store in stores[-2:]:
            store.wait()

        def store(t):
            return pltpu.make_async_copy(
                o_ref.at[t, :, pl.ds(0, width)], into(m + t), s_o.at[n + t]
            )

        @pl.loop(0, 2)
        def _(t):
            o_ref[t, :, :width] = lax.dot_general(
                a_ref[m + t], rows(), NT, preferred_element_type=jnp.float32
            )
            store(t).start()

        stores.extend([store(0), store(1)])

    def own_tile(m):
        for i in range(2):
            a_load(m + i).wait()
        if m == 0:
            each(fill([side_ref], b_ref, 0, 2), "wait")
        dots(m, lambda: b_ref[...], 2 * own, lambda m: pre_ref.at[m])

    def near_tile(m):
        if m == 0:
            each(fill([up1], b0_ref, 0, 3), "wait")
        span = pl.ds(near_at, wide)
        dots(m, lambda: b0_ref[span, :], wide, lambda m: pre0_ref.at[m, :, span])

    def rest_tile(m):
        if m == 0:
            each(fill([up2a, up2b], b0_ref, 0, 4), "wait")
        span = pl.ds(rest_at, rest)
        dots(m, lambda: b0_ref[span, :], rest, lambda m: pre0_ref.at[m, :, span])

    def side_tile(m):
        if m == 0:
            each(fill([up2a, up2b], b1_ref, 0, 6), "wait")
        at = pl.multiple_of(y * (own - wide), own - wide)
        dots(m, lambda: b1_ref[pl.ds(at, wide), :], wide, lambda m: pre1_ref.at[m])

    hop = 1
    lag = parts // 2
    v_at = [ahead + i * (ahead + 1) for i in range(5)] + [steps - 3, steps - 1]
    work = {}
    for m in range(0, n_row, 2):
        work.setdefault(parts + 1 + (lag + 1) * (m // 2), []).append((own_tile, m))
        work.setdefault(2 * parts - 3 + m // 2, []).append((near_tile, m))
        work.setdefault(2 * parts + m // 2, []).append((rest_tile, m))
        work.setdefault(2 * parts + 3 + m // 2, []).append((side_tile, m))
    for s in range(steps):
        for way in range(2):
            rings[s][way].wait_recv()
        if s in v_at:
            v_next()
        if s % 3 == 2 and hop <= far:
            for copy in terrs[hop]:
                copy.wait_recv()
            hop += 1
            if hop <= far:
                for copy in terrs[hop]:
                    start(copy)
        if s + ahead < steps:
            for way in range(2):
                start(rings[s + ahead][way])
        j = s - lag
        if 0 <= j < parts:
            for key in later:
                row_wait(filled[key[0] - key[1]], j)
                start(copies[key][j])
        if s == parts - 1:
            other_start()
            put.wait()
            a_load(0).start()
            for j in range(parts):
                row_wait(filled[1], j)
            a_load(1).start()
        if s == parts + lag - 1:
            for m in range(2, n_row):
                for j in range(parts):
                    row_wait(filled[m], j)
                a_load(m).start()
        if s == 2 * parts - 1:
            second_start()
        for do, m in work.get(s, []):
            do(m)
    while hop <= far:
        for copy in terrs[hop]:
            copy.wait_recv()
        hop += 1
        if hop <= far:
            for copy in terrs[hop]:
                start(copy)
    while todo:
        v_next()
    edges.wait_recv()
    keep_pack.wait()
    for store in stores[-2:]:
        store.wait()
    for copy in sends:
        copy.wait_send()


def exchange(n_row, n_col, whitened, terr_stored, directions):
    own, total = whitened.shape
    cols = directions.shape[1]
    block = terr_stored.shape[1]
    packed = ((2 * own // block // 2 + 1) * block // 2 + 16, block)
    parts = 12
    far = n_col // 2
    any_spec = pl.BlockSpec(memory_space=pl.ANY)
    vmem = pl.BlockSpec(memory_space=pltpu.VMEM)
    whole = jax.ShapeDtypeStruct((own, total), jnp.bfloat16)
    part = jax.ShapeDtypeStruct((own // 2, total), jnp.bfloat16)
    levels = 2 * n_row.bit_length() + n_col
    moves = n_row - 1
    dma = pltpu.SemaphoreType.DMA
    return pl.pallas_call(
        functools.partial(exchange_kernel, n_row, n_col, parts),
        in_specs=[any_spec, vmem, vmem],
        out_specs=[any_spec] * 15 + [vmem],
        out_shape=[
            jax.ShapeDtypeStruct((n_row, own, total), jnp.bfloat16),
            whole, part, part, part, whole, part, part, part,
            jax.ShapeDtypeStruct((n_col,) + packed, jnp.bfloat16),
            jax.ShapeDtypeStruct((block // 2, cols), jnp.float32),
            whole,
            jax.ShapeDtypeStruct((n_row, own, 2 * own), jnp.float32),
            jax.ShapeDtypeStruct((n_row, own, 2 * own), jnp.float32),
            jax.ShapeDtypeStruct((n_row, own, own // 128 * 128), jnp.float32),
            jax.ShapeDtypeStruct((total, cols), jnp.float32),
        ],
        scratch_shapes=[
            pltpu.VMEM((2 * own, total), jnp.bfloat16),
            pltpu.VMEM((2 * own, total), jnp.bfloat16),
            pltpu.VMEM((own, total), jnp.bfloat16),
            pltpu.VMEM((n_row, own, total), jnp.bfloat16),
            pltpu.VMEM((2, own, 2 * own), jnp.float32),
            pltpu.VMEM((total, cols), jnp.float32),
            pltpu.VMEM((total, cols), jnp.float32),
            pltpu.VMEM(packed, jnp.bfloat16),
            dma((9,)),
            dma((n_row,)),
            dma((4 * n_row,)),
            dma((2, 3 * parts)), dma((2, 3 * parts)),
            dma((moves, parts)), dma((moves, parts)),
            dma((2, far)), dma((2, far)),
            dma((levels,)), dma((levels,)),
            dma((2,)), dma((2,)),
        ],
        name="exchange",
        compiler_params=pltpu.CompilerParams(
            collective_id=0, has_side_effects=True, vmem_limit_bytes=VMEM_BYTES
        ),
        cost_estimate=pl.CostEstimate(
            flops=1000000, bytes_accessed=40 * own * total, transcendentals=0
        ),
    )(whitened, terr_stored, directions)


def carry_kernel(at, n_row, s_ref, order_ref, t_ref, w_ref, d_ref, e_ref, v_ref, *refs):
    pre_ref, pre0_ref, pre1_ref, p_ref, out_ref, inv_ref, q_ref, q1_ref, pull_sem, push_sem = refs
    own, span = q_ref.shape[1:]
    wide = q1_ref.shape[2]
    half = e_ref.shape[0]
    block = 2 * half
    per = own // half
    count = order_ref.shape[0]
    side = s_ref[at["side"]]
    pair = s_ref[at["pair"]]

    def pull(n):
        src = (pre_ref, pre0_ref, pre1_ref)[n // n_row].at[n % n_row]
        dst = q_ref.at[n] if n < 2 * n_row else q1_ref.at[n - 2 * n_row]
        return pltpu.make_async_copy(src, dst, pull_sem.at[n])

    def push(n):
        kind, m = n // n_row, n % n_row
        zz = s_ref[at["own"] + kind]
        column = zz * span if kind < 2 else zz * span + side * (span - wide)
        src = q_ref.at[n] if kind < 2 else q1_ref.at[m]
        return pltpu.make_async_copy(
            src,
            out_ref.at[
                pl.ds(pl.multiple_of(s_ref[at["rows"] + m] * own, own), own),
                pl.ds(pl.multiple_of(column, 128), span if kind < 2 else wide),
            ],
            push_sem.at[n],
        )

    total = 3 * n_row
    for n in range(total):
        pull(n).start()

    @pl.loop(0, count)
    def _(t):
        inv_ref[order_ref[t] - s_ref[at["first"]]] = t

    def pass_on(lo, hi):
        for n in range(lo, hi):
            pull(n).wait()
            push(n).start()

    size = v_ref.shape[0] // n_row
    for m in range(n_row):
        part = slice(m * size, (m + 1) * size)
        term = fold3(
            jnp.dot(w_ref[:, part], wide3(v_ref[part, :]), preferred_element_type=jnp.float32)
        )
        p_ref[...] = p_ref[...] + term if m else term
        pass_on(1 + 2 * m, 3 + 2 * m)
    pull(0).wait()
    k = lax.broadcasted_iota(jnp.int32, (block, block), 0)
    j = lax.broadcasted_iota(jnp.int32, (block, block), 1)

    pairs = per // 2
    zero = jnp.zeros((half, block), jnp.float32)
    upper = lax.broadcasted_iota(jnp.int32, (half, block), 0)
    lane = lax.broadcasted_iota(jnp.int32, (half, block), 1)
    line = lax.broadcasted_iota(jnp.int32, (16, block), 0)

    def symmetric(t):
        one, two = 2 * t // per, (2 * t + 1) // per
        p = 2 * t % per // 2
        slot = s_ref[at["spots"] + one]
        split = one != two

        def read(slot, first, n):
            return t_ref[slot, pl.ds(first, n), :].astype(jnp.float32)

        top = read(slot, pl.multiple_of(p * half, half), half)
        low = read(s_ref[at["spots"] + two], pairs * half, half)
        row = jnp.sum(
            jnp.where(line == p, read(slot, (pairs + 1) * half, 16), 0.0), axis=0, keepdims=True
        )
        turned = jnp.where((upper > lane) & (lane < half), top, 0.0)
        turned = jnp.where(split, zero, pltpu.roll(turned, half, 1))
        s = jnp.concatenate([top, jnp.where(split, low, zero)], 0)
        strict = jnp.where(k < j, s, 0.0) + jnp.concatenate([zero, turned], 0)
        diagonal = jnp.where(split | (k < half), s, row)
        return strict + strict.T + jnp.where(k == j, diagonal, 0.0)

    edge = e_ref[...]
    for q in range(span // block):
        lo = 2 * q

        @pl.when((lo + 1 >= side * per) & (lo < side * per + per))
        def _(q=q, lo=lo):
            sym = symmetric(inv_ref[pair + q])
            for h in range(2):
                i = lo + h - side * per

                @pl.when((i >= 0) & (i < per))
                def _():
                    mine = pl.ds(pl.multiple_of(i * half, half), half)
                    rows = sym[h * half : (h + 1) * half]
                    q_ref[0, mine, q * block : (q + 1) * block] += rows
                    other = i + 1 - 2 * h
                    inside = (other >= 0) & (other < per)
                    safe = jnp.minimum(jnp.maximum(other, 0), per - 1)
                    beside = d_ref[pl.ds(pl.multiple_of(safe * half, half), half), :]
                    beside = jnp.where(inside, beside, edge)
                    this = d_ref[mine, :]
                    near = jnp.concatenate([beside, this] if h else [this, beside], 0)
                    p_ref[mine, :] += fold3(
                        jnp.dot(
                            rows.astype(jnp.bfloat16), wide3(near),
                            preferred_element_type=jnp.float32,
                        )
                    )

    push(0).start()
    pass_on(1 + 2 * n_row, total)
    for n in range(total):
        push(n).wait()


def carry_job(at, scalars, order, terr_all, whitened, directions, edge, v, pres, out):
    own = whitened.shape[0]
    cols = directions.shape[1]
    n_row = pres[0].shape[0]
    vmem = pl.BlockSpec(memory_space=pltpu.VMEM)
    smem = pl.BlockSpec(memory_space=pltpu.SMEM)
    any_spec = pl.BlockSpec(memory_space=pl.ANY)
    return pl.pallas_call(
        functools.partial(carry_kernel, at, n_row),
        in_specs=[smem] * 2 + [vmem] * 5 + [any_spec] * 3,
        out_specs=[vmem, any_spec],
        out_shape=[jax.ShapeDtypeStruct((own, cols), jnp.float32), out],
        scratch_shapes=[
            pltpu.SMEM((order.shape[0],), jnp.int32),
            pltpu.VMEM((2 * n_row, own, 2 * own), jnp.float32),
            pltpu.VMEM((n_row, own, pres[2].shape[2]), jnp.float32),
            pltpu.SemaphoreType.DMA((3 * n_row,)),
            pltpu.SemaphoreType.DMA((3 * n_row,)),
        ],
        name="carry",
        compiler_params=pltpu.CompilerParams(vmem_limit_bytes=VMEM_BYTES),
        cost_estimate=pl.CostEstimate(
            flops=6 * own * whitened.shape[1] * cols, bytes_accessed=60000000, transcendentals=0
        ),
    )(scalars, order, terr_all, whitened, directions, edge, v, *pres)


def tile_kernel(parts, rows_at, s_ref, *refs):
    n = 1 + max(i for _, _, sources, _ in parts for pair in sources.values() for i, _ in pair)
    bufs = refs[:n]
    a_ref, _, o_hbm, b_ref, o_ref, sem, o_sem = refs[n:]
    i = pl.program_id(0)
    steps = pl.num_programs(0)
    own = a_ref.shape[1]
    half = own // 2
    span = b_ref.shape[1]

    def copy(p, k, y, h):
        spot, row = parts[p][2][k][h]
        return pltpu.make_async_copy(
            bufs[spot].at[pl.ds(row, half)],
            b_ref.at[p, pl.ds((2 * y + h) * half, half)],
            sem.at[p, 2 * y + h],
        )

    @pl.when(i == 0)
    def _():
        for p, (at, wants, sources, _) in enumerate(parts):
            for y in range(2):
                for h in range(2):
                    needed = wants(s_ref[at + 4], y, h)
                    for k in sources:

                        @pl.when((s_ref[at + 1 + y] == k) & needed)
                        def _():
                            copy(p, k, y, h).start()

    slot = i % 2

    def outs(i, slot):
        copies = []
        first = 0
        for p, (at, _, _, width) in enumerate(parts):
            copies.append(
                pltpu.make_async_copy(
                    o_ref.at[slot, :, pl.ds(first, width)],
                    o_hbm.at[
                        pl.ds(pl.multiple_of(s_ref[rows_at + i] * own, own), own),
                        pl.ds(pl.multiple_of(s_ref[at] * span + s_ref[at + 3], 128), width),
                    ],
                    o_sem.at[p, slot],
                )
            )
            first += width
        return copies

    @pl.when(i >= 2)
    def _():
        for out in outs(i - 2, slot):
            out.wait()

    first = 0
    for p, (at, wants, sources, width) in enumerate(parts):

        @pl.when(i == 0)
        def _():
            for y in range(2):
                for h in range(2):

                    @pl.when(wants(s_ref[at + 4], y, h))
                    def _():
                        copy(p, next(iter(sources)), y, h).wait()

        o_ref[slot, :, first : first + width] = lax.dot_general(
            a_ref[0],
            b_ref[p, pl.ds(pl.multiple_of(s_ref[at + 3], 128), width), :],
            NT,
            preferred_element_type=jnp.float32,
        )
        outs(i, slot)[p].start()
        first += width

    @pl.when(i == steps - 1)
    def _():
        for out in outs(i - 1, 1 - slot) + outs(i, slot):
            out.wait()


def tile_job(scalars, rows_at, parts, bufs, rows, out):
    count, own, total = rows.shape
    span = 2 * own
    any_spec = pl.BlockSpec(memory_space=pl.ANY)
    arrays, made = [], []
    for at, wants, cands, width in parts:
        sources = {}
        for k in cands:
            pair = []
            for array, row in bufs[k]:
                spot = [i for i, a in enumerate(arrays) if a is array]
                if not spot:
                    arrays.append(array)
                    spot = [len(arrays) - 1]
                pair.append((spot[0], row))
            sources[k] = pair
        made.append((at, wants, sources, width))
    columns = sum(width for *_, width in parts)
    return pl.pallas_call(
        functools.partial(tile_kernel, made, rows_at),
        grid_spec=pltpu.PrefetchScalarGridSpec(
            num_scalar_prefetch=1,
            grid=(count,),
            in_specs=[any_spec] * len(arrays)
            + [pl.BlockSpec((1, own, total), lambda i, s: (i, 0, 0)), any_spec],
            out_specs=any_spec,
            scratch_shapes=[
                pltpu.VMEM((len(parts), span, total), jnp.bfloat16),
                pltpu.VMEM((2, own, columns), jnp.float32),
                pltpu.SemaphoreType.DMA((len(parts), 4)),
                pltpu.SemaphoreType.DMA((len(parts), 2)),
            ],
        ),
        out_shape=jax.ShapeDtypeStruct(out.shape, out.dtype),
        input_output_aliases={2 + len(arrays): 0},
        compiler_params=pltpu.CompilerParams(vmem_limit_bytes=VMEM_BYTES),
        cost_estimate=pl.CostEstimate(
            flops=2 * count * own * columns * total,
            bytes_accessed=2 * count * own * total + 4 * count * own * columns,
            transcendentals=0,
        ),
    )(scalars, *arrays, rows, out)


def ring_body(n_row, n_col, design, arc_filter, arc_of_row, terr_stored, block_order, directions):
    own, _ = design.shape
    block = terr_stored.shape[1]
    r = lax.axis_index("row")
    c = lax.axis_index("col")
    zs = n_col // 2
    half = own // 2
    far = n_col // 2

    def hop(a, perm):
        return lax.ppermute(a, "col", perm)

    col_of = [2 * p if p < zs else 2 * (n_col - 1 - p) + 1 for p in range(n_col)]
    pos_of = [0] * n_col
    for p, col in enumerate(col_of):
        pos_of[col] = p
    forward = [(col_of[p], col_of[(p + 1) % n_col]) for p in range(n_col)]
    backward = [(d, s) for s, d in forward]

    whitened = whiten_rows(design, arc_filter, arc_of_row)
    rows, up1, up2a, up2b, up3a, dn1, dn2a, dn2b, dn3b, terr_all, edge, _, *pres, v = exchange(
        n_row, n_col, whitened, terr_stored, directions
    )
    last = far - 1
    bufs = {
        2: [(dn2a, 0), (dn2b, 0)],
        n_col - 2: [(up2a, 0), (up2b, 0)],
        1: [(dn1, 0), (dn1, half)],
        n_col - 1: [(up1, 0), (up1, half)],
    }
    upper = hop(up2b, forward)
    lower = hop(dn2a, backward)
    bufs[n_col - last] = [(up3a, 0), (upper, 0)]
    bufs[last] = [(lower, 0), (dn3b, 0)]
    bufs[far] = [(hop(up3a, forward), 0), (hop(dn3b, backward), 0)]

    per_pair = 2 * own // block

    wide = own // 128 * 128
    names = ["tile1b", "tile2a", "tile2b"]
    by_col, by_row, ks_of = [], [], {name: [set(), set()] for name in names}
    for col in range(n_col):
        z, y = col // 2, col % 2
        line = []
        for name in names:
            zz = z ^ 2 if name == "tile1b" else z ^ 3
            ks = [(pos_of[2 * zz + yy] - pos_of[col]) % n_col for yy in range(2)]
            near = [min(k, n_col - k) for k in ks]
            late = int(near[1] > near[0])
            soon = name[-1] == "a"
            lo = (2 * own - wide) * (1 - late) if soon else wide * late
            line += [zz, ks[0], ks[1], lo, late]
            ks_of[name][0].add(ks[1 - late])
            ks_of[name][1].add(ks[late])
        line += [(pos_of[s] - pos_of[col]) % n_col for s in range(n_col)]
        by_col.append(line + [y, z * per_pair, z, z ^ 1, z ^ 2])
    for row in range(n_row):
        by_row.append([row ^ m for m in range(n_row)] + [row * per_pair * zs])
    scalars = jnp.concatenate(
        [jnp.asarray(by_col, jnp.int32)[c], jnp.asarray(by_row, jnp.int32)[r]]
    )
    at = {"spots": 5 * len(names)}
    at["side"] = at["spots"] + n_col
    at["pair"] = at["side"] + 1
    at["own"] = at["side"] + 2
    at["rows"] = at["side"] + 5
    at["first"] = at["rows"] + n_row

    out = jax.ShapeDtypeStruct((n_row * own, n_col * own), jnp.float32)
    products, out = carry_job(
        at, scalars, block_order, terr_all, whitened, directions, edge,
        v, pres, out,
    )
    early = lambda late, y, h: late == 1 - y
    tail = lambda late, y, h: (late == y) | (h == 1 - y)
    parts = []
    for j, name in enumerate(names):
        soon, late = ks_of[name]
        if name[-1] == "a":
            parts.append((5 * j, early, sorted(soon), wide))
        else:
            parts.append((5 * j, tail, sorted(soon | late), 2 * own - wide))
    for some in (parts[:2], parts[2:]):
        out = tile_job(scalars, at["rows"], some, bufs, rows, out)
    return out.reshape(n_row, 1, own, n_col * own), products


def power_of_two(n):
    return n > 1 and n & (n - 1) == 0


def solution(mesh):
    n_row, n_col = mesh.shape["row"], mesh.shape["col"]

    def body(design, arc_filter, arc_of_row, terr_stored, block_order, directions):
        args = (design, arc_filter, arc_of_row, terr_stored, block_order, directions)
        own, block = design.shape[0], terr_stored.shape[1]
        aligned = n_row > 2 and own % 192 == 0 and own % block == block // 2 and (2 * own) % 128 == 0
        if power_of_two(n_row) and n_col == 8 and aligned:
            return ring_body(n_row, n_col, *args)
        return general_body(*args)

    return jax.shard_map(
        body,
        mesh=mesh,
        in_specs=(
            P(("row", "col"), None),
            P(),
            P(),
            P(("row", "col"), None),
            P("row"),
            P(("row", "col"), None),
        ),
        out_specs=(P(None, "col", None, "row"), P(("row", "col"), None)),
        check_vma=False,
    )
```
